128 devices in a mesh: row: 8 (over y, core), col: 16 (over x, z).
Axes of the slice: x: 4, y: 4, z: 4, core: 2. Of those that a mesh axis runs over, the one named last changes fastest.
Arguments:
- tile_data: float32 [8, 16, 288, 128, 128], P('row', 'col'), as said below
- tile_rows: int32 [8, 16, 288], P('row', 'col'), may hold values from 0 to 2047, as said below
- tile_cols: int32 [8, 16, 288], P('row', 'col'), may hold values from 0 to 1023, as said below
- tile_counts: int32 [8, 16], P('row', 'col'), may hold values from 128 to 288, as said below
Outputs:
- row_scale: float32 [2097152], P('row')
- column_scale: float32 [2097152], P('col')
The draws below stay inside these ranges and needn't reach their ends.
Inputs may be any that keep to these rules, and one draw needn't show every extreme that they name: `tile_rows`: within one device the blocks of the slots are all different. Slot k < 128 of device (p, q) holds row block q * 128 + k and column block p * 128 + k, so every row and column of A meets a used slot. `tile_cols`: column blocks of the slots, as above. `tile_counts`: some device uses all 288 slots in every draw. `tile_data`: entries are nonzero reals whose tiles have row and column scales of differing sizes.
All inputs are finite; a program needn't handle non-finite values.
Results may differ from the reference program's by a relative error of at most 0.0001.
Values sent between devices are 32-bit elements; how exact they have to be, the bound alone decides.
A program may use at most 64 MiB of HBM per device.

```python
import math
import jax
import jax.numpy as jnp
from jax import lax

TILE = 128
DIAG = 128
EXTRA = 160
SWEEPS = 4
TMAX = 288
RBD = 2048
CBD = 1024
N_ROW = 8
N_COL = 16


def layout(key):
    base = jax.random.fold_in(key, 11)
    ndev = N_ROW * N_COL
    keys = jax.random.split(base, ndev)

    def single(device_key, device):
        first, second = jax.random.split(device_key)
        row_group = device // N_COL
        col_group = device % N_COL
        offsets_diag = jnp.arange(DIAG, dtype=jnp.int32)
        diag_rows = col_group * DIAG + offsets_diag
        diag_cols = row_group * DIAG + offsets_diag
        picks = jax.random.permutation(first, RBD * (DIAG - 1))[:EXTRA].astype(jnp.int32)
        extra_rows = picks // (DIAG - 1)
        shifts = picks % (DIAG - 1)
        groups = jax.random.randint(second, (EXTRA,), 0, N_ROW, dtype=jnp.int32)
        extra_cols = groups * DIAG + (extra_rows % DIAG + 1 + shifts) % DIAG
        rows_all = jnp.concatenate([diag_rows, extra_rows]).astype(jnp.int32)
        cols_all = jnp.concatenate([diag_cols, extra_cols]).astype(jnp.int32)
        return (rows_all, cols_all)
    rows_all, cols_all = jax.vmap(single)(keys, jnp.arange(ndev, dtype=jnp.int32))
    count_key = jax.random.fold_in(key, 12)
    draw_key, busy_key = jax.random.split(count_key)
    spread = jax.random.randint(draw_key, (ndev,), 0, EXTRA + 1, dtype=jnp.int32)
    further = spread * spread // EXTRA
    busiest = jax.random.randint(busy_key, (), 0, ndev, dtype=jnp.int32)
    further = jnp.where(jnp.arange(ndev, dtype=jnp.int32) == busiest, EXTRA, further)
    used = (DIAG + further).astype(jnp.int32)
    return (rows_all.reshape(N_ROW, N_COL, TMAX), cols_all.reshape(N_ROW, N_COL, TMAX), used.reshape(N_ROW, N_COL))


def draw_tile_rows(key, part):
    return layout(key)[0]


def draw_tile_cols(key, part):
    return layout(key)[1]


def draw_tile_counts(key, part):
    return layout(key)[2]


def draw_tile_data(key, part):
    first, second, third = jax.random.split(jax.random.fold_in(key, 21), 3)
    shape = (N_ROW, N_COL, TMAX, TILE, TILE)
    values = jax.random.normal(first, shape, jnp.float32)
    low, high = (0.0, math.log(10.0))
    row_factor = jnp.exp(jax.random.uniform(second, (N_ROW, N_COL, TMAX, TILE, 1), jnp.float32, low, high))
    col_factor = jnp.exp(jax.random.uniform(third, (N_ROW, N_COL, TMAX, 1, TILE), jnp.float32, low, high))
    return (values * row_factor * col_factor).astype(jnp.float32)


def setup_inputs(seed: int = 0) -> dict:
    key_list = jax.random.split(jax.random.key(seed), 5)
    tile_data = draw_tile_data(jax.random.fold_in(key_list[4], 71), 0)
    tile_rows = draw_tile_rows(jax.random.fold_in(key_list[4], 71), 0)
    tile_cols = draw_tile_cols(jax.random.fold_in(key_list[4], 71), 0)
    tile_counts = draw_tile_counts(jax.random.fold_in(key_list[4], 71), 0)
    return dict(tile_data=tile_data, tile_rows=tile_rows, tile_cols=tile_cols, tile_counts=tile_counts)


epsilon = 1e-06

def measure(flat_tiles, global_rows, global_cols, in_use, row_scale, column_scale, want_peak):

    def visit(carry, item):
        row_acc, col_acc = carry
        blocks, rows_here, cols_here, used = item
        scaled = jnp.abs(blocks) * row_scale[rows_here][:, :, None] * column_scale[cols_here][:, None, :]
        scaled = jnp.where(used[:, None, None], scaled, jnp.float32(0.0))
        if want_peak:
            row_acc = row_acc.at[rows_here].max(scaled.max(axis=2))
            col_acc = col_acc.at[cols_here].max(scaled.max(axis=1))
        else:
            row_acc = row_acc.at[rows_here].add(scaled.sum(axis=2))
            col_acc = col_acc.at[cols_here].add(scaled.sum(axis=1))
        return ((row_acc, col_acc), None)
    start = (jnp.zeros_like(row_scale), jnp.zeros_like(column_scale))
    (row_acc, col_acc), _ = lax.scan(visit, start, (flat_tiles, global_rows, global_cols, in_use))
    return (row_acc, col_acc)

def reference(tile_data, tile_rows, tile_cols, tile_counts):
    ndev = N_ROW * N_COL
    flat_tiles = tile_data.reshape(ndev, TMAX, TILE, TILE)
    device = jnp.arange(ndev, dtype=jnp.int32)
    global_rows = ((device // N_COL)[:, None] * RBD + tile_rows.reshape(ndev, TMAX)).astype(jnp.int32)
    global_cols = ((device % N_COL)[:, None] * CBD + tile_cols.reshape(ndev, TMAX)).astype(jnp.int32)
    in_use = jnp.arange(TMAX, dtype=jnp.int32)[None, :] < tile_counts.reshape(ndev, 1)
    row_scale = jnp.ones((RBD * N_ROW, TILE), jnp.float32)
    column_scale = jnp.ones((CBD * N_COL, TILE), jnp.float32)
    for sweep in range(SWEEPS):
        peak_row, peak_col = measure(flat_tiles, global_rows, global_cols, in_use, row_scale, column_scale, True)
        row_scale = row_scale * lax.rsqrt(peak_row + epsilon)
        column_scale = column_scale * lax.rsqrt(peak_col + epsilon)
    total_row, total_col = measure(flat_tiles, global_rows, global_cols, in_use, row_scale, column_scale, False)
    row_scale = row_scale * lax.rsqrt(total_row + epsilon)
    column_scale = column_scale * lax.rsqrt(total_col + epsilon)
    return (row_scale.reshape(-1), column_scale.reshape(-1))
```

```python
import functools

import jax
import jax.numpy as jnp
from jax import lax
from jax.experimental import pallas as pl
from jax.experimental.pallas import tpu as pltpu
from jax.sharding import PartitionSpec as P

TILE = 128
DIAG = 128
SWEEPS = 4
epsilon = 1e-06

EXT = 256
ROW_CAP = 32
COL_CAP = 48
LEVELS = 8
GROUP = 8
CHUNK = 16

f32 = jnp.float32
bf16 = jnp.bfloat16
MESH = pltpu.DeviceIdType.MESH if hasattr(pltpu, "DeviceIdType") else pl.DeviceIdType.MESH


def halves(x):
    hi = x.astype(bf16)
    lo = (x - hi.astype(f32)).astype(bf16)
    return jnp.concatenate([hi, lo], axis=1)


def select_rows(onehot, x):
    y = jnp.dot(onehot, halves(x), preferred_element_type=f32)
    return y[:, :TILE] + y[:, TILE:]


def iota(shape, dim):
    return lax.broadcasted_iota(jnp.int32, shape, dim).astype(f32)


def columns(row):
    parts = [
        jnp.broadcast_to(row[:, i : i + TILE], (TILE, TILE)).T for i in range(0, row.shape[1], TILE)
    ]
    return jnp.concatenate(parts, axis=0)


def earlier_equal(cols, rows):
    count = cols.shape[0] // TILE
    out = []
    before = iota((TILE, TILE), 0) < iota((TILE, TILE), 1)
    for b in range(count):
        total = jnp.zeros((1, TILE), f32)
        here = rows[b]
        for a in range(b + 1):
            same = cols[a * TILE : (a + 1) * TILE] == here
            if a == b:
                same = same & before
            total = total + jnp.sum(jnp.where(same, 1.0, 0.0), axis=0, keepdims=True)
        out.append(total)
    return out


class Side:
    def __init__(self, axis, count, cap, key_row, refs):
        self.axis, self.count, self.cap, self.key_row = axis, count, cap, key_row
        self.entries = count * cap
        (
            self.own,
            self.ext,
            self.diag_term,
            self.ext_term,
            self.pack,
            self.unpack,
            self.levels,
            self.expand,
            self.id_recv,
            self.p1_send,
            self.p1_recv,
            self.p2_send,
            self.p2_recv,
            self.fin,
            self.send_sems,
            self.recv_sems,
        ) = refs
        self.me = lax.axis_index(axis)

    def partner(self, d):
        return lax.rem(self.me + d, self.count)

    def sender(self, d):
        return lax.rem(self.me + self.count - d, self.count)

    def copy(self, kind, d, src, dst, peer):
        kind, slot = kind
        return pltpu.make_async_remote_copy(
            src_ref=src,
            dst_ref=dst,
            send_sem=self.send_sems.at[kind, d],
            recv_sem=self.recv_sems.at[kind, slot, d],
            device_id={self.axis: peer},
            device_id_type=MESH,
        )

    def send(self, kind, send, recv):
        for d in range(1, self.count):
            peer = self.partner(d)
            self.copy(kind, d, send.at[peer], recv.at[self.me], peer).start()
        recv[self.me] = send[self.me]

    def wait_send(self, kind, send, recv):
        for d in range(1, self.count):
            peer = self.partner(d)
            self.copy(kind, d, send.at[peer], recv.at[self.me], peer).wait_send()

    def wait_recv(self, kind, send, recv):
        for d in range(1, self.count):
            peer = self.sender(d)
            self.copy(kind, d, send.at[peer], recv.at[peer], peer).wait_recv()


def ID():
    return (0, 0)


def FIRST(slot):
    return (1, slot)


def BACK(slot):
    return (2, slot)


def LAST():
    return (3, 0)


def prepare(side, info_ref, flag_ref):
    n, cap, entries = side.count, side.cap, side.entries
    key = info_ref[side.key_row : side.key_row + 1, :]
    owner = jnp.floor(key * (1.0 / DIAG))
    local = key - owner * DIAG
    used = key >= 0.0
    owner_cols = columns(owner)
    rank = earlier_equal(owner_cols, [owner[:, :TILE], owner[:, TILE:]])
    rank = jnp.concatenate(rank, axis=1)
    fits = used & (rank < cap - 1.0)
    dest = jnp.where(fits, owner * cap + rank, -1.0)
    over = jnp.where(used & (rank >= cap - 1.0), 1.0, 0.0)
    flag_ref[...] = jnp.maximum(flag_ref[...], jnp.max(over, axis=1, keepdims=True))
    side.pack[...] = jnp.where(iota((entries, EXT), 0) == dest, 1.0, 0.0).astype(bf16)
    dest_cols = columns(dest)
    for i in range(0, entries, TILE):
        lanes = iota((EXT, TILE), 1) + float(i)
        side.unpack[:, i : i + TILE] = jnp.where(dest_cols == lanes, 1.0, 0.0).astype(bf16)
    side.ext_term[...] = jnp.where(columns(jnp.where(used, 1.0, 0.0)) > 0.0, columns(local) + 1.0, 0.0)


def fill(side, flag_ref):
    side.p1_send[...] = select_rows(side.pack[...], side.ext_term[...]).reshape(side.count, side.cap, TILE)
    flag = jnp.broadcast_to(flag_ref[0:1, :].reshape(1, 1, TILE), (side.count, 1, TILE))
    side.p1_send[:, side.cap - 1 : side.cap, :] = flag


def take_flag(side, recv, flag_ref):
    seen = recv[:, side.cap - 1, :]
    flag_ref[...] = jnp.maximum(flag_ref[...], jnp.max(seen, axis=0, keepdims=True))


def learn(side, flag_ref):
    n, cap, entries = side.count, side.cap, side.entries
    take_flag(side, side.id_recv, flag_ref)
    place = lax.broadcasted_iota(jnp.int32, (n, cap, TILE), 1)
    ids = jnp.where(place == cap - 1, 0.0, side.id_recv[...]).reshape(entries, TILE)
    lanes = iota((TILE, TILE), 1)
    rows = []
    for i in range(0, entries, TILE):
        block = ids[i : i + TILE]
        side.expand[i : i + TILE, :] = jnp.where(block == lanes + 1.0, 1.0, 0.0).astype(bf16)
        rows.append(block.T)
    level = earlier_equal(ids, rows)
    wanted = iota((TILE, TILE), 0) + 1.0
    over = jnp.zeros((1, TILE), f32)
    for b, i in enumerate(range(0, entries, TILE)):
        hit = rows[b] == wanted
        over = jnp.maximum(
            over, jnp.where((rows[b][0:1] > 0.0) & (level[b] >= float(LEVELS)), 1.0, 0.0)
        )
        for t in range(LEVELS):
            side.levels[t * TILE : (t + 1) * TILE, i : i + TILE] = jnp.where(
                hit & (level[b] == float(t)), 1.0, 0.0
            ).astype(bf16)
    flag_ref[...] = jnp.maximum(flag_ref[...], jnp.max(over, axis=1, keepdims=True))


def put(side, slot):
    side.send(FIRST(slot), side.p1_send, side.p1_recv.at[slot])


def put_done(side, slot):
    side.wait_send(FIRST(slot), side.p1_send, side.p1_recv.at[slot])


def combine(side, flag_ref, slot, final):
    recv = side.p1_recv.at[slot]
    side.wait_recv(FIRST(slot), side.p1_send, recv)
    take_flag(side, recv, flag_ref)
    terms = select_rows(side.levels[...], recv[...].reshape(side.entries, TILE))
    terms = terms.reshape(LEVELS, TILE, TILE)
    if final:
        total = side.diag_term[...] + jnp.sum(terms, axis=0)
    else:
        total = jnp.maximum(side.diag_term[...], jnp.max(terms, axis=0))
    own = side.own[...]
    side.own[...] = own * lax.rsqrt((2.0 * total) * own + epsilon)


def give_back(side, slot):
    side.p2_send[...] = select_rows(side.expand[...], side.own[...]).reshape(side.count, side.cap, TILE)
    side.send(BACK(slot), side.p2_send, side.p2_recv.at[slot])


def take_back(side, slot):
    recv = side.p2_recv.at[slot]
    side.wait_recv(BACK(slot), side.p2_send, recv)
    side.ext[...] = select_rows(side.unpack[...], recv[...].reshape(side.entries, TILE))
    side.wait_send(BACK(slot), side.p2_send, recv)


def reduce_tiles(tiles, first, scale, out, count, final):
    def step(g, carry):
        base = pl.multiple_of(g * GROUP, GROUP)
        cols = scale[pl.ds(base, GROUP), :].T
        results = []
        for j in range(GROUP):
            x = tiles[first + base + j] * jnp.broadcast_to(cols[:, j : j + 1], (TILE, TILE))
            if final:
                results.append(jnp.sum(x, axis=0, keepdims=True))
            else:
                results.append(jnp.max(x, axis=0, keepdims=True))
        out[pl.ds(base, GROUP), :] = jnp.concatenate(results, axis=0)
        return carry

    lax.fori_loop(0, count // GROUP, step, 0)


def kernel(
    n_row, n_col, slots, info_ref, data_ref, row_out, col_out, flag_out, tiles, turned, flag_ref, load_sems, out_sems, *rest
):
    rows = Side("col", n_col, ROW_CAP, 0, rest[: len(rest) // 2])
    cols = Side("row", n_row, COL_CAP, 1, rest[len(rest) // 2 :])
    sides = (cols, rows)

    barrier = pltpu.get_barrier_semaphore()
    for side in sides:
        for d in range(1, side.count):
            pl.semaphore_signal(barrier, inc=1, device_id={side.axis: side.partner(d)}, device_id_type=MESH)

    extra = slots - DIAG
    order = list(range(DIAG // CHUNK, slots // CHUNK)) + list(range(DIAG // CHUNK))

    def load(c):
        return pltpu.make_async_copy(
            data_ref.at[pl.ds(c * CHUNK, CHUNK)], tiles.at[pl.ds(c * CHUNK, CHUNK)], load_sems.at[c]
        )

    for c in order:
        load(c).start()

    flag_ref[...] = jnp.zeros_like(flag_ref)
    for side in sides:
        prepare(side, info_ref, flag_ref)
    for side in sides:
        fill(side, flag_ref)
    pl.semaphore_wait(barrier, n_row + n_col - 2)
    for side in sides:
        side.send(ID(), side.p1_send, side.id_recv)

    count = info_ref[2:3, :TILE]

    def first_terms(c, side_terms, offset):
        row_term, col_term = side_terms
        load(c).wait()

        def step(g, carry):
            base = pl.multiple_of(c * CHUNK + g * GROUP, GROUP)
            row_results, col_results = [], []
            for j in range(GROUP):
                slot = base + j
                half = jnp.where(jnp.full((1, TILE), slot, jnp.int32).astype(f32) < count, 0.5, 0.0)
                x = jnp.abs(tiles[slot]) * half
                y = x.T
                tiles[slot] = x
                turned[slot] = y
                col_results.append(jnp.max(x, axis=0, keepdims=True))
                row_results.append(jnp.max(y, axis=0, keepdims=True))
            col_term[pl.ds(base - offset, GROUP), :] = jnp.concatenate(col_results, axis=0)
            row_term[pl.ds(base - offset, GROUP), :] = jnp.concatenate(row_results, axis=0)
            return carry

        lax.fori_loop(0, CHUNK // GROUP, step, 0)

    for side in sides:
        side.ext_term[...] = jnp.zeros_like(side.ext_term)
        side.own[...] = jnp.ones_like(side.own)
    for c in range(DIAG // CHUNK, slots // CHUNK):
        first_terms(c, (rows.ext_term, cols.ext_term), DIAG)
    for side in sides:
        side.wait_send(ID(), side.p1_send, side.id_recv)
        fill(side, flag_ref)
        put(side, 0)
    for c in range(DIAG // CHUNK):
        first_terms(c, (rows.diag_term, cols.diag_term), 0)
    for side in sides:
        side.wait_recv(ID(), side.p1_send, side.id_recv)
        learn(side, flag_ref)
    for side in sides:
        combine(side, flag_ref, 0, False)
        give_back(side, 0)
        put_done(side, 0)

    def sweep(t, final):
        slot, before = t % 2, (t + 1) % 2
        take_back(cols, before)
        reduce_tiles(turned, DIAG, cols.ext, rows.ext_term, extra, final)
        fill(rows, flag_ref)
        put(rows, slot)
        take_back(rows, before)
        reduce_tiles(tiles, DIAG, rows.ext, cols.ext_term, extra, final)
        fill(cols, flag_ref)
        put(cols, slot)
        reduce_tiles(turned, 0, cols.own, rows.diag_term, DIAG, final)
        reduce_tiles(tiles, 0, rows.own, cols.diag_term, DIAG, final)
        for side in sides:
            combine(side, flag_ref, slot, final)
            if not final:
                give_back(side, slot)
        for side in sides:
            put_done(side, slot)

    def middle(t, carry):
        sweep(t, False)
        return carry

    lax.fori_loop(1, SWEEPS, middle, 0)
    sweep(SWEEPS, True)

    flag_out[...] = flag_ref[...]
    for i, (side, out) in enumerate(((rows, row_out), (cols, col_out))):
        side.fin[...] = side.own[...]
        place = out.at[pl.ds(pl.multiple_of(side.me * DIAG, DIAG), DIAG)]
        for d in range(1, side.count):
            side.copy(LAST(), d, side.fin, place, side.partner(d)).start()
        pltpu.make_async_copy(side.fin, place, out_sems.at[i]).start()
    for i, (side, out) in enumerate(((rows, row_out), (cols, col_out))):
        place = out.at[pl.ds(pl.multiple_of(side.me * DIAG, DIAG), DIAG)]
        for d in range(1, side.count):
            peer = side.sender(d)
            there = out.at[pl.ds(pl.multiple_of(peer * DIAG, DIAG), DIAG)]
            side.copy(LAST(), d, side.fin, there, peer).wait_recv()
        for d in range(1, side.count):
            side.copy(LAST(), d, side.fin, place, side.partner(d)).wait_send()
        pltpu.make_async_copy(side.fin, place, out_sems.at[i]).wait()


def side_scratch(count, cap):
    entries = count * cap
    return [
        pltpu.VMEM((DIAG, TILE), f32),
        pltpu.VMEM((EXT, TILE), f32),
        pltpu.VMEM((DIAG, TILE), f32),
        pltpu.VMEM((EXT, TILE), f32),
        pltpu.VMEM((entries, EXT), bf16),
        pltpu.VMEM((EXT, entries), bf16),
        pltpu.VMEM((LEVELS * DIAG, entries), bf16),
        pltpu.VMEM((entries, DIAG), bf16),
        pltpu.VMEM((count, cap, TILE), f32),
        pltpu.VMEM((count, cap, TILE), f32),
        pltpu.VMEM((2, count, cap, TILE), f32),
        pltpu.VMEM((count, cap, TILE), f32),
        pltpu.VMEM((2, count, cap, TILE), f32),
        pltpu.VMEM((DIAG, TILE), f32),
        pltpu.SemaphoreType.DMA((4, count)),
        pltpu.SemaphoreType.DMA((4, 2, count)),
    ]


def sparse(tiles, row_blocks, column_blocks, used_count, n_row, n_col):
    slots = tiles.shape[0]
    in_use = jnp.arange(slots, dtype=jnp.int32) < used_count
    spare = EXT - (slots - DIAG)
    key = jnp.stack([row_blocks, column_blocks])[:, DIAG:]
    key = jnp.where(in_use[None, DIAG:], key, -1).astype(f32)
    key = jnp.pad(key, ((0, 0), (0, spare)), constant_values=-1.0)
    info = jnp.concatenate([key, jnp.full((6, EXT), used_count, jnp.int32).astype(f32)])
    return pl.pallas_call(
        functools.partial(kernel, n_row, n_col, slots),
        out_shape=(
            jax.ShapeDtypeStruct((n_col * DIAG, TILE), f32),
            jax.ShapeDtypeStruct((n_row * DIAG, TILE), f32),
            jax.ShapeDtypeStruct((8, TILE), f32),
        ),
        in_specs=[pl.BlockSpec(memory_space=pltpu.VMEM), pl.BlockSpec(memory_space=pl.ANY)],
        out_specs=(
            pl.BlockSpec(memory_space=pl.ANY),
            pl.BlockSpec(memory_space=pl.ANY),
            pl.BlockSpec(memory_space=pltpu.VMEM),
        ),
        scratch_shapes=[
            pltpu.VMEM((slots, TILE, TILE), f32),
            pltpu.VMEM((slots, TILE, TILE), f32),
            pltpu.VMEM((8, TILE), f32),
            pltpu.SemaphoreType.DMA((slots // CHUNK,)),
            pltpu.SemaphoreType.DMA((2,)),
            *side_scratch(n_col, ROW_CAP),
            *side_scratch(n_row, COL_CAP),
        ],
        compiler_params=pltpu.CompilerParams(
            collective_id=0, has_side_effects=True, vmem_limit_bytes=60 << 20
        ),
    )(info, tiles)


def gathered(x, axis):
    n = lax.axis_size(axis)
    me = lax.axis_index(axis)
    ring = [(i, (i + 1) % n) for i in range(n)]
    out = jnp.zeros((n,) + x.shape, x.dtype).at[me].set(x)

    def step(i, carry):
        out, y = carry
        y = lax.ppermute(y, axis, ring)
        return out.at[lax.rem(me + n - i, n)].set(y), y

    return lax.fori_loop(1, n, step, (out, x))[0]


def dense(blocks, row_blocks, column_blocks, used_count):
    slots, side = blocks.shape[:2]
    row_length = DIAG * lax.axis_size("col")
    column_length = DIAG * lax.axis_size("row")
    in_use = jnp.arange(slots, dtype=jnp.int32) < used_count
    magnitude = jnp.where(in_use[:, None, None], jnp.abs(blocks), f32(0.0))

    def sweep(t, carry):
        row_scale, column_scale = carry
        scaled = magnitude * row_scale[row_blocks][:, :, None] * column_scale[column_blocks][:, None, :]
        no_rows = jnp.zeros((row_length, side), f32)
        no_columns = jnp.zeros((column_length, side), f32)
        peak = t < SWEEPS

        def peaks():
            rows = no_rows.at[row_blocks].max(scaled.max(axis=2))
            columns = no_columns.at[column_blocks].max(scaled.max(axis=1))
            return rows, columns

        def totals():
            rows = no_rows.at[row_blocks].add(scaled.sum(axis=2))
            columns = no_columns.at[column_blocks].add(scaled.sum(axis=1))
            return rows, columns

        rows, columns = lax.cond(peak, peaks, totals)
        rows, columns = gathered(rows, "col"), gathered(columns, "row")
        rows = jnp.where(peak, rows.max(axis=0), rows.sum(axis=0))
        columns = jnp.where(peak, columns.max(axis=0), columns.sum(axis=0))
        return row_scale * lax.rsqrt(rows + epsilon), column_scale * lax.rsqrt(columns + epsilon)

    start = (jnp.ones((row_length, side), f32), jnp.ones((column_length, side), f32))
    return lax.fori_loop(0, SWEEPS + 1, sweep, start)


def on_device(tile_data, tile_rows, tile_cols, tile_counts):
    blocks = tile_data[0, 0]
    row_blocks = tile_rows[0, 0]
    column_blocks = tile_cols[0, 0]
    used_count = tile_counts[0, 0]
    n_row, n_col = lax.axis_size("row"), lax.axis_size("col")
    row_scale, column_scale, flag = sparse(blocks, row_blocks, column_blocks, used_count, n_row, n_col)
    row_scale, column_scale = lax.cond(
        flag[0, 0] > 0.0,
        lambda: dense(blocks, row_blocks, column_blocks, used_count),
        lambda: (row_scale, column_scale),
    )
    return (row_scale.reshape(-1), column_scale.reshape(-1))


def solution(mesh):
    placed = (
        P("row", "col", None, None, None),
        P("row", "col", None),
        P("row", "col", None),
        P("row", "col"),
    )
    return jax.shard_map(
        on_device, mesh=mesh, in_specs=placed, out_specs=(P("row"), P("col")), check_vma=False
    )
```

```python
import functools

import jax
import jax.numpy as jnp
from jax import lax
from jax.experimental import pallas as pl
from jax.experimental.pallas import tpu as pltpu
from jax.sharding import PartitionSpec as P

TILE = 128
DIAG = 128
SWEEPS = 4
epsilon = 1e-06

EXT = 256
ROW_CAP = 32
COL_CAP = 48
LEVELS = 8
GROUP = 8
PARTS = 2
TAIL = 32
QUARTERS = TILE // TAIL

f32 = jnp.float32
bf16 = jnp.bfloat16
MESH = pltpu.DeviceIdType.MESH if hasattr(pltpu, "DeviceIdType") else pl.DeviceIdType.MESH


def halves(x):
    hi = x.astype(bf16)
    lo = (x - hi.astype(f32)).astype(bf16)
    return jnp.concatenate([hi, lo], axis=1)


def select_rows(onehot, x):
    y = jnp.dot(onehot, halves(x), preferred_element_type=f32)
    return y[:, :TILE] + y[:, TILE:]


def iota(shape, dim):
    return lax.broadcasted_iota(jnp.int32, shape, dim).astype(f32)


def columns(row):
    parts = [
        jnp.broadcast_to(row[:, i : i + TILE], (TILE, TILE)).T for i in range(0, row.shape[1], TILE)
    ]
    return jnp.concatenate(parts, axis=0)


def earlier_equal(cols, rows):
    count = cols.shape[0] // TILE
    out = []
    before = iota((TILE, TILE), 0) < iota((TILE, TILE), 1)
    for b in range(count):
        total = jnp.zeros((1, TILE), f32)
        here = rows[b]
        for a in range(b + 1):
            same = cols[a * TILE : (a + 1) * TILE] == here
            if a == b:
                same = same & before
            total = total + jnp.sum(jnp.where(same, 1.0, 0.0), axis=0, keepdims=True)
        out.append(total)
    return out


class Side:
    def __init__(self, axis, count, cap, key_row, refs):
        self.axis, self.count, self.cap, self.key_row = axis, count, cap, key_row
        self.entries = count * cap
        (
            self.own,
            self.own_turned,
            self.ext,
            self.tail,
            self.diag_term,
            self.ext_turned,
            self.tail_term,
            self.ext_term,
            self.pack,
            self.unpack,
            self.levels,
            self.expand,
            self.id_recv,
            self.p1_send,
            self.p1_recv,
            self.p2_send,
            self.p2_recv,
            self.fin,
            self.send_sems,
            self.recv_sems,
        ) = refs
        self.me = lax.axis_index(axis)

    def partner(self, d):
        return lax.rem(self.me + d, self.count)

    def sender(self, d):
        return lax.rem(self.me + self.count - d, self.count)

    def copy(self, kind, d, src, dst, peer):
        kind, slot = kind
        return pltpu.make_async_remote_copy(
            src_ref=src,
            dst_ref=dst,
            send_sem=self.send_sems.at[kind, d],
            recv_sem=self.recv_sems.at[kind, slot, d],
            device_id={self.axis: peer},
            device_id_type=MESH,
        )

    def send(self, kind, send, recv):
        for d in range(1, self.count):
            peer = self.partner(d)
            self.copy(kind, d, send.at[peer], recv.at[self.me], peer).start()
        recv[self.me] = send[self.me]

    def wait_send(self, kind, send, recv):
        for d in range(1, self.count):
            peer = self.partner(d)
            self.copy(kind, d, send.at[peer], recv.at[self.me], peer).wait_send()

    def wait_recv(self, kind, send, recv):
        for d in range(1, self.count):
            peer = self.sender(d)
            self.copy(kind, d, send.at[peer], recv.at[peer], peer).wait_recv()


def ID():
    return (0, 0)


def FIRST(slot):
    return (1, slot)


def BACK(slot):
    return (2, slot)


def LAST():
    return (3, 0)


def prepare(side, info_ref, flag_ref):
    n, cap, entries = side.count, side.cap, side.entries
    key = info_ref[side.key_row : side.key_row + 1, :]
    owner = jnp.floor(key * (1.0 / DIAG))
    local = key - owner * DIAG
    used = key >= 0.0
    owner_cols = columns(owner)
    rank = earlier_equal(owner_cols, [owner[:, :TILE], owner[:, TILE:]])
    rank = jnp.concatenate(rank, axis=1)
    fits = used & (rank < cap - 1.0)
    dest = jnp.where(fits, owner * cap + rank, -1.0)
    over = jnp.where(used & (rank >= cap - 1.0), 1.0, 0.0)
    flag_ref[...] = jnp.maximum(flag_ref[...], jnp.max(over, axis=1, keepdims=True))
    side.pack[...] = jnp.where(iota((entries, EXT), 0) == dest, 1.0, 0.0).astype(bf16)
    dest_cols = columns(dest)
    for i in range(0, entries, TILE):
        lanes = iota((EXT, TILE), 1) + float(i)
        side.unpack[:, i : i + TILE] = jnp.where(dest_cols == lanes, 1.0, 0.0).astype(bf16)
    side.ext_term[...] = jnp.where(columns(jnp.where(used, 1.0, 0.0)) > 0.0, columns(local) + 1.0, 0.0)


def fill(side, flag_ref):
    side.p1_send[...] = select_rows(side.pack[...], side.ext_term[...]).reshape(side.count, side.cap, TILE)
    flag = jnp.broadcast_to(flag_ref[0:1, :].reshape(1, 1, TILE), (side.count, 1, TILE))
    side.p1_send[:, side.cap - 1 : side.cap, :] = flag


def take_flag(side, recv, flag_ref):
    seen = recv[:, side.cap - 1, :]
    flag_ref[...] = jnp.maximum(flag_ref[...], jnp.max(seen, axis=0, keepdims=True))


def learn(side, flag_ref):
    n, cap, entries = side.count, side.cap, side.entries
    take_flag(side, side.id_recv, flag_ref)
    place = lax.broadcasted_iota(jnp.int32, (n, cap, TILE), 1)
    ids = jnp.where(place == cap - 1, 0.0, side.id_recv[...]).reshape(entries, TILE)
    lanes = iota((TILE, TILE), 1)
    rows = []
    for i in range(0, entries, TILE):
        block = ids[i : i + TILE]
        side.expand[i : i + TILE, :] = jnp.where(block == lanes + 1.0, 1.0, 0.0).astype(bf16)
        rows.append(block.T)
    level = earlier_equal(ids, rows)
    wanted = iota((TILE, TILE), 0) + 1.0
    over = jnp.zeros((1, TILE), f32)
    for b, i in enumerate(range(0, entries, TILE)):
        hit = rows[b] == wanted
        over = jnp.maximum(
            over, jnp.where((rows[b][0:1] > 0.0) & (level[b] >= float(LEVELS)), 1.0, 0.0)
        )
        for t in range(LEVELS):
            side.levels[t * TILE : (t + 1) * TILE, i : i + TILE] = jnp.where(
                hit & (level[b] == float(t)), 1.0, 0.0
            ).astype(bf16)
    flag_ref[...] = jnp.maximum(flag_ref[...], jnp.max(over, axis=1, keepdims=True))


def put(side, slot):
    side.send(FIRST(slot), side.p1_send, side.p1_recv.at[slot])


def put_done(side, slot):
    side.wait_send(FIRST(slot), side.p1_send, side.p1_recv.at[slot])


def combine(side, flag_ref, slot, final):
    recv = side.p1_recv.at[slot]
    side.wait_recv(FIRST(slot), side.p1_send, recv)
    take_flag(side, recv, flag_ref)
    terms = select_rows(side.levels[...], recv[...].reshape(side.entries, TILE))
    terms = terms.reshape(LEVELS, TILE, TILE)
    if final:
        total = side.diag_term[...].T + jnp.sum(terms, axis=0)
    else:
        total = jnp.maximum(side.diag_term[...].T, jnp.max(terms, axis=0))
    own = side.own[...]
    own = own * lax.rsqrt((2.0 * total) * own + epsilon)
    side.own[...] = own
    side.own_turned[...] = own.T


def give_back(side, slot):
    side.p2_send[...] = select_rows(side.expand[...], side.own[...]).reshape(side.count, side.cap, TILE)
    side.send(BACK(slot), side.p2_send, side.p2_recv.at[slot])


def take_back(side, slot):
    recv = side.p2_recv.at[slot]
    side.wait_recv(BACK(slot), side.p2_send, recv)
    scale = select_rows(side.unpack[...], recv[...].reshape(side.entries, TILE))
    side.ext[...] = scale[:TILE].T
    tail = scale[TILE : TILE + TAIL]
    if side.axis == "col":
        tail = [tail] + [pltpu.roll(tail, TILE - q * TAIL, 1) for q in range(1, QUARTERS)]
        side.tail[...] = jnp.concatenate(tail, axis=0).T[:TAIL]
    else:
        side.tail[...] = jnp.concatenate([tail] * QUARTERS, axis=0).T
    side.wait_send(BACK(slot), side.p2_send, recv)


def gather_terms(side, final):
    side.ext_term[:TILE, :] = side.ext_turned[...].T
    if side.axis == "col":
        empty = jnp.zeros((TILE - TAIL, TILE), f32)
        turned = jnp.concatenate([side.tail_term[...], empty], axis=0).T
        parts = [turned[:TAIL]]
        parts += [pltpu.roll(turned[q * TAIL : (q + 1) * TAIL], q * TAIL, 1) for q in range(1, QUARTERS)]
        side.ext_term[TILE : TILE + TAIL, :] = parts[0] + parts[1] + parts[2] + parts[3]
    else:
        parts = side.tail_term[...].T.reshape(QUARTERS, TAIL, TILE)
        side.ext_term[TILE : TILE + TAIL, :] = jnp.sum(parts, axis=0) if final else jnp.max(parts, axis=0)


def row_pass(tiles, scale, out, final):
    scale = scale[...]

    def step(g, carry):
        base = pl.multiple_of(g * GROUP, GROUP)
        results = []
        for j in range(GROUP):
            x = tiles[base + j] * scale
            reduce = jnp.sum if final else jnp.max
            results.append(reduce(x, axis=0, keepdims=True))
        out[pl.ds(base, GROUP), :] = jnp.concatenate(results, axis=0)
        return carry

    lax.fori_loop(0, tiles.shape[0] // GROUP, step, 0)


def col_pass(tiles, scale, out, final):
    def step(g, total):
        base = pl.multiple_of(g * GROUP, GROUP)
        for j in range(GROUP):
            x = tiles[base + j] * scale[pl.ds(base + j, 1), :]
            total = total + x if final else jnp.maximum(total, x)
        return total

    out[...] = lax.fori_loop(0, tiles.shape[0] // GROUP, step, jnp.zeros((TILE, TILE), f32))


def kernel(
    n_row,
    n_col,
    info_ref,
    data_ref,
    row_out,
    col_out,
    flag_out,
    diag_tiles,
    ext_tiles,
    tail_loaded,
    tail_tiles,
    flag_ref,
    load_sems,
    out_sems,
    *rest,
):
    rows = Side("col", n_col, ROW_CAP, 0, rest[: len(rest) // 2])
    cols = Side("row", n_row, COL_CAP, 1, rest[len(rest) // 2 :])
    sides = (cols, rows)

    barrier = pltpu.get_barrier_semaphore()
    for side in sides:
        for d in range(1, side.count):
            pl.semaphore_signal(barrier, inc=1, device_id={side.axis: side.partner(d)}, device_id_type=MESH)

    def load(group, part):
        tiles, first, count = ((ext_tiles, DIAG, TILE), (tail_loaded, DIAG + TILE, TAIL), (diag_tiles, 0, DIAG))[group]
        height = TILE // PARTS
        at = part * height
        sem = load_sems.at[group, part]

        def step(s, carry):
            for j in range(GROUP):
                slot = s * GROUP + j
                pltpu.make_async_copy(
                    data_ref.at[first + slot, pl.ds(at, height)], tiles.at[pl.ds(at, height), slot], sem
                ).start()
            return carry

        lax.fori_loop(0, count // GROUP, step, 0)

    def loaded(group, part):
        tiles = (ext_tiles, tail_loaded, diag_tiles)[group]
        height = TILE // PARTS
        whole = tiles.at[pl.ds(part * height, height)]
        pltpu.make_async_copy(whole, whole, load_sems.at[group, part]).wait()

    for group in range(3):
        for part in range(PARTS):
            load(group, part)

    flag_ref[...] = jnp.zeros_like(flag_ref)
    for side in sides:
        prepare(side, info_ref, flag_ref)
    for side in sides:
        fill(side, flag_ref)
    pl.semaphore_wait(barrier, n_row + n_col - 2)
    for side in sides:
        side.send(ID(), side.p1_send, side.id_recv)

    count = info_ref[2:3, :TILE]
    lane = iota((1, TILE), 1)
    ext_half = jnp.where(lane + float(DIAG) < count, 0.5, 0.0)
    tail_slot = lax.broadcasted_iota(jnp.int32, (1, TILE), 1) % TAIL + (DIAG + TILE)
    tail_half = jnp.where(tail_slot.astype(f32) < count, 0.5, 0.0)

    def first_pass(group, tiles, half, row_term, col_term):
        total = jnp.zeros((TILE, TILE), f32)
        steps = TILE // PARTS // GROUP
        for part in range(PARTS):
            loaded(group, part)

            def step(g, total):
                base = pl.multiple_of(g * GROUP, GROUP)
                results = []
                for j in range(GROUP):
                    x = jnp.abs(tiles[base + j]).T * half
                    tiles[base + j] = x
                    results.append(jnp.max(x, axis=0, keepdims=True))
                    total = jnp.maximum(total, x)
                row_term[pl.ds(base, GROUP), :] = jnp.concatenate(results, axis=0)
                return total

            total = lax.fori_loop(part * steps, (part + 1) * steps, step, total)
        col_term[...] = total

    def first_tail():
        for part in range(PARTS):
            loaded(1, part)

        def step(g, total):
            base = pl.multiple_of(g * GROUP, GROUP)
            results = []
            for j in range(GROUP):
                x = jnp.concatenate([tail_loaded[q * TAIL + base + j] for q in range(QUARTERS)], axis=0)
                x = jnp.abs(x).T * tail_half
                tail_tiles[base + j] = x
                results.append(jnp.max(x, axis=0, keepdims=True))
                total = jnp.maximum(total, x)
            rows.tail_term[pl.ds(base, GROUP), :] = jnp.concatenate(results, axis=0)
            return total

        cols.tail_term[...] = lax.fori_loop(0, TAIL // GROUP, step, jnp.zeros((TILE, TILE), f32))

    for side in sides:
        side.ext_term[...] = jnp.zeros_like(side.ext_term)
        side.own[...] = jnp.ones_like(side.own)
    first_pass(0, ext_tiles, ext_half, rows.ext_turned, cols.ext_turned)
    first_tail()
    for side in sides:
        side.wait_send(ID(), side.p1_send, side.id_recv)
        gather_terms(side, False)
        fill(side, flag_ref)
        put(side, 0)
    first_pass(2, diag_tiles, 0.5, rows.diag_term, cols.diag_term)
    for side in sides:
        side.wait_recv(ID(), side.p1_send, side.id_recv)
        learn(side, flag_ref)
    for side in sides:
        combine(side, flag_ref, 0, False)
        give_back(side, 0)
        put_done(side, 0)

    def sweep(t, final):
        slot, before = t % 2, (t + 1) % 2
        take_back(cols, before)
        row_pass(ext_tiles, cols.ext, rows.ext_turned, final)
        row_pass(tail_tiles, cols.tail, rows.tail_term, final)
        gather_terms(rows, final)
        fill(rows, flag_ref)
        put(rows, slot)
        take_back(rows, before)
        col_pass(ext_tiles, rows.ext, cols.ext_turned, final)
        col_pass(tail_tiles, rows.tail, cols.tail_term, final)
        gather_terms(cols, final)
        fill(cols, flag_ref)
        put(cols, slot)
        row_pass(diag_tiles, cols.own_turned, rows.diag_term, final)
        col_pass(diag_tiles, rows.own_turned, cols.diag_term, final)
        for side in sides:
            combine(side, flag_ref, slot, final)
            if not final:
                give_back(side, slot)
        for side in sides:
            put_done(side, slot)

    def middle(t, carry):
        sweep(t, False)
        return carry

    lax.fori_loop(1, SWEEPS, middle, 0)
    sweep(SWEEPS, True)

    flag_out[...] = flag_ref[...]
    for i, (side, out) in enumerate(((rows, row_out), (cols, col_out))):
        side.fin[...] = side.own[...]
        place = out.at[pl.ds(pl.multiple_of(side.me * DIAG, DIAG), DIAG)]
        for d in range(1, side.count):
            side.copy(LAST(), d, side.fin, place, side.partner(d)).start()
        pltpu.make_async_copy(side.fin, place, out_sems.at[i]).start()
    for i, (side, out) in enumerate(((rows, row_out), (cols, col_out))):
        place = out.at[pl.ds(pl.multiple_of(side.me * DIAG, DIAG), DIAG)]
        for d in range(1, side.count):
            peer = side.sender(d)
            there = out.at[pl.ds(pl.multiple_of(peer * DIAG, DIAG), DIAG)]
            side.copy(LAST(), d, side.fin, there, peer).wait_recv()
        for d in range(1, side.count):
            side.copy(LAST(), d, side.fin, place, side.partner(d)).wait_send()
        pltpu.make_async_copy(side.fin, place, out_sems.at[i]).wait()


def side_scratch(count, cap, tail_scale, tail_term):
    entries = count * cap
    return [
        pltpu.VMEM((DIAG, TILE), f32),
        pltpu.VMEM((TILE, DIAG), f32),
        pltpu.VMEM((TILE, TILE), f32),
        pltpu.VMEM((tail_scale, TILE), f32),
        pltpu.VMEM((TILE, DIAG), f32),
        pltpu.VMEM((TILE, TILE), f32),
        pltpu.VMEM((tail_term, TILE), f32),
        pltpu.VMEM((EXT, TILE), f32),
        pltpu.VMEM((entries, EXT), bf16),
        pltpu.VMEM((EXT, entries), bf16),
        pltpu.VMEM((LEVELS * DIAG, entries), bf16),
        pltpu.VMEM((entries, DIAG), bf16),
        pltpu.VMEM((count, cap, TILE), f32),
        pltpu.VMEM((count, cap, TILE), f32),
        pltpu.VMEM((2, count, cap, TILE), f32),
        pltpu.VMEM((count, cap, TILE), f32),
        pltpu.VMEM((2, count, cap, TILE), f32),
        pltpu.VMEM((DIAG, TILE), f32),
        pltpu.SemaphoreType.DMA((4, count)),
        pltpu.SemaphoreType.DMA((4, 2, count)),
    ]


def sparse(tiles, row_blocks, column_blocks, used_count, n_row, n_col):
    slots = tiles.shape[0]
    assert slots == DIAG + TILE + TAIL
    in_use = jnp.arange(slots, dtype=jnp.int32) < used_count
    spare = EXT - (slots - DIAG)
    key = jnp.stack([row_blocks, column_blocks])[:, DIAG:]
    key = jnp.where(in_use[None, DIAG:], key, -1).astype(f32)
    key = jnp.pad(key, ((0, 0), (0, spare)), constant_values=-1.0)
    info = jnp.concatenate([key, jnp.full((6, EXT), used_count, jnp.int32).astype(f32)])
    return pl.pallas_call(
        functools.partial(kernel, n_row, n_col),
        out_shape=(
            jax.ShapeDtypeStruct((n_col * DIAG, TILE), f32),
            jax.ShapeDtypeStruct((n_row * DIAG, TILE), f32),
            jax.ShapeDtypeStruct((8, TILE), f32),
        ),
        in_specs=[pl.BlockSpec(memory_space=pltpu.VMEM), pl.BlockSpec(memory_space=pl.ANY)],
        out_specs=(
            pl.BlockSpec(memory_space=pl.ANY),
            pl.BlockSpec(memory_space=pl.ANY),
            pl.BlockSpec(memory_space=pltpu.VMEM),
        ),
        scratch_shapes=[
            pltpu.VMEM((TILE, TILE, DIAG), f32),
            pltpu.VMEM((TILE, TILE, TILE), f32),
            pltpu.VMEM((TILE, TAIL, TILE), f32),
            pltpu.VMEM((TAIL, TILE, TILE), f32),
            pltpu.VMEM((8, TILE), f32),
            pltpu.SemaphoreType.DMA((3, PARTS)),
            pltpu.SemaphoreType.DMA((2,)),
            *side_scratch(n_col, ROW_CAP, TAIL, TAIL),
            *side_scratch(n_row, COL_CAP, TILE, TILE),
        ],
        compiler_params=pltpu.CompilerParams(
            collective_id=0, has_side_effects=True, vmem_limit_bytes=60 << 20
        ),
    )(info, tiles)


def gathered(x, axis):
    n = lax.axis_size(axis)
    me = lax.axis_index(axis)
    ring = [(i, (i + 1) % n) for i in range(n)]
    out = jnp.zeros((n,) + x.shape, x.dtype).at[me].set(x)

    def step(i, carry):
        out, y = carry
        y = lax.ppermute(y, axis, ring)
        return out.at[lax.rem(me + n - i, n)].set(y), y

    return lax.fori_loop(1, n, step, (out, x))[0]


def dense(blocks, row_blocks, column_blocks, used_count):
    slots, side = blocks.shape[:2]
    row_length = DIAG * lax.axis_size("col")
    column_length = DIAG * lax.axis_size("row")
    in_use = jnp.arange(slots, dtype=jnp.int32) < used_count
    magnitude = jnp.where(in_use[:, None, None], jnp.abs(blocks), f32(0.0))

    def sweep(t, carry):
        row_scale, column_scale = carry
        scaled = magnitude * row_scale[row_blocks][:, :, None] * column_scale[column_blocks][:, None, :]
        no_rows = jnp.zeros((row_length, side), f32)
        no_columns = jnp.zeros((column_length, side), f32)
        peak = t < SWEEPS

        def peaks():
            rows = no_rows.at[row_blocks].max(scaled.max(axis=2))
            columns = no_columns.at[column_blocks].max(scaled.max(axis=1))
            return rows, columns

        def totals():
            rows = no_rows.at[row_blocks].add(scaled.sum(axis=2))
            columns = no_columns.at[column_blocks].add(scaled.sum(axis=1))
            return rows, columns

        rows, columns = lax.cond(peak, peaks, totals)
        rows, columns = gathered(rows, "col"), gathered(columns, "row")
        rows = jnp.where(peak, rows.max(axis=0), rows.sum(axis=0))
        columns = jnp.where(peak, columns.max(axis=0), columns.sum(axis=0))
        return row_scale * lax.rsqrt(rows + epsilon), column_scale * lax.rsqrt(columns + epsilon)

    start = (jnp.ones((row_length, side), f32), jnp.ones((column_length, side), f32))
    return lax.fori_loop(0, SWEEPS + 1, sweep, start)


def on_device(tile_data, tile_rows, tile_cols, tile_counts):
    blocks = tile_data[0, 0]
    row_blocks = tile_rows[0, 0]
    column_blocks = tile_cols[0, 0]
    used_count = tile_counts[0, 0]
    n_row, n_col = lax.axis_size("row"), lax.axis_size("col")
    row_scale, column_scale, flag = sparse(blocks, row_blocks, column_blocks, used_count, n_row, n_col)
    row_scale, column_scale = lax.cond(
        flag[0, 0] > 0.0,
        lambda: dense(blocks, row_blocks, column_blocks, used_count),
        lambda: (row_scale, column_scale),
    )
    return (row_scale.reshape(-1), column_scale.reshape(-1))


def solution(mesh):
    placed = (
        P("row", "col", None, None, None),
        P("row", "col", None),
        P("row", "col", None),
        P("row", "col"),
    )
    return jax.shard_map(
        on_device, mesh=mesh, in_specs=placed, out_specs=(P("row"), P("col")), check_vma=False
    )
```

```python
import functools

import jax
import jax.numpy as jnp
from jax import lax
from jax.experimental import pallas as pl
from jax.experimental.pallas import tpu as pltpu
from jax.sharding import PartitionSpec as P

TILE = 128
DIAG = 128
SWEEPS = 4
epsilon = 1e-06

EXT = 256
ROW_CAP = 24
COL_CAP = 40
LEVELS = 8
GROUP = 8
PARTS = (2, 1, 1)
WIDTH = 4
TAIL = 32
QUARTERS = TILE // TAIL

f32 = jnp.float32
bf16 = jnp.bfloat16
MESH = pltpu.DeviceIdType.MESH if hasattr(pltpu, "DeviceIdType") else pl.DeviceIdType.MESH


def halves(x):
    hi = x.astype(bf16)
    lo = (x - hi.astype(f32)).astype(bf16)
    return jnp.concatenate([hi, lo], axis=1)


def select_rows(onehot, x):
    y = jnp.dot(onehot, halves(x), preferred_element_type=f32)
    return y[:, :TILE] + y[:, TILE:]


def iota(shape, dim):
    return lax.broadcasted_iota(jnp.int32, shape, dim).astype(f32)


def columns(row):
    parts = [
        jnp.broadcast_to(row[:, i : i + TILE], (TILE, TILE)).T for i in range(0, row.shape[1], TILE)
    ]
    return jnp.concatenate(parts, axis=0)


def earlier_equal(cols, rows):
    count = cols.shape[0] // TILE
    out = []
    before = iota((TILE, TILE), 0) < iota((TILE, TILE), 1)
    for b in range(count):
        total = jnp.zeros((1, TILE), f32)
        here = rows[b]
        for a in range(b + 1):
            same = cols[a * TILE : (a + 1) * TILE] == here
            if a == b:
                same = same & before
            total = total + jnp.sum(jnp.where(same, 1.0, 0.0), axis=0, keepdims=True)
        out.append(total)
    return out


def padded(entries):
    return -(-entries // TILE) * TILE


class Side:
    def __init__(self, axis, count, cap, key_row, refs):
        self.axis, self.count, self.cap, self.key_row = axis, count, cap, key_row
        self.entries = padded(count * cap)
        (
            self.own,
            self.own_turned,
            self.ext,
            self.tail,
            self.diag_term,
            self.ext_turned,
            self.tail_term,
            self.ext_term,
            self.pack,
            self.unpack,
            self.levels,
            self.expand,
            self.id_recv,
            self.p1_send,
            self.p1_recv,
            self.p2_send,
            self.p2_recv,
            self.fin,
            self.flags,
            self.send_sems,
            self.recv_sems,
        ) = refs
        self.me = lax.axis_index(axis)

    def partner(self, d):
        return lax.rem(self.me + d, self.count)

    def sender(self, d):
        return lax.rem(self.me + self.count - d, self.count)

    def copy(self, kind, d, src, dst, peer):
        kind, slot = kind
        return pltpu.make_async_remote_copy(
            src_ref=src,
            dst_ref=dst,
            send_sem=self.send_sems.at[kind, d],
            recv_sem=self.recv_sems.at[kind, slot, d],
            device_id={self.axis: peer},
            device_id_type=MESH,
        )

    def place(self, ref, peer):
        return ref.at[pl.ds(pl.multiple_of(peer * self.cap, 8), self.cap)]

    def send(self, kind, send, recv):
        for d in range(1, self.count):
            peer = self.partner(d)
            self.copy(kind, d, self.place(send, peer), self.place(recv, self.me), peer).start()
        self.place(recv, self.me)[...] = self.place(send, self.me)[...]

    def wait_send(self, kind, send, recv):
        for d in range(1, self.count):
            peer = self.partner(d)
            self.copy(kind, d, self.place(send, peer), self.place(recv, self.me), peer).wait_send()

    def wait_recv(self, kind, send, recv):
        for d in range(1, self.count):
            peer = self.sender(d)
            self.copy(kind, d, self.place(send, peer), self.place(recv, peer), peer).wait_recv()

    def tell(self, flag_ref):
        for d in range(1, self.count):
            self.copy((4, 0), d, flag_ref, self.flags.at[self.me], self.partner(d)).start()
        self.flags[self.me] = flag_ref[...]

    def told(self, flag_ref):
        for d in range(1, self.count):
            peer = self.sender(d)
            self.copy((4, 0), d, flag_ref, self.flags.at[peer], peer).wait_recv()
            self.copy((4, 0), d, flag_ref, self.flags.at[self.me], self.partner(d)).wait_send()
        return jnp.max(self.flags[...], axis=0)


def ID():
    return (0, 0)


def FIRST(slot):
    return (1, slot)


def BACK(slot):
    return (2, slot)


def LAST():
    return (3, 0)


def prepare(side, blocks_ref, used_count, key_ref, flag_ref):
    cap, entries = side.cap, side.entries
    blocks = blocks_ref[...].astype(f32)
    key_ref[...] = jnp.full_like(key_ref, -1.0)
    key_ref[0:1, :TILE] = blocks[:, DIAG : DIAG + TILE]
    key_ref[0:1, TILE : TILE + TAIL] = blocks[:, DIAG + TILE :]
    slot = lax.broadcasted_iota(jnp.int32, (1, EXT), 1) + DIAG
    key = jnp.where(slot < used_count, key_ref[0:1, :], -1.0)
    owner = jnp.floor(key * (1.0 / DIAG))
    local = key - owner * DIAG
    used = key >= 0.0
    owner_cols = columns(owner)
    rank = earlier_equal(owner_cols, [owner[:, :TILE], owner[:, TILE:]])
    rank = jnp.concatenate(rank, axis=1)
    fits = used & (rank < float(cap))
    dest = jnp.where(fits, owner * cap + rank, -1.0)
    over = jnp.where(used & (rank >= float(cap)), 1.0, 0.0)
    flag_ref[...] = jnp.maximum(flag_ref[...], jnp.max(over, axis=1, keepdims=True))
    side.pack[...] = jnp.where(iota((entries, EXT), 0) == dest, 1.0, 0.0).astype(bf16)
    dest_cols = columns(dest)
    for i in range(0, entries, TILE):
        lanes = iota((EXT, TILE), 1) + float(i)
        side.unpack[:, i : i + TILE] = jnp.where(dest_cols == lanes, 1.0, 0.0).astype(bf16)
    side.ext_term[...] = jnp.where(columns(jnp.where(used, 1.0, 0.0)) > 0.0, columns(local) + 1.0, 0.0)


def fill(side):
    side.p1_send[...] = select_rows(side.pack[...], side.ext_term[...])


def learn(side, flag_ref):
    entries = side.entries
    ids = side.id_recv[...]
    lanes = iota((TILE, TILE), 1)
    rows = []
    for i in range(0, entries, TILE):
        block = ids[i : i + TILE]
        side.expand[i : i + TILE, :] = jnp.where(block == lanes + 1.0, 1.0, 0.0).astype(bf16)
        rows.append(block.T)
    level = earlier_equal(ids, rows)
    wanted = iota((TILE, TILE), 0) + 1.0
    over = jnp.zeros((1, TILE), f32)
    for b, i in enumerate(range(0, entries, TILE)):
        hit = rows[b] == wanted
        over = jnp.maximum(
            over, jnp.where((rows[b][0:1] > 0.0) & (level[b] >= float(LEVELS)), 1.0, 0.0)
        )
        for t in range(LEVELS):
            side.levels[t * TILE : (t + 1) * TILE, i : i + TILE] = jnp.where(
                hit & (level[b] == float(t)), 1.0, 0.0
            ).astype(bf16)
    flag_ref[...] = jnp.maximum(flag_ref[...], jnp.max(over, axis=1, keepdims=True))


def put(side, slot):
    side.send(FIRST(slot), side.p1_send, side.p1_recv.at[slot])


def put_done(side, slot):
    side.wait_send(FIRST(slot), side.p1_send, side.p1_recv.at[slot])


def combine(side, slot, final):
    recv = side.p1_recv.at[slot]
    side.wait_recv(FIRST(slot), side.p1_send, recv)
    terms = select_rows(side.levels[...], recv[...])
    terms = terms.reshape(LEVELS, TILE, TILE)
    if final:
        total = side.diag_term[...].T + jnp.sum(terms, axis=0)
    else:
        total = jnp.maximum(side.diag_term[...].T, jnp.max(terms, axis=0))
    own = side.own[...]
    own = own * lax.rsqrt((2.0 * total) * own + epsilon)
    side.own[...] = own
    side.own_turned[...] = own.T


def give_back(side, slot):
    side.p2_send[...] = select_rows(side.expand[...], side.own[...])
    side.send(BACK(slot), side.p2_send, side.p2_recv.at[slot])


def take_back(side, slot):
    recv = side.p2_recv.at[slot]
    side.wait_recv(BACK(slot), side.p2_send, recv)
    scale = select_rows(side.unpack[...], recv[...])
    side.ext[...] = scale[:TILE].T
    tail = scale[TILE : TILE + TAIL]
    if side.axis == "col":
        tail = [tail] + [pltpu.roll(tail, TILE - q * TAIL, 1) for q in range(1, QUARTERS)]
        side.tail[...] = jnp.concatenate(tail, axis=0).T[:TAIL]
    else:
        side.tail[...] = jnp.concatenate([tail] * QUARTERS, axis=0).T
    side.wait_send(BACK(slot), side.p2_send, recv)


def gather_terms(side, final):
    side.ext_term[:TILE, :] = side.ext_turned[...].T
    if side.axis == "col":
        empty = jnp.zeros((TILE - TAIL, TILE), f32)
        turned = jnp.concatenate([side.tail_term[...], empty], axis=0).T
        parts = [turned[:TAIL]]
        parts += [pltpu.roll(turned[q * TAIL : (q + 1) * TAIL], q * TAIL, 1) for q in range(1, QUARTERS)]
        side.ext_term[TILE : TILE + TAIL, :] = parts[0] + parts[1] + parts[2] + parts[3]
    else:
        parts = side.tail_term[...].T.reshape(QUARTERS, TAIL, TILE)
        side.ext_term[TILE : TILE + TAIL, :] = jnp.sum(parts, axis=0) if final else jnp.max(parts, axis=0)


def row_pass(tiles, scale, out, final):
    scale = scale[...]

    def step(g, carry):
        base = pl.multiple_of(g * GROUP, GROUP)
        results = []
        for j in range(GROUP):
            x = tiles[base + j] * scale
            reduce = jnp.sum if final else jnp.max
            results.append(reduce(x, axis=0, keepdims=True))
        out[pl.ds(base, GROUP), :] = jnp.concatenate(results, axis=0)
        return carry

    lax.fori_loop(0, tiles.shape[0] // GROUP, step, 0)


def col_pass(tiles, scale, out, final):
    def step(g, total):
        base = pl.multiple_of(g * GROUP, GROUP)
        for j in range(GROUP):
            x = tiles[base + j] * scale[pl.ds(base + j, 1), :]
            total = total + x if final else jnp.maximum(total, x)
        return total

    out[...] = lax.fori_loop(0, tiles.shape[0] // GROUP, step, jnp.zeros((TILE, TILE), f32))


def kernel(
    n_row,
    n_col,
    count_ref,
    rows_ref,
    cols_ref,
    data_ref,
    row_out,
    col_out,
    flag_out,
    diag_tiles,
    ext_tiles,
    tail_loaded,
    tail_tiles,
    key_ref,
    flag_ref,
    all_flags,
    load_sems,
    out_sems,
    near_sems,
    far_sems,
    *rest,
):
    rows = Side("col", n_col, ROW_CAP, 0, rest[: len(rest) // 2])
    cols = Side("row", n_row, COL_CAP, 1, rest[len(rest) // 2 :])
    sides = (cols, rows)

    barrier = pltpu.get_barrier_semaphore()
    for side in sides:
        for d in range(1, side.count):
            pl.semaphore_signal(barrier, inc=1, device_id={side.axis: side.partner(d)}, device_id_type=MESH)

    def load(group, part):
        tiles, first, count = ((ext_tiles, DIAG, TILE), (tail_loaded, DIAG + TILE, TAIL), (diag_tiles, 0, DIAG))[group]
        height = TILE // PARTS[group]
        at = part * height
        sem = load_sems.at[group, part]

        def step(s, carry):
            for j in range(GROUP):
                slot = s * GROUP + j
                pltpu.make_async_copy(
                    data_ref.at[first + slot, pl.ds(at, height)], tiles.at[pl.ds(at, height), slot], sem
                ).start()
            return carry

        lax.fori_loop(0, count // GROUP, step, 0)

    def loaded(group, part):
        tiles = (ext_tiles, tail_loaded, diag_tiles)[group]
        height = TILE // PARTS[group]
        whole = tiles.at[pl.ds(part * height, height)]
        pltpu.make_async_copy(whole, whole, load_sems.at[group, part]).wait()

    for group in range(3):
        for part in range(PARTS[group]):
            load(group, part)

    flag_ref[...] = jnp.zeros_like(flag_ref)
    count = count_ref[0, 0]
    for side, blocks_ref in ((cols, cols_ref), (rows, rows_ref)):
        prepare(side, blocks_ref, count, key_ref, flag_ref)
        for ref in (side.id_recv, side.p1_recv, side.p2_recv):
            empty = side.entries - side.count * side.cap
            if empty:
                ref[..., side.entries - empty :, :] = jnp.zeros((*ref.shape[:-2], empty, TILE), f32)
    for side in sides:
        fill(side)
    pl.semaphore_wait(barrier, n_row + n_col - 2)
    for side in sides:
        side.send(ID(), side.p1_send, side.id_recv)

    lane = lax.broadcasted_iota(jnp.int32, (1, TILE), 1)
    ext_half = jnp.where(lane + DIAG < count, 0.5, 0.0)
    tail_half = jnp.where(lane % TAIL + (DIAG + TILE) < count, 0.5, 0.0)

    def first_pass(group, tiles, half, row_term, col_term):
        total = jnp.zeros((TILE, TILE), f32)
        steps = TILE // PARTS[group] // GROUP
        for part in range(PARTS[group]):
            loaded(group, part)

            def step(g, total):
                base = pl.multiple_of(g * GROUP, GROUP)
                results = []
                for j in range(GROUP):
                    x = jnp.abs(tiles[base + j]).T * half
                    tiles[base + j] = x
                    results.append(jnp.max(x, axis=0, keepdims=True))
                    total = jnp.maximum(total, x)
                row_term[pl.ds(base, GROUP), :] = jnp.concatenate(results, axis=0)
                return total

            total = lax.fori_loop(part * steps, (part + 1) * steps, step, total)
        col_term[...] = total

    def first_tail():
        loaded(1, 0)

        def step(g, total):
            base = pl.multiple_of(g * GROUP, GROUP)
            results = []
            for j in range(GROUP):
                x = jnp.concatenate([tail_loaded[q * TAIL + base + j] for q in range(QUARTERS)], axis=0)
                x = jnp.abs(x).T * tail_half
                tail_tiles[base + j] = x
                results.append(jnp.max(x, axis=0, keepdims=True))
                total = jnp.maximum(total, x)
            rows.tail_term[pl.ds(base, GROUP), :] = jnp.concatenate(results, axis=0)
            return total

        cols.tail_term[...] = lax.fori_loop(0, TAIL // GROUP, step, jnp.zeros((TILE, TILE), f32))

    for side in sides:
        side.ext_term[...] = jnp.zeros_like(side.ext_term)
        side.own[...] = jnp.ones_like(side.own)
    first_pass(0, ext_tiles, ext_half, rows.ext_turned, cols.ext_turned)
    first_tail()
    for side in sides:
        side.wait_send(ID(), side.p1_send, side.id_recv)
        gather_terms(side, False)
        fill(side)
        put(side, 0)
    first_pass(2, diag_tiles, 0.5, rows.diag_term, cols.diag_term)
    for side in sides:
        side.wait_recv(ID(), side.p1_send, side.id_recv)
        learn(side, flag_ref)
    rows.tell(flag_ref)
    for side in sides:
        combine(side, 0, False)
        give_back(side, 0)
        put_done(side, 0)

    def sweep(t, final):
        slot, before = t % 2, (t + 1) % 2
        take_back(cols, before)
        row_pass(ext_tiles, cols.ext, rows.ext_turned, final)
        row_pass(tail_tiles, cols.tail, rows.tail_term, final)
        gather_terms(rows, final)
        fill(rows)
        put(rows, slot)
        take_back(rows, before)
        col_pass(ext_tiles, rows.ext, cols.ext_turned, final)
        col_pass(tail_tiles, rows.tail, cols.tail_term, final)
        gather_terms(cols, final)
        fill(cols)
        put(cols, slot)
        row_pass(diag_tiles, cols.own_turned, rows.diag_term, final)
        col_pass(diag_tiles, rows.own_turned, cols.diag_term, final)
        for side in sides:
            combine(side, slot, final)
            if not final:
                give_back(side, slot)
        for side in sides:
            put_done(side, slot)

    def middle(t, carry):
        sweep(t, False)
        return carry

    lax.fori_loop(1, SWEEPS, middle, 0)
    all_flags[...] = rows.told(flag_ref)
    cols.tell(all_flags)
    sweep(SWEEPS, True)

    height = DIAG // 2
    x, z = lax.div(rows.me, WIDTH), lax.rem(rows.me, WIDTH)

    def at(half, near, far):
        first, second = (z, x) if half == 0 else (x, z)
        first, second = lax.rem(first + near, WIDTH), lax.rem(second + far, WIDTH)
        return second * WIDTH + first if half == 0 else first * WIDTH + second

    def block(half, device):
        return row_out.at[pl.ds(pl.multiple_of(device * DIAG + half * height, 8), height)]

    def row_copy(half, source, sems, device):
        there = block(half, source[1])
        return pltpu.make_async_remote_copy(
            src_ref=source[0],
            dst_ref=there,
            send_sem=sems[0],
            recv_sem=sems[1],
            device_id={"col": device},
            device_id_type=MESH,
        )

    def near_copy(half, d, device, owner):
        sems = near_sems.at[0, half, d], near_sems.at[1, half, d]
        return row_copy(half, (rows.fin.at[pl.ds(half * height, height)], owner), sems, device)

    def far_copy(half, e, d, device, owner):
        sems = far_sems.at[0, half, e, d], far_sems.at[1, half, e, d]
        source = rows.fin.at[pl.ds(half * height, height)] if e == 0 else block(half, owner)
        return row_copy(half, (source, owner), sems, device)

    rows.fin[...] = rows.own[...]
    for d in range(1, WIDTH):
        for half in range(2):
            near_copy(half, d, at(half, d, 0), rows.me).start()
    cols.fin[...] = cols.own[...]
    col_place = col_out.at[pl.ds(pl.multiple_of(cols.me * DIAG, DIAG), DIAG)]
    for d in range(1, cols.count):
        cols.copy(LAST(), d, cols.fin, col_place, cols.partner(d)).start()
    for d in range(1, WIDTH):
        for half in range(2):
            far_copy(half, 0, d, at(half, 0, d), rows.me).start()
    row_place = row_out.at[pl.ds(pl.multiple_of(rows.me * DIAG, DIAG), DIAG)]
    kept = (
        pltpu.make_async_copy(rows.fin, row_place, out_sems.at[0]),
        pltpu.make_async_copy(cols.fin, col_place, out_sems.at[1]),
    )
    for copy in kept:
        copy.start()
    flag_out[0, 0] = jnp.max(cols.told(all_flags)).astype(jnp.int32)
    for e in range(1, WIDTH):
        for half in range(2):
            owner = at(half, WIDTH - e, 0)
            near_copy(half, e, owner, owner).wait_recv()
            for d in range(1, WIDTH):
                far_copy(half, e, d, at(half, 0, d), owner).start()
    for d in range(1, WIDTH):
        for half in range(2):
            for e in range(WIDTH):
                sender = at(half, 0, WIDTH - d)
                far_copy(half, e, d, sender, at(half, WIDTH - e, WIDTH - d)).wait_recv()
    for d in range(1, cols.count):
        peer = cols.sender(d)
        there = col_out.at[pl.ds(pl.multiple_of(peer * DIAG, DIAG), DIAG)]
        cols.copy(LAST(), d, cols.fin, there, peer).wait_recv()
        cols.copy(LAST(), d, cols.fin, col_place, cols.partner(d)).wait_send()
    for d in range(1, WIDTH):
        for half in range(2):
            near_copy(half, d, at(half, d, 0), rows.me).wait_send()
            for e in range(WIDTH):
                owner = at(half, WIDTH - e, 0) if e else rows.me
                far_copy(half, e, d, at(half, 0, d), owner).wait_send()
    for copy in kept:
        copy.wait()


def side_scratch(count, cap, tail_scale, tail_term):
    entries = padded(count * cap)
    return [
        pltpu.VMEM((DIAG, TILE), f32),
        pltpu.VMEM((TILE, DIAG), f32),
        pltpu.VMEM((TILE, TILE), f32),
        pltpu.VMEM((tail_scale, TILE), f32),
        pltpu.VMEM((TILE, DIAG), f32),
        pltpu.VMEM((TILE, TILE), f32),
        pltpu.VMEM((tail_term, TILE), f32),
        pltpu.VMEM((EXT, TILE), f32),
        pltpu.VMEM((entries, EXT), bf16),
        pltpu.VMEM((EXT, entries), bf16),
        pltpu.VMEM((LEVELS * DIAG, entries), bf16),
        pltpu.VMEM((entries, DIAG), bf16),
        pltpu.VMEM((entries, TILE), f32),
        pltpu.VMEM((entries, TILE), f32),
        pltpu.VMEM((2, entries, TILE), f32),
        pltpu.VMEM((entries, TILE), f32),
        pltpu.VMEM((2, entries, TILE), f32),
        pltpu.VMEM((DIAG, TILE), f32),
        pltpu.VMEM((count, 8, TILE), f32),
        pltpu.SemaphoreType.DMA((5, count)),
        pltpu.SemaphoreType.DMA((5, 2, count)),
    ]


def sparse(tiles, row_blocks, column_blocks, used_count, n_row, n_col):
    assert tiles.shape[0] == DIAG + TILE + TAIL and n_col == WIDTH * WIDTH
    return pl.pallas_call(
        functools.partial(kernel, n_row, n_col),
        out_shape=(
            jax.ShapeDtypeStruct((n_col * DIAG, TILE), f32),
            jax.ShapeDtypeStruct((n_row * DIAG, TILE), f32),
            jax.ShapeDtypeStruct((1, 1), jnp.int32),
        ),
        in_specs=[
            pl.BlockSpec(memory_space=pltpu.SMEM),
            pl.BlockSpec(memory_space=pltpu.VMEM),
            pl.BlockSpec(memory_space=pltpu.VMEM),
            pl.BlockSpec(memory_space=pltpu.HBM),
        ],
        out_specs=(
            pl.BlockSpec(memory_space=pl.ANY),
            pl.BlockSpec(memory_space=pl.ANY),
            pl.BlockSpec(memory_space=pltpu.SMEM),
        ),
        scratch_shapes=[
            pltpu.VMEM((TILE, TILE, DIAG), f32),
            pltpu.VMEM((TILE, TILE, TILE), f32),
            pltpu.VMEM((TILE, TAIL, TILE), f32),
            pltpu.VMEM((TAIL, TILE, TILE), f32),
            pltpu.VMEM((8, EXT), f32),
            pltpu.VMEM((8, TILE), f32),
            pltpu.VMEM((8, TILE), f32),
            pltpu.SemaphoreType.DMA((3, max(PARTS))),
            pltpu.SemaphoreType.DMA((2,)),
            pltpu.SemaphoreType.DMA((2, 2, WIDTH)),
            pltpu.SemaphoreType.DMA((2, 2, WIDTH, WIDTH)),
            *side_scratch(n_col, ROW_CAP, TAIL, TAIL),
            *side_scratch(n_row, COL_CAP, TILE, TILE),
        ],
        compiler_params=pltpu.CompilerParams(
            collective_id=0, has_side_effects=True, vmem_limit_bytes=52 << 20
        ),
    )(used_count.reshape(1, 1), row_blocks.reshape(1, -1), column_blocks.reshape(1, -1), tiles)


def gathered(x, axis):
    n = lax.axis_size(axis)
    me = lax.axis_index(axis)
    ring = [(i, (i + 1) % n) for i in range(n)]
    out = jnp.zeros((n,) + x.shape, x.dtype).at[me].set(x)

    def step(i, carry):
        out, y = carry
        y = lax.ppermute(y, axis, ring)
        return out.at[lax.rem(me + n - i, n)].set(y), y

    return lax.fori_loop(1, n, step, (out, x))[0]


def dense(blocks, row_blocks, column_blocks, used_count):
    slots, side = blocks.shape[:2]
    row_length = DIAG * lax.axis_size("col")
    column_length = DIAG * lax.axis_size("row")
    in_use = jnp.arange(slots, dtype=jnp.int32) < used_count
    magnitude = jnp.where(in_use[:, None, None], jnp.abs(blocks), f32(0.0))

    def sweep(t, carry):
        row_scale, column_scale = carry
        scaled = magnitude * row_scale[row_blocks][:, :, None] * column_scale[column_blocks][:, None, :]
        no_rows = jnp.zeros((row_length, side), f32)
        no_columns = jnp.zeros((column_length, side), f32)
        peak = t < SWEEPS

        def peaks():
            rows = no_rows.at[row_blocks].max(scaled.max(axis=2))
            columns = no_columns.at[column_blocks].max(scaled.max(axis=1))
            return rows, columns

        def totals():
            rows = no_rows.at[row_blocks].add(scaled.sum(axis=2))
            columns = no_columns.at[column_blocks].add(scaled.sum(axis=1))
            return rows, columns

        rows, columns = lax.cond(peak, peaks, totals)
        rows, columns = gathered(rows, "col"), gathered(columns, "row")
        rows = jnp.where(peak, rows.max(axis=0), rows.sum(axis=0))
        columns = jnp.where(peak, columns.max(axis=0), columns.sum(axis=0))
        return row_scale * lax.rsqrt(rows + epsilon), column_scale * lax.rsqrt(columns + epsilon)

    start = (jnp.ones((row_length, side), f32), jnp.ones((column_length, side), f32))
    return lax.fori_loop(0, SWEEPS + 1, sweep, start)


def on_device(tile_data, tile_rows, tile_cols, tile_counts):
    blocks = tile_data[0, 0]
    row_blocks = tile_rows[0, 0]
    column_blocks = tile_cols[0, 0]
    used_count = tile_counts[0, 0]
    n_row, n_col = lax.axis_size("row"), lax.axis_size("col")
    row_scale, column_scale, flag = sparse(blocks, row_blocks, column_blocks, used_count, n_row, n_col)
    row_scale, column_scale = lax.cond(
        flag[0, 0] > 0,
        lambda: dense(blocks, row_blocks, column_blocks, used_count),
        lambda: (row_scale, column_scale),
    )
    return (row_scale.reshape(-1), column_scale.reshape(-1))


def solution(mesh):
    placed = (
        P("row", "col", None, None, None),
        P("row", "col", None),
        P("row", "col", None),
        P("row", "col"),
    )
    return jax.shard_map(
        on_device, mesh=mesh, in_specs=placed, out_specs=(P("row"), P("col")), check_vma=False
    )
```

```python
import functools

import jax
import jax.numpy as jnp
from jax import lax
from jax.experimental import pallas as pl
from jax.experimental.pallas import tpu as pltpu
from jax.sharding import PartitionSpec as P

TILE = 128
DIAG = 128
SWEEPS = 4
epsilon = 1e-06

EXT = 256
ROW_CAP = 24
COL_CAP = 40
LEVELS = 8
GROUP = 8
PARTS = (2, 1, 1)
PIECE = 256
HOPS = (0, 1, 2, 1)
WIDTH = 4
TAIL = 32
QUARTERS = TILE // TAIL

f32 = jnp.float32
bf16 = jnp.bfloat16
MESH = pltpu.DeviceIdType.MESH if hasattr(pltpu, "DeviceIdType") else pl.DeviceIdType.MESH


def halves(x):
    hi = x.astype(bf16)
    lo = (x - hi.astype(f32)).astype(bf16)
    return jnp.concatenate([hi, lo], axis=1)


def select_rows(onehot, x):
    y = jnp.dot(onehot, halves(x), preferred_element_type=f32)
    return y[:, :TILE] + y[:, TILE:]


def iota(shape, dim):
    return lax.broadcasted_iota(jnp.int32, shape, dim).astype(f32)


def columns(row):
    parts = [
        jnp.broadcast_to(row[:, i : i + TILE], (TILE, TILE)).T for i in range(0, row.shape[1], TILE)
    ]
    return jnp.concatenate(parts, axis=0)


def earlier_equal(cols, rows):
    count = cols.shape[0] // TILE
    out = []
    before = iota((TILE, TILE), 0) < iota((TILE, TILE), 1)
    for b in range(count):
        total = jnp.zeros((1, TILE), f32)
        here = rows[b]
        for a in range(b + 1):
            same = cols[a * TILE : (a + 1) * TILE] == here
            if a == b:
                same = same & before
            total = total + jnp.sum(jnp.where(same, 1.0, 0.0), axis=0, keepdims=True)
        out.append(total)
    return out


def padded(entries):
    return -(-entries // TILE) * TILE


class Side:
    def __init__(self, axis, count, cap, key_row, refs):
        self.axis, self.count, self.cap, self.key_row = axis, count, cap, key_row
        self.entries = padded(count * cap)
        (
            self.own,
            self.own_turned,
            self.ext,
            self.tail,
            self.diag_term,
            self.ext_turned,
            self.tail_term,
            self.ext_term,
            self.pack,
            self.unpack,
            self.levels,
            self.expand,
            self.id_recv,
            self.p1_send,
            self.p1_recv,
            self.p2_send,
            self.p2_recv,
            self.fin,
            self.flags,
            self.send_sems,
            self.recv_sems,
        ) = refs
        self.me = lax.axis_index(axis)
        self.minor = minor = count // WIDTH
        steps = [(a, b) for a in range(WIDTH) for b in range(minor) if a or b]
        self.steps = sorted(steps, key=lambda s: -sum(HOPS[i] for i in s))
        self.major_me, self.minor_me = lax.div(self.me, minor), lax.rem(self.me, minor)

    def shifted(self, a, b):
        return lax.rem(self.major_me + a, WIDTH) * self.minor + lax.rem(self.minor_me + b, self.minor)

    def partner(self, d):
        a, b = self.steps[d - 1]
        return self.shifted(a, b)

    def sender(self, d):
        a, b = self.steps[d - 1]
        return self.shifted(WIDTH - a, self.minor - b)

    def copy(self, kind, d, src, dst, peer):
        kind, slot = kind
        return pltpu.make_async_remote_copy(
            src_ref=src,
            dst_ref=dst,
            send_sem=self.send_sems.at[kind, d],
            recv_sem=self.recv_sems.at[kind, slot, d],
            device_id={self.axis: peer},
            device_id_type=MESH,
        )

    def place(self, ref, peer):
        return ref.at[pl.ds(pl.multiple_of(peer * self.cap, 8), self.cap)]

    def send(self, kind, send, recv):
        for d in range(1, self.count):
            peer = self.partner(d)
            self.copy(kind, d, self.place(send, peer), self.place(recv, self.me), peer).start()
        self.place(recv, self.me)[...] = self.place(send, self.me)[...]

    def wait_send(self, kind, send, recv):
        for d in range(1, self.count):
            peer = self.partner(d)
            self.copy(kind, d, self.place(send, peer), self.place(recv, self.me), peer).wait_send()

    def wait_recv(self, kind, send, recv):
        for d in range(1, self.count):
            peer = self.sender(d)
            self.copy(kind, d, self.place(send, peer), self.place(recv, peer), peer).wait_recv()

    def tell(self, flag_ref):
        for d in range(1, self.count):
            self.copy((4, 0), d, flag_ref, self.flags.at[self.me], self.partner(d)).start()
        self.flags[self.me] = flag_ref[...]

    def told(self, flag_ref):
        for d in range(1, self.count):
            peer = self.sender(d)
            self.copy((4, 0), d, flag_ref, self.flags.at[peer], peer).wait_recv()
            self.copy((4, 0), d, flag_ref, self.flags.at[self.me], self.partner(d)).wait_send()
        return jnp.max(self.flags[...], axis=0)


def ID():
    return (0, 0)


def FIRST(slot):
    return (1, slot)


def BACK(slot):
    return (2, slot)


def LAST():
    return (3, 0)


def prepare(side, blocks_ref, used_count, key_ref, flag_ref):
    cap, entries = side.cap, side.entries
    blocks = blocks_ref[...].astype(f32)
    key_ref[...] = jnp.full_like(key_ref, -1.0)
    key_ref[0:1, :TILE] = blocks[:, DIAG : DIAG + TILE]
    key_ref[0:1, TILE : TILE + TAIL] = blocks[:, DIAG + TILE :]
    slot = lax.broadcasted_iota(jnp.int32, (1, EXT), 1) + DIAG
    key = jnp.where(slot < used_count, key_ref[0:1, :], -1.0)
    owner = jnp.floor(key * (1.0 / DIAG))
    local = key - owner * DIAG
    used = key >= 0.0
    owner_cols = columns(owner)
    rank = earlier_equal(owner_cols, [owner[:, :TILE], owner[:, TILE:]])
    rank = jnp.concatenate(rank, axis=1)
    fits = used & (rank < float(cap))
    dest = jnp.where(fits, owner * cap + rank, -1.0)
    over = jnp.where(used & (rank >= float(cap)), 1.0, 0.0)
    flag_ref[...] = jnp.maximum(flag_ref[...], jnp.max(over, axis=1, keepdims=True))
    side.pack[...] = jnp.where(iota((entries, EXT), 0) == dest, 1.0, 0.0).astype(bf16)
    dest_cols = columns(dest)
    for i in range(0, entries, TILE):
        lanes = iota((EXT, TILE), 1) + float(i)
        side.unpack[:, i : i + TILE] = jnp.where(dest_cols == lanes, 1.0, 0.0).astype(bf16)
    side.ext_term[...] = jnp.where(columns(jnp.where(used, 1.0, 0.0)) > 0.0, columns(local) + 1.0, 0.0)


def fill(side):
    side.p1_send[...] = select_rows(side.pack[...], side.ext_term[...])


def learn(side, flag_ref):
    entries = side.entries
    ids = side.id_recv[...]
    lanes = iota((TILE, TILE), 1)
    rows = []
    for i in range(0, entries, TILE):
        block = ids[i : i + TILE]
        side.expand[i : i + TILE, :] = jnp.where(block == lanes + 1.0, 1.0, 0.0).astype(bf16)
        rows.append(block.T)
    level = earlier_equal(ids, rows)
    wanted = iota((TILE, TILE), 0) + 1.0
    over = jnp.zeros((1, TILE), f32)
    for b, i in enumerate(range(0, entries, TILE)):
        hit = rows[b] == wanted
        over = jnp.maximum(
            over, jnp.where((rows[b][0:1] > 0.0) & (level[b] >= float(LEVELS)), 1.0, 0.0)
        )
        for t in range(LEVELS):
            side.levels[t * TILE : (t + 1) * TILE, i : i + TILE] = jnp.where(
                hit & (level[b] == float(t)), 1.0, 0.0
            ).astype(bf16)
    flag_ref[...] = jnp.maximum(flag_ref[...], jnp.max(over, axis=1, keepdims=True))


def put(side, slot):
    side.send(FIRST(slot), side.p1_send, side.p1_recv.at[slot])


def put_done(side, slot):
    side.wait_send(FIRST(slot), side.p1_send, side.p1_recv.at[slot])


def combine(side, slot, final):
    recv = side.p1_recv.at[slot]
    side.wait_recv(FIRST(slot), side.p1_send, recv)
    terms = select_rows(side.levels[...], recv[...])
    terms = terms.reshape(LEVELS, TILE, TILE)
    if final:
        total = side.diag_term[...].T + jnp.sum(terms, axis=0)
    else:
        total = jnp.maximum(side.diag_term[...].T, jnp.max(terms, axis=0))
    own = side.own[...]
    own = own * lax.rsqrt((2.0 * total) * own + epsilon)
    side.own[...] = own
    side.own_turned[...] = own.T


def give_back(side, slot):
    side.p2_send[...] = select_rows(side.expand[...], side.own[...])
    side.send(BACK(slot), side.p2_send, side.p2_recv.at[slot])


def take_back(side, slot):
    recv = side.p2_recv.at[slot]
    side.wait_recv(BACK(slot), side.p2_send, recv)
    scale = select_rows(side.unpack[...], recv[...])
    side.ext[...] = scale[:TILE].T
    tail = scale[TILE : TILE + TAIL]
    if side.axis == "col":
        tail = [tail] + [pltpu.roll(tail, TILE - q * TAIL, 1) for q in range(1, QUARTERS)]
        side.tail[...] = jnp.concatenate(tail, axis=0).T[:TAIL]
    else:
        side.tail[...] = jnp.concatenate([tail] * QUARTERS, axis=0).T
    side.wait_send(BACK(slot), side.p2_send, recv)


def gather_terms(side, final):
    side.ext_term[:TILE, :] = side.ext_turned[...].T
    if side.axis == "col":
        empty = jnp.zeros((TILE - TAIL, TILE), f32)
        turned = jnp.concatenate([side.tail_term[...], empty], axis=0).T
        parts = [turned[:TAIL]]
        parts += [pltpu.roll(turned[q * TAIL : (q + 1) * TAIL], q * TAIL, 1) for q in range(1, QUARTERS)]
        side.ext_term[TILE : TILE + TAIL, :] = parts[0] + parts[1] + parts[2] + parts[3]
    else:
        parts = side.tail_term[...].T.reshape(QUARTERS, TAIL, TILE)
        side.ext_term[TILE : TILE + TAIL, :] = jnp.sum(parts, axis=0) if final else jnp.max(parts, axis=0)


def row_pass(tiles, scale, out, final):
    scale = scale[...]

    def step(g, carry):
        base = pl.multiple_of(g * GROUP, GROUP)
        results = []
        for j in range(GROUP):
            x = tiles[base + j] * scale
            reduce = jnp.sum if final else jnp.max
            results.append(reduce(x, axis=0, keepdims=True))
        out[pl.ds(base, GROUP), :] = jnp.concatenate(results, axis=0)
        return carry

    lax.fori_loop(0, tiles.shape[0] // GROUP, step, 0)


def col_pass(tiles, scale, out, final):
    def step(g, total):
        base = pl.multiple_of(g * GROUP, GROUP)
        for j in range(GROUP):
            x = tiles[base + j] * scale[pl.ds(base + j, 1), :]
            total = total + x if final else jnp.maximum(total, x)
        return total

    out[...] = lax.fori_loop(0, tiles.shape[0] // GROUP, step, jnp.zeros((TILE, TILE), f32))


def kernel(
    n_row,
    n_col,
    count_ref,
    rows_ref,
    cols_ref,
    data_ref,
    row_out,
    col_out,
    flag_out,
    diag_tiles,
    ext_tiles,
    tail_loaded,
    tail_tiles,
    key_ref,
    flag_ref,
    all_flags,
    load_sems,
    out_sems,
    near_sems,
    far_sems,
    *rest,
):
    rows = Side("col", n_col, ROW_CAP, 0, rest[: len(rest) // 2])
    cols = Side("row", n_row, COL_CAP, 1, rest[len(rest) // 2 :])
    sides = (cols, rows)

    barrier = pltpu.get_barrier_semaphore()
    for side in sides:
        for d in range(1, side.count):
            pl.semaphore_signal(barrier, inc=1, device_id={side.axis: side.partner(d)}, device_id_type=MESH)

    def load(group, part):
        tiles, first, count = ((ext_tiles, DIAG, TILE), (tail_loaded, DIAG + TILE, TAIL), (diag_tiles, 0, DIAG))[group]
        height = TILE // PARTS[group]
        at = part * height
        sem = load_sems.at[group, part]

        def step(s, carry):
            for j in range(GROUP):
                slot = s * GROUP + j
                pltpu.make_async_copy(
                    data_ref.at[first + slot, pl.ds(at, height)], tiles.at[pl.ds(at, height), slot], sem
                ).start()
            return carry

        lax.fori_loop(0, count // GROUP, step, 0)

    def loaded(group, part):
        tiles = (ext_tiles, tail_loaded, diag_tiles)[group]
        height = TILE // PARTS[group]
        whole = tiles.at[pl.ds(part * height, height)]
        pltpu.make_async_copy(whole, whole, load_sems.at[group, part]).wait()

    for group in range(2):
        for part in range(PARTS[group]):
            load(group, part)

    flag_ref[...] = jnp.zeros_like(flag_ref)
    count = count_ref[0, 0]
    for side, blocks_ref in ((cols, cols_ref), (rows, rows_ref)):
        prepare(side, blocks_ref, count, key_ref, flag_ref)
        for ref in (side.id_recv, side.p1_recv, side.p2_recv):
            empty = side.entries - side.count * side.cap
            if empty:
                ref[..., side.entries - empty :, :] = jnp.zeros((*ref.shape[:-2], empty, TILE), f32)
    for side in sides:
        fill(side)
    pl.semaphore_wait(barrier, n_row + n_col - 2)
    for side in sides:
        side.send(ID(), side.p1_send, side.id_recv)

    for part in range(PARTS[2]):
        load(2, part)

    lane = lax.broadcasted_iota(jnp.int32, (1, TILE), 1)
    ext_half = jnp.where(lane + DIAG < count, 0.5, 0.0)
    tail_half = jnp.where(lane % TAIL + (DIAG + TILE) < count, 0.5, 0.0)

    def first_pass(group, tiles, half, row_term, col_term):
        total = jnp.zeros((TILE, TILE), f32)
        steps = TILE // PARTS[group] // GROUP
        for part in range(PARTS[group]):
            loaded(group, part)

            def step(g, total):
                base = pl.multiple_of(g * GROUP, GROUP)
                results = []
                for j in range(GROUP):
                    x = jnp.abs(tiles[base + j]).T * half
                    tiles[base + j] = x
                    results.append(jnp.max(x, axis=0, keepdims=True))
                    total = jnp.maximum(total, x)
                row_term[pl.ds(base, GROUP), :] = jnp.concatenate(results, axis=0)
                return total

            total = lax.fori_loop(part * steps, (part + 1) * steps, step, total)
        col_term[...] = total

    def first_tail():
        loaded(1, 0)

        def step(g, total):
            base = pl.multiple_of(g * GROUP, GROUP)
            results = []
            for j in range(GROUP):
                x = jnp.concatenate([tail_loaded[q * TAIL + base + j] for q in range(QUARTERS)], axis=0)
                x = jnp.abs(x).T * tail_half
                tail_tiles[base + j] = x
                results.append(jnp.max(x, axis=0, keepdims=True))
                total = jnp.maximum(total, x)
            rows.tail_term[pl.ds(base, GROUP), :] = jnp.concatenate(results, axis=0)
            return total

        cols.tail_term[...] = lax.fori_loop(0, TAIL // GROUP, step, jnp.zeros((TILE, TILE), f32))

    for side in sides:
        side.ext_term[...] = jnp.zeros_like(side.ext_term)
        side.own[...] = jnp.ones_like(side.own)
    first_pass(0, ext_tiles, ext_half, rows.ext_turned, cols.ext_turned)
    first_tail()
    for side in sides:
        side.wait_send(ID(), side.p1_send, side.id_recv)
        gather_terms(side, False)
        fill(side)
        put(side, 0)
    first_pass(2, diag_tiles, 0.5, rows.diag_term, cols.diag_term)
    for side in sides:
        side.wait_recv(ID(), side.p1_send, side.id_recv)
        learn(side, flag_ref)
    rows.tell(flag_ref)
    for side in sides:
        combine(side, 0, False)
        give_back(side, 0)
        put_done(side, 0)

    def row_step(slot, before, final):
        take_back(cols, before)
        row_pass(ext_tiles, cols.ext, rows.ext_turned, final)
        row_pass(tail_tiles, cols.tail, rows.tail_term, final)
        gather_terms(rows, final)
        fill(rows)
        put(rows, slot)

    def col_step(slot, before, final):
        take_back(rows, before)
        col_pass(ext_tiles, rows.ext, cols.ext_turned, final)
        col_pass(tail_tiles, rows.tail, cols.tail_term, final)
        gather_terms(cols, final)
        fill(cols)
        put(cols, slot)

    def sweep(t, final):
        slot, before = t % 2, (t + 1) % 2
        first, second = (row_step, col_step) if t % 2 else (col_step, row_step)
        first(slot, before, final)
        second(slot, before, final)
        row_pass(diag_tiles, cols.own_turned, rows.diag_term, final)
        col_pass(diag_tiles, rows.own_turned, cols.diag_term, final)
        for side in (rows, cols) if t % 2 else (cols, rows):
            combine(side, slot, final)
            if not final:
                give_back(side, slot)
        for side in sides:
            put_done(side, slot)

    for t in range(1, SWEEPS):
        sweep(t, False)
    all_flags[...] = rows.told(flag_ref)
    cols.tell(all_flags)
    sweep(SWEEPS, True)

    height = DIAG // 2
    x, z = lax.div(rows.me, WIDTH), lax.rem(rows.me, WIDTH)

    def at(half, near, far):
        first, second = (z, x) if half == 0 else (x, z)
        first, second = lax.rem(first + near, WIDTH), lax.rem(second + far, WIDTH)
        return second * WIDTH + first if half == 0 else first * WIDTH + second

    def block(half, device):
        return row_out.at[pl.ds(pl.multiple_of(device * DIAG + half * height, 8), height)]

    def row_copy(half, source, sems, device):
        there = block(half, source[1])
        return pltpu.make_async_remote_copy(
            src_ref=source[0],
            dst_ref=there,
            send_sem=sems[0],
            recv_sem=sems[1],
            device_id={"col": device},
            device_id_type=MESH,
        )

    def near_copy(half, d, device, owner):
        sems = near_sems.at[0, half, d], near_sems.at[1, half, d]
        return row_copy(half, (rows.fin.at[pl.ds(half * height, height)], owner), sems, device)

    def far_copy(half, e, d, device, owner):
        sems = far_sems.at[0, half, e, d], far_sems.at[1, half, e, d]
        source = rows.fin.at[pl.ds(half * height, height)] if e == 0 else block(half, owner)
        return row_copy(half, (source, owner), sems, device)

    rows.fin[...] = rows.own[...]
    for d in range(1, WIDTH):
        for half in range(2):
            near_copy(half, d, at(half, d, 0), rows.me).start()
    cols.fin[...] = cols.own[...]
    col_place = col_out.at[pl.ds(pl.multiple_of(cols.me * DIAG, DIAG), DIAG)]
    for d in range(1, cols.count):
        cols.copy(LAST(), d, cols.fin, col_place, cols.partner(d)).start()
    for d in range(1, WIDTH):
        for half in range(2):
            far_copy(half, 0, d, at(half, 0, d), rows.me).start()
    row_place = row_out.at[pl.ds(pl.multiple_of(rows.me * DIAG, DIAG), DIAG)]
    kept = (
        pltpu.make_async_copy(rows.fin, row_place, out_sems.at[0]),
        pltpu.make_async_copy(cols.fin, col_place, out_sems.at[1]),
    )
    for copy in kept:
        copy.start()
    flag_out[0, 0] = jnp.max(cols.told(all_flags)).astype(jnp.int32)
    for e in range(1, WIDTH):
        for half in range(2):
            owner = at(half, WIDTH - e, 0)
            near_copy(half, e, owner, owner).wait_recv()
            for d in range(1, WIDTH):
                far_copy(half, e, d, at(half, 0, d), owner).start()
    for d in range(1, WIDTH):
        for half in range(2):
            for e in range(WIDTH):
                sender = at(half, 0, WIDTH - d)
                far_copy(half, e, d, sender, at(half, WIDTH - e, WIDTH - d)).wait_recv()
    for d in range(1, cols.count):
        peer = cols.sender(d)
        there = col_out.at[pl.ds(pl.multiple_of(peer * DIAG, DIAG), DIAG)]
        cols.copy(LAST(), d, cols.fin, there, peer).wait_recv()
        cols.copy(LAST(), d, cols.fin, col_place, cols.partner(d)).wait_send()
    for d in range(1, WIDTH):
        for half in range(2):
            near_copy(half, d, at(half, d, 0), rows.me).wait_send()
            for e in range(WIDTH):
                owner = at(half, WIDTH - e, 0) if e else rows.me
                far_copy(half, e, d, at(half, 0, d), owner).wait_send()
    for copy in kept:
        copy.wait()


def side_scratch(count, cap, tail_scale, tail_term):
    entries = padded(count * cap)
    return [
        pltpu.VMEM((DIAG, TILE), f32),
        pltpu.VMEM((TILE, DIAG), f32),
        pltpu.VMEM((TILE, TILE), f32),
        pltpu.VMEM((tail_scale, TILE), f32),
        pltpu.VMEM((TILE, DIAG), f32),
        pltpu.VMEM((TILE, TILE), f32),
        pltpu.VMEM((tail_term, TILE), f32),
        pltpu.VMEM((EXT, TILE), f32),
        pltpu.VMEM((entries, EXT), bf16),
        pltpu.VMEM((EXT, entries), bf16),
        pltpu.VMEM((LEVELS * DIAG, entries), bf16),
        pltpu.VMEM((entries, DIAG), bf16),
        pltpu.VMEM((entries, TILE), f32),
        pltpu.VMEM((entries, TILE), f32),
        pltpu.VMEM((2, entries, TILE), f32),
        pltpu.VMEM((entries, TILE), f32),
        pltpu.VMEM((2, entries, TILE), f32),
        pltpu.VMEM((DIAG, TILE), f32),
        pltpu.VMEM((count, 8, TILE), f32),
        pltpu.SemaphoreType.DMA((5, count)),
        pltpu.SemaphoreType.DMA((5, 2, count)),
    ]


def sparse(tiles, row_blocks, column_blocks, used_count, n_row, n_col):
    assert tiles.shape[0] == DIAG + TILE + TAIL and n_col == WIDTH * WIDTH
    return pl.pallas_call(
        functools.partial(kernel, n_row, n_col),
        out_shape=(
            jax.ShapeDtypeStruct((n_col * DIAG, TILE), f32),
            jax.ShapeDtypeStruct((n_row * DIAG, TILE), f32),
            jax.ShapeDtypeStruct((1, 1), jnp.int32),
        ),
        in_specs=[
            pl.BlockSpec(memory_space=pltpu.SMEM),
            pl.BlockSpec(memory_space=pltpu.VMEM),
            pl.BlockSpec(memory_space=pltpu.VMEM),
            pl.BlockSpec(memory_space=pltpu.HBM),
        ],
        out_specs=(
            pl.BlockSpec(memory_space=pl.ANY),
            pl.BlockSpec(memory_space=pl.ANY),
            pl.BlockSpec(memory_space=pltpu.SMEM),
        ),
        scratch_shapes=[
            pltpu.VMEM((TILE, TILE, DIAG), f32),
            pltpu.VMEM((TILE, TILE, TILE), f32),
            pltpu.VMEM((TILE, TAIL, TILE), f32),
            pltpu.VMEM((TAIL, TILE, TILE), f32),
            pltpu.VMEM((8, EXT), f32),
            pltpu.VMEM((8, TILE), f32),
            pltpu.VMEM((8, TILE), f32),
            pltpu.SemaphoreType.DMA((3, max(PARTS))),
            pltpu.SemaphoreType.DMA((2,)),
            pltpu.SemaphoreType.DMA((2, 2, WIDTH)),
            pltpu.SemaphoreType.DMA((2, 2, WIDTH, WIDTH)),
            *side_scratch(n_col, ROW_CAP, TAIL, TAIL),
            *side_scratch(n_row, COL_CAP, TILE, TILE),
        ],
        compiler_params=pltpu.CompilerParams(
            collective_id=0, has_side_effects=True, vmem_limit_bytes=52 << 20
        ),
    )(used_count.reshape(1, 1), row_blocks.reshape(1, -1), column_blocks.reshape(1, -1), tiles)


def settle_kernel(row_ref, col_ref, row_out, col_out, sems):
    copies = []
    for ref, out in ((row_ref, row_out), (col_ref, col_out)):
        for i in range(ref.shape[0] // PIECE):
            at = pl.ds(i * PIECE, PIECE)
            copies.append(pltpu.make_async_copy(ref.at[at], out.at[at], sems.at[len(copies)]))
    for copy in copies:
        copy.start()
    for copy in copies:
        copy.wait()


def settle(row_scale, column_scale):
    pieces = (row_scale.shape[0] + column_scale.shape[0]) // PIECE
    anywhere = pl.BlockSpec(memory_space=pl.ANY)
    return pl.pallas_call(
        settle_kernel,
        out_shape=tuple(jax.ShapeDtypeStruct(x.shape, x.dtype) for x in (row_scale, column_scale)),
        in_specs=[anywhere, anywhere],
        out_specs=(anywhere, anywhere),
        scratch_shapes=[pltpu.SemaphoreType.DMA((pieces,))],
    )(row_scale, column_scale)


def gathered(x, axis):
    n = lax.axis_size(axis)
    me = lax.axis_index(axis)
    ring = [(i, (i + 1) % n) for i in range(n)]
    out = jnp.zeros((n,) + x.shape, x.dtype).at[me].set(x)

    def step(i, carry):
        out, y = carry
        y = lax.ppermute(y, axis, ring)
        return out.at[lax.rem(me + n - i, n)].set(y), y

    return lax.fori_loop(1, n, step, (out, x))[0]


def dense(blocks, row_blocks, column_blocks, used_count):
    slots, side = blocks.shape[:2]
    row_length = DIAG * lax.axis_size("col")
    column_length = DIAG * lax.axis_size("row")
    in_use = jnp.arange(slots, dtype=jnp.int32) < used_count
    magnitude = jnp.where(in_use[:, None, None], jnp.abs(blocks), f32(0.0))

    def sweep(t, carry):
        row_scale, column_scale = carry
        scaled = magnitude * row_scale[row_blocks][:, :, None] * column_scale[column_blocks][:, None, :]
        no_rows = jnp.zeros((row_length, side), f32)
        no_columns = jnp.zeros((column_length, side), f32)
        peak = t < SWEEPS

        def peaks():
            rows = no_rows.at[row_blocks].max(scaled.max(axis=2))
            columns = no_columns.at[column_blocks].max(scaled.max(axis=1))
            return rows, columns

        def totals():
            rows = no_rows.at[row_blocks].add(scaled.sum(axis=2))
            columns = no_columns.at[column_blocks].add(scaled.sum(axis=1))
            return rows, columns

        rows, columns = lax.cond(peak, peaks, totals)
        rows, columns = gathered(rows, "col"), gathered(columns, "row")
        rows = jnp.where(peak, rows.max(axis=0), rows.sum(axis=0))
        columns = jnp.where(peak, columns.max(axis=0), columns.sum(axis=0))
        return row_scale * lax.rsqrt(rows + epsilon), column_scale * lax.rsqrt(columns + epsilon)

    start = (jnp.ones((row_length, side), f32), jnp.ones((column_length, side), f32))
    return lax.fori_loop(0, SWEEPS + 1, sweep, start)


def on_device(tile_data, tile_rows, tile_cols, tile_counts):
    blocks = tile_data[0, 0]
    row_blocks = tile_rows[0, 0]
    column_blocks = tile_cols[0, 0]
    used_count = tile_counts[0, 0]
    n_row, n_col = lax.axis_size("row"), lax.axis_size("col")
    row_scale, column_scale, flag = sparse(blocks, row_blocks, column_blocks, used_count, n_row, n_col)
    row_scale, column_scale = lax.cond(
        flag[0, 0] > 0,
        lambda: dense(blocks, row_blocks, column_blocks, used_count),
        lambda: settle(row_scale, column_scale),
    )
    return (row_scale.reshape(-1), column_scale.reshape(-1))


def solution(mesh):
    placed = (
        P("row", "col", None, None, None),
        P("row", "col", None),
        P("row", "col", None),
        P("row", "col"),
    )
    return jax.shard_map(
        on_device, mesh=mesh, in_specs=placed, out_specs=(P("row"), P("col")), check_vma=False
    )
```

```python
import functools

import jax
import jax.numpy as jnp
from jax import lax
from jax.experimental import pallas as pl
from jax.experimental.pallas import tpu as pltpu
from jax.sharding import PartitionSpec as P

TILE = 128
DIAG = 128
SWEEPS = 4
epsilon = 1e-06

EXT = 256
ROW_CAP = 24
COL_CAP = 40
LEVELS = 8
GROUP = 8
PARTS = (2, 1, 1)
PIECE = 256
HOPS = (0, 1, 2, 1)
WIDTH = 4
TAIL = 32
QUARTERS = TILE // TAIL

f32 = jnp.float32
bf16 = jnp.bfloat16
MESH = pltpu.DeviceIdType.MESH if hasattr(pltpu, "DeviceIdType") else pl.DeviceIdType.MESH


def halves(x):
    hi = x.astype(bf16)
    lo = (x - hi.astype(f32)).astype(bf16)
    return jnp.concatenate([hi, lo], axis=1)


def select_rows(onehot, x):
    y = jnp.dot(onehot, halves(x), preferred_element_type=f32)
    return y[:, :TILE] + y[:, TILE:]


def iota(shape, dim):
    return lax.broadcasted_iota(jnp.int32, shape, dim).astype(f32)


def columns(row):
    parts = [
        jnp.broadcast_to(row[:, i : i + TILE], (TILE, TILE)).T for i in range(0, row.shape[1], TILE)
    ]
    return jnp.concatenate(parts, axis=0)


def earlier_equal(cols, rows):
    count = cols.shape[0] // TILE
    out = []
    before = iota((TILE, TILE), 0) < iota((TILE, TILE), 1)
    for b in range(count):
        total = jnp.zeros((1, TILE), f32)
        here = rows[b]
        for a in range(b + 1):
            same = cols[a * TILE : (a + 1) * TILE] == here
            if a == b:
                same = same & before
            total = total + jnp.sum(jnp.where(same, 1.0, 0.0), axis=0, keepdims=True)
        out.append(total)
    return out


def padded(entries):
    return -(-entries // TILE) * TILE


class Side:
    def __init__(self, axis, count, cap, key_row, refs):
        self.axis, self.count, self.cap, self.key_row = axis, count, cap, key_row
        self.entries = padded(count * cap)
        (
            self.own,
            self.own_turned,
            self.ext,
            self.tail,
            self.diag_term,
            self.ext_turned,
            self.tail_term,
            self.ext_term,
            self.pack,
            self.unpack,
            self.levels,
            self.expand,
            self.id_recv,
            self.p1_send,
            self.p1_recv,
            self.p2_send,
            self.p2_recv,
            self.fin,
            self.flags,
            self.send_sems,
            self.recv_sems,
        ) = refs
        self.me = lax.axis_index(axis)
        self.minor = minor = count // WIDTH
        steps = [(a, b) for a in range(WIDTH) for b in range(minor) if a or b]
        self.steps = sorted(steps, key=lambda s: -sum(HOPS[i] for i in s))
        self.major_me, self.minor_me = lax.div(self.me, minor), lax.rem(self.me, minor)

    def shifted(self, a, b):
        return lax.rem(self.major_me + a, WIDTH) * self.minor + lax.rem(self.minor_me + b, self.minor)

    def partner(self, d):
        a, b = self.steps[d - 1]
        return self.shifted(a, b)

    def sender(self, d):
        a, b = self.steps[d - 1]
        return self.shifted(WIDTH - a, self.minor - b)

    def copy(self, kind, d, src, dst, peer):
        kind, slot = kind
        return pltpu.make_async_remote_copy(
            src_ref=src,
            dst_ref=dst,
            send_sem=self.send_sems.at[kind, d],
            recv_sem=self.recv_sems.at[kind, slot, d],
            device_id={self.axis: peer},
            device_id_type=MESH,
        )

    def place(self, ref, peer):
        return ref.at[pl.ds(pl.multiple_of(peer * self.cap, 8), self.cap)]

    def send(self, kind, send, recv):
        for d in range(1, self.count):
            peer = self.partner(d)
            self.copy(kind, d, self.place(send, peer), self.place(recv, self.me), peer).start()
        self.place(recv, self.me)[...] = self.place(send, self.me)[...]

    def wait_send(self, kind, send, recv):
        for d in range(1, self.count):
            peer = self.partner(d)
            self.copy(kind, d, self.place(send, peer), self.place(recv, self.me), peer).wait_send()

    def wait_recv(self, kind, send, recv):
        for d in range(1, self.count):
            peer = self.sender(d)
            self.copy(kind, d, self.place(send, peer), self.place(recv, peer), peer).wait_recv()

    def tell(self, flag_ref):
        for d in range(1, self.count):
            self.copy((4, 0), d, flag_ref, self.flags.at[self.me], self.partner(d)).start()
        self.flags[self.me] = flag_ref[...]

    def told(self, flag_ref):
        for d in range(1, self.count):
            peer = self.sender(d)
            self.copy((4, 0), d, flag_ref, self.flags.at[peer], peer).wait_recv()
            self.copy((4, 0), d, flag_ref, self.flags.at[self.me], self.partner(d)).wait_send()
        return jnp.max(self.flags[...], axis=0)


def ID():
    return (0, 0)


def FIRST(slot):
    return (1, slot)


def BACK(slot):
    return (2, slot)


def prepare(side, blocks_ref, used_count, key_ref, flag_ref):
    cap, entries = side.cap, side.entries
    blocks = blocks_ref[...].astype(f32)
    key_ref[...] = jnp.full_like(key_ref, -1.0)
    key_ref[0:1, :TILE] = blocks[:, DIAG : DIAG + TILE]
    key_ref[0:1, TILE : TILE + TAIL] = blocks[:, DIAG + TILE :]
    slot = lax.broadcasted_iota(jnp.int32, (1, EXT), 1) + DIAG
    key = jnp.where(slot < used_count, key_ref[0:1, :], -1.0)
    owner = jnp.floor(key * (1.0 / DIAG))
    local = key - owner * DIAG
    used = key >= 0.0
    owner_cols = columns(owner)
    rank = earlier_equal(owner_cols, [owner[:, :TILE], owner[:, TILE:]])
    rank = jnp.concatenate(rank, axis=1)
    fits = used & (rank < float(cap))
    dest = jnp.where(fits, owner * cap + rank, -1.0)
    over = jnp.where(used & (rank >= float(cap)), 1.0, 0.0)
    flag_ref[...] = jnp.maximum(flag_ref[...], jnp.max(over, axis=1, keepdims=True))
    side.pack[...] = jnp.where(iota((entries, EXT), 0) == dest, 1.0, 0.0).astype(bf16)
    dest_cols = columns(dest)
    for i in range(0, entries, TILE):
        lanes = iota((EXT, TILE), 1) + float(i)
        side.unpack[:, i : i + TILE] = jnp.where(dest_cols == lanes, 1.0, 0.0).astype(bf16)
    side.ext_term[...] = jnp.where(columns(jnp.where(used, 1.0, 0.0)) > 0.0, columns(local) + 1.0, 0.0)


def fill(side):
    side.p1_send[...] = select_rows(side.pack[...], side.ext_term[...])


def learn(side, flag_ref):
    entries = side.entries
    ids = side.id_recv[...]
    lanes = iota((TILE, TILE), 1)
    rows = []
    for i in range(0, entries, TILE):
        block = ids[i : i + TILE]
        side.expand[i : i + TILE, :] = jnp.where(block == lanes + 1.0, 1.0, 0.0).astype(bf16)
        rows.append(block.T)
    level = earlier_equal(ids, rows)
    wanted = iota((TILE, TILE), 0) + 1.0
    over = jnp.zeros((1, TILE), f32)
    for b, i in enumerate(range(0, entries, TILE)):
        hit = rows[b] == wanted
        over = jnp.maximum(
            over, jnp.where((rows[b][0:1] > 0.0) & (level[b] >= float(LEVELS)), 1.0, 0.0)
        )
        for t in range(LEVELS):
            side.levels[t * TILE : (t + 1) * TILE, i : i + TILE] = jnp.where(
                hit & (level[b] == float(t)), 1.0, 0.0
            ).astype(bf16)
    flag_ref[...] = jnp.maximum(flag_ref[...], jnp.max(over, axis=1, keepdims=True))


def put(side, slot):
    side.send(FIRST(slot), side.p1_send, side.p1_recv.at[slot])


def put_done(side, slot):
    side.wait_send(FIRST(slot), side.p1_send, side.p1_recv.at[slot])


def combine(side, slot, final):
    recv = side.p1_recv.at[slot]
    side.wait_recv(FIRST(slot), side.p1_send, recv)
    terms = select_rows(side.levels[...], recv[...])
    terms = terms.reshape(LEVELS, TILE, TILE)
    if final:
        total = side.diag_term[...].T + jnp.sum(terms, axis=0)
    else:
        total = jnp.maximum(side.diag_term[...].T, jnp.max(terms, axis=0))
    own = side.own[...]
    own = own * lax.rsqrt((2.0 * total) * own + epsilon)
    side.own[...] = own
    side.own_turned[...] = own.T


def give_back(side, slot):
    side.p2_send[...] = select_rows(side.expand[...], side.own[...])
    side.send(BACK(slot), side.p2_send, side.p2_recv.at[slot])


def take_back(side, slot):
    recv = side.p2_recv.at[slot]
    side.wait_recv(BACK(slot), side.p2_send, recv)
    scale = select_rows(side.unpack[...], recv[...])
    side.ext[...] = scale[:TILE].T
    tail = scale[TILE : TILE + TAIL]
    if side.axis == "col":
        tail = [tail] + [pltpu.roll(tail, TILE - q * TAIL, 1) for q in range(1, QUARTERS)]
        side.tail[...] = jnp.concatenate(tail, axis=0).T[:TAIL]
    else:
        side.tail[...] = jnp.concatenate([tail] * QUARTERS, axis=0).T
    side.wait_send(BACK(slot), side.p2_send, recv)


def gather_terms(side, final):
    side.ext_term[:TILE, :] = side.ext_turned[...].T
    if side.axis == "col":
        empty = jnp.zeros((TILE - TAIL, TILE), f32)
        turned = jnp.concatenate([side.tail_term[...], empty], axis=0).T
        parts = [turned[:TAIL]]
        parts += [pltpu.roll(turned[q * TAIL : (q + 1) * TAIL], q * TAIL, 1) for q in range(1, QUARTERS)]
        side.ext_term[TILE : TILE + TAIL, :] = parts[0] + parts[1] + parts[2] + parts[3]
    else:
        parts = side.tail_term[...].T.reshape(QUARTERS, TAIL, TILE)
        side.ext_term[TILE : TILE + TAIL, :] = jnp.sum(parts, axis=0) if final else jnp.max(parts, axis=0)


def row_pass(tiles, scale, out, final):
    scale = scale[...]

    def step(g, carry):
        base = pl.multiple_of(g * GROUP, GROUP)
        results = []
        for j in range(GROUP):
            x = tiles[base + j] * scale
            reduce = jnp.sum if final else jnp.max
            results.append(reduce(x, axis=0, keepdims=True))
        out[pl.ds(base, GROUP), :] = jnp.concatenate(results, axis=0)
        return carry

    lax.fori_loop(0, tiles.shape[0] // GROUP, step, 0)


def col_pass(tiles, scale, out, final):
    def step(g, total):
        base = pl.multiple_of(g * GROUP, GROUP)
        for j in range(GROUP):
            x = tiles[base + j] * scale[pl.ds(base + j, 1), :]
            total = total + x if final else jnp.maximum(total, x)
        return total

    out[...] = lax.fori_loop(0, tiles.shape[0] // GROUP, step, jnp.zeros((TILE, TILE), f32))


def kernel(
    n_row,
    n_col,
    count_ref,
    rows_ref,
    cols_ref,
    data_ref,
    row_out,
    col_out,
    flag_out,
    diag_tiles,
    ext_tiles,
    tail_loaded,
    tail_tiles,
    key_ref,
    flag_ref,
    all_flags,
    load_sems,
    out_sems,
    near_sems,
    far_sems,
    ring_sems,
    core_sems,
    *rest,
):
    rows = Side("col", n_col, ROW_CAP, 0, rest[: len(rest) // 2])
    cols = Side("row", n_row, COL_CAP, 1, rest[len(rest) // 2 :])
    sides = (cols, rows)

    barrier = pltpu.get_barrier_semaphore()
    for side in sides:
        for d in range(1, side.count):
            pl.semaphore_signal(barrier, inc=1, device_id={side.axis: side.partner(d)}, device_id_type=MESH)

    def load(group, part):
        tiles, first, count = ((ext_tiles, DIAG, TILE), (tail_loaded, DIAG + TILE, TAIL), (diag_tiles, 0, DIAG))[group]
        height = TILE // PARTS[group]
        at = part * height
        sem = load_sems.at[group, part]

        def step(s, carry):
            for j in range(GROUP):
                slot = s * GROUP + j
                pltpu.make_async_copy(
                    data_ref.at[first + slot, pl.ds(at, height)], tiles.at[pl.ds(at, height), slot], sem
                ).start()
            return carry

        lax.fori_loop(0, count // GROUP, step, 0)

    def loaded(group, part):
        tiles = (ext_tiles, tail_loaded, diag_tiles)[group]
        height = TILE // PARTS[group]
        whole = tiles.at[pl.ds(part * height, height)]
        pltpu.make_async_copy(whole, whole, load_sems.at[group, part]).wait()

    for group in range(2):
        for part in range(PARTS[group]):
            load(group, part)

    flag_ref[...] = jnp.zeros_like(flag_ref)
    count = count_ref[0, 0]
    for side, blocks_ref in ((cols, cols_ref), (rows, rows_ref)):
        prepare(side, blocks_ref, count, key_ref, flag_ref)
        for ref in (side.id_recv, side.p1_recv, side.p2_recv):
            empty = side.entries - side.count * side.cap
            if empty:
                ref[..., side.entries - empty :, :] = jnp.zeros((*ref.shape[:-2], empty, TILE), f32)
    for side in sides:
        fill(side)
    pl.semaphore_wait(barrier, n_row + n_col - 2)
    for side in sides:
        side.send(ID(), side.p1_send, side.id_recv)

    for part in range(PARTS[2]):
        load(2, part)

    lane = lax.broadcasted_iota(jnp.int32, (1, TILE), 1)
    ext_half = jnp.where(lane + DIAG < count, 0.5, 0.0)
    tail_half = jnp.where(lane % TAIL + (DIAG + TILE) < count, 0.5, 0.0)

    def first_pass(group, tiles, half, row_term, col_term):
        total = jnp.zeros((TILE, TILE), f32)
        steps = TILE // PARTS[group] // GROUP
        for part in range(PARTS[group]):
            loaded(group, part)

            def step(g, total):
                base = pl.multiple_of(g * GROUP, GROUP)
                results = []
                for j in range(GROUP):
                    x = jnp.abs(tiles[base + j]).T * half
                    tiles[base + j] = x
                    results.append(jnp.max(x, axis=0, keepdims=True))
                    total = jnp.maximum(total, x)
                row_term[pl.ds(base, GROUP), :] = jnp.concatenate(results, axis=0)
                return total

            total = lax.fori_loop(part * steps, (part + 1) * steps, step, total)
        col_term[...] = total

    def first_tail():
        loaded(1, 0)

        def step(g, total):
            base = pl.multiple_of(g * GROUP, GROUP)
            results = []
            for j in range(GROUP):
                x = jnp.concatenate([tail_loaded[q * TAIL + base + j] for q in range(QUARTERS)], axis=0)
                x = jnp.abs(x).T * tail_half
                tail_tiles[base + j] = x
                results.append(jnp.max(x, axis=0, keepdims=True))
                total = jnp.maximum(total, x)
            rows.tail_term[pl.ds(base, GROUP), :] = jnp.concatenate(results, axis=0)
            return total

        cols.tail_term[...] = lax.fori_loop(0, TAIL // GROUP, step, jnp.zeros((TILE, TILE), f32))

    for side in sides:
        side.ext_term[...] = jnp.zeros_like(side.ext_term)
        side.own[...] = jnp.ones_like(side.own)
    first_pass(0, ext_tiles, ext_half, rows.ext_turned, cols.ext_turned)
    first_tail()
    for side in sides:
        side.wait_send(ID(), side.p1_send, side.id_recv)
        gather_terms(side, False)
        fill(side)
        put(side, 0)
    first_pass(2, diag_tiles, 0.5, rows.diag_term, cols.diag_term)
    for side in sides:
        side.wait_recv(ID(), side.p1_send, side.id_recv)
        learn(side, flag_ref)
    rows.tell(flag_ref)
    for side in sides:
        combine(side, 0, False)
        give_back(side, 0)
        put_done(side, 0)

    def row_step(slot, before, final):
        take_back(cols, before)
        row_pass(ext_tiles, cols.ext, rows.ext_turned, final)
        row_pass(tail_tiles, cols.tail, rows.tail_term, final)
        gather_terms(rows, final)
        fill(rows)
        put(rows, slot)

    def col_step(slot, before, final):
        take_back(rows, before)
        col_pass(ext_tiles, rows.ext, cols.ext_turned, final)
        col_pass(tail_tiles, rows.tail, cols.tail_term, final)
        gather_terms(cols, final)
        fill(cols)
        put(cols, slot)

    def sweep(t, final):
        slot, before = t % 2, (t + 1) % 2
        first, second = (row_step, col_step) if t % 2 else (col_step, row_step)
        first(slot, before, final)
        second(slot, before, final)
        row_pass(diag_tiles, cols.own_turned, rows.diag_term, final)
        col_pass(diag_tiles, rows.own_turned, cols.diag_term, final)
        for side in (rows, cols) if t % 2 else (cols, rows):
            combine(side, slot, final)
            if not final:
                give_back(side, slot)
        for side in sides:
            put_done(side, slot)

    for t in range(1, SWEEPS):
        sweep(t, False)
    all_flags[...] = rows.told(flag_ref)
    cols.tell(all_flags)
    sweep(SWEEPS, True)

    height = DIAG // 2
    x, z = rows.major_me, rows.minor_me
    sent = []

    def at(half, near, far):
        first, second = (z, x) if half == 0 else (x, z)
        first, second = lax.rem(first + near, WIDTH), lax.rem(second + far, WIDTH)
        return second * WIDTH + first if half == 0 else first * WIDTH + second

    def region(out, device, offset, size):
        return out.at[pl.ds(pl.multiple_of(device * DIAG + offset, 8), size)]

    def remote(src, dst, sems, index, axis, device):
        return pltpu.make_async_remote_copy(
            src_ref=src,
            dst_ref=dst,
            send_sem=sems.at[(0, *index)],
            recv_sem=sems.at[(1, *index)],
            device_id={axis: device},
            device_id_type=MESH,
        )

    def row_region(half, owner, part):
        if part is None:
            return region(row_out, owner, half * height, height)
        return region(row_out, owner, half * height + part * (height // 2), height // 2)

    def row_send(half, owner, part, sems, index, device, src=None):
        dst = row_region(half, owner, part)
        copy = remote(dst if src is None else src, dst, sems, index, "col", device)
        copy.start()
        sent.append(copy)

    def row_wait(half, owner, part, sems, index, device):
        there = row_region(half, owner, part)
        remote(there, there, sems, index, "col", device).wait_recv()

    def far_send(half, e, owner, src=None):
        for way, far in enumerate((1, 3)):
            row_send(half, owner, None, far_sems, (half, e, 0, way), at(half, 0, far), src)

    def far_pass(half, e, near):
        for way, (far, on) in enumerate(((3, 1), (1, 3))):
            owner = at(half, near, far)
            row_wait(half, owner, None, far_sems, (half, e, 0, way), at(half, 0, far))
            row_send(half, owner, way, far_sems, (half, e, 1, way), at(half, 0, on))

    def col_region(owner, part):
        if part is None:
            return region(col_out, owner, 0, DIAG)
        return region(col_out, owner, part * height, height)

    def col_send(owner, part, sems, index, device, src=None):
        dst = col_region(owner, part)
        copy = remote(dst if src is None else src, dst, sems, index, "row", device)
        copy.start()
        sent.append(copy)

    def col_wait(owner, part, sems, index, device):
        there = col_region(owner, part)
        remote(there, there, sems, index, "row", device).wait_recv()

    other = cols.shifted(0, 1)
    rows.fin[...] = rows.own[...]
    mine = [rows.fin.at[pl.ds(half * height, height)] for half in range(2)]
    for half in range(2):
        for way, near in enumerate((1, 3)):
            row_send(half, rows.me, None, near_sems, (half, 0, way), at(half, near, 0), mine[half])
    cols.fin[...] = cols.own[...]
    for way, step in enumerate((1, 3)):
        col_send(cols.me, None, ring_sems, (0, way), cols.shifted(step, 0), cols.fin)
    for half in range(2):
        far_send(half, 0, rows.me, mine[half])
    col_send(cols.me, None, core_sems, (0,), other, cols.fin)
    kept = (
        pltpu.make_async_copy(rows.fin, region(row_out, rows.me, 0, DIAG), out_sems.at[0]),
        pltpu.make_async_copy(cols.fin, region(col_out, cols.me, 0, DIAG), out_sems.at[1]),
    )
    for copy in kept:
        copy.start()
    flag_out[0, 0] = jnp.max(cols.told(all_flags)).astype(jnp.int32)
    ways = ((3, 1), (1, 3))
    for way, (near, on) in enumerate(ways):
        for half in range(2):
            owner = at(half, near, 0)
            row_wait(half, owner, None, near_sems, (half, 0, way), owner)
            row_send(half, owner, way, near_sems, (half, 1, way), at(half, on, 0))
            far_send(half, 1 + way, owner)
        owner = cols.shifted(near, 0)
        col_wait(owner, None, ring_sems, (0, way), owner)
        col_send(owner, way, ring_sems, (1, way), cols.shifted(on, 0))
        col_send(owner, None, core_sems, (1 + way,), other)
    for half in range(2):
        far_pass(half, 0, 0)
    for half in range(2):
        owner = at(half, 2, 0)
        for way, (near, on) in enumerate(ways):
            row_wait(half, owner, way, near_sems, (half, 1, way), at(half, near, 0))
        far_send(half, 3, owner)
    owner = cols.shifted(2, 0)
    for way, (near, on) in enumerate(ways):
        col_wait(owner, way, ring_sems, (1, way), cols.shifted(near, 0))
    col_send(owner, None, core_sems, (3,), other)
    nears = (0, 3, 1, 2)
    for e in range(1, WIDTH):
        for half in range(2):
            far_pass(half, e, nears[e])
    for e in range(WIDTH):
        for half in range(2):
            for way, (far, on) in enumerate(ways):
                row_wait(half, at(half, nears[e], 2), way, far_sems, (half, e, 1, way), at(half, 0, far))
        col_wait(cols.shifted(nears[e], 1), None, core_sems, (e,), other)
    for copy in sent:
        copy.wait_send()
    for copy in kept:
        copy.wait()


def side_scratch(count, cap, tail_scale, tail_term):
    entries = padded(count * cap)
    return [
        pltpu.VMEM((DIAG, TILE), f32),
        pltpu.VMEM((TILE, DIAG), f32),
        pltpu.VMEM((TILE, TILE), f32),
        pltpu.VMEM((tail_scale, TILE), f32),
        pltpu.VMEM((TILE, DIAG), f32),
        pltpu.VMEM((TILE, TILE), f32),
        pltpu.VMEM((tail_term, TILE), f32),
        pltpu.VMEM((EXT, TILE), f32),
        pltpu.VMEM((entries, EXT), bf16),
        pltpu.VMEM((EXT, entries), bf16),
        pltpu.VMEM((LEVELS * DIAG, entries), bf16),
        pltpu.VMEM((entries, DIAG), bf16),
        pltpu.VMEM((entries, TILE), f32),
        pltpu.VMEM((entries, TILE), f32),
        pltpu.VMEM((2, entries, TILE), f32),
        pltpu.VMEM((entries, TILE), f32),
        pltpu.VMEM((2, entries, TILE), f32),
        pltpu.VMEM((DIAG, TILE), f32),
        pltpu.VMEM((count, 8, TILE), f32),
        pltpu.SemaphoreType.DMA((5, count)),
        pltpu.SemaphoreType.DMA((5, 2, count)),
    ]


def sparse(tiles, row_blocks, column_blocks, used_count, n_row, n_col):
    assert tiles.shape[0] == DIAG + TILE + TAIL and n_col == WIDTH * WIDTH
    return pl.pallas_call(
        functools.partial(kernel, n_row, n_col),
        out_shape=(
            jax.ShapeDtypeStruct((n_col * DIAG, TILE), f32),
            jax.ShapeDtypeStruct((n_row * DIAG, TILE), f32),
            jax.ShapeDtypeStruct((1, 1), jnp.int32),
        ),
        in_specs=[
            pl.BlockSpec(memory_space=pltpu.SMEM),
            pl.BlockSpec(memory_space=pltpu.VMEM),
            pl.BlockSpec(memory_space=pltpu.VMEM),
            pl.BlockSpec(memory_space=pltpu.HBM),
        ],
        out_specs=(
            pl.BlockSpec(memory_space=pl.ANY),
            pl.BlockSpec(memory_space=pl.ANY),
            pl.BlockSpec(memory_space=pltpu.SMEM),
        ),
        scratch_shapes=[
            pltpu.VMEM((TILE, TILE, DIAG), f32),
            pltpu.VMEM((TILE, TILE, TILE), f32),
            pltpu.VMEM((TILE, TAIL, TILE), f32),
            pltpu.VMEM((TAIL, TILE, TILE), f32),
            pltpu.VMEM((8, EXT), f32),
            pltpu.VMEM((8, TILE), f32),
            pltpu.VMEM((8, TILE), f32),
            pltpu.SemaphoreType.DMA((3, max(PARTS))),
            pltpu.SemaphoreType.DMA((2,)),
            pltpu.SemaphoreType.DMA((2, 2, 2, 2)),
            pltpu.SemaphoreType.DMA((2, 2, WIDTH, 2, 2)),
            pltpu.SemaphoreType.DMA((2, 2, 2)),
            pltpu.SemaphoreType.DMA((2, WIDTH)),
            *side_scratch(n_col, ROW_CAP, TAIL, TAIL),
            *side_scratch(n_row, COL_CAP, TILE, TILE),
        ],
        compiler_params=pltpu.CompilerParams(
            collective_id=0, has_side_effects=True, vmem_limit_bytes=52 << 20
        ),
    )(used_count.reshape(1, 1), row_blocks.reshape(1, -1), column_blocks.reshape(1, -1), tiles)


def settle_kernel(row_ref, col_ref, row_out, col_out, sems):
    copies = []
    for ref, out in ((row_ref, row_out), (col_ref, col_out)):
        for i in range(ref.shape[0] // PIECE):
            at = pl.ds(i * PIECE, PIECE)
            copies.append(pltpu.make_async_copy(ref.at[at], out.at[at], sems.at[len(copies)]))
    for copy in copies:
        copy.start()
    for copy in copies:
        copy.wait()


def settle(row_scale, column_scale):
    pieces = (row_scale.shape[0] + column_scale.shape[0]) // PIECE
    anywhere = pl.BlockSpec(memory_space=pl.ANY)
    return pl.pallas_call(
        settle_kernel,
        out_shape=tuple(jax.ShapeDtypeStruct(x.shape, x.dtype) for x in (row_scale, column_scale)),
        in_specs=[anywhere, anywhere],
        out_specs=(anywhere, anywhere),
        scratch_shapes=[pltpu.SemaphoreType.DMA((pieces,))],
    )(row_scale, column_scale)


def gathered(x, axis):
    n = lax.axis_size(axis)
    me = lax.axis_index(axis)
    ring = [(i, (i + 1) % n) for i in range(n)]
    out = jnp.zeros((n,) + x.shape, x.dtype).at[me].set(x)

    def step(i, carry):
        out, y = carry
        y = lax.ppermute(y, axis, ring)
        return out.at[lax.rem(me + n - i, n)].set(y), y

    return lax.fori_loop(1, n, step, (out, x))[0]


def dense(blocks, row_blocks, column_blocks, used_count):
    slots, side = blocks.shape[:2]
    row_length = DIAG * lax.axis_size("col")
    column_length = DIAG * lax.axis_size("row")
    in_use = jnp.arange(slots, dtype=jnp.int32) < used_count
    magnitude = jnp.where(in_use[:, None, None], jnp.abs(blocks), f32(0.0))

    def sweep(t, carry):
        row_scale, column_scale = carry
        scaled = magnitude * row_scale[row_blocks][:, :, None] * column_scale[column_blocks][:, None, :]
        no_rows = jnp.zeros((row_length, side), f32)
        no_columns = jnp.zeros((column_length, side), f32)
        peak = t < SWEEPS

        def peaks():
            rows = no_rows.at[row_blocks].max(scaled.max(axis=2))
            columns = no_columns.at[column_blocks].max(scaled.max(axis=1))
            return rows, columns

        def totals():
            rows = no_rows.at[row_blocks].add(scaled.sum(axis=2))
            columns = no_columns.at[column_blocks].add(scaled.sum(axis=1))
            return rows, columns

        rows, columns = lax.cond(peak, peaks, totals)
        rows, columns = gathered(rows, "col"), gathered(columns, "row")
        rows = jnp.where(peak, rows.max(axis=0), rows.sum(axis=0))
        columns = jnp.where(peak, columns.max(axis=0), columns.sum(axis=0))
        return row_scale * lax.rsqrt(rows + epsilon), column_scale * lax.rsqrt(columns + epsilon)

    start = (jnp.ones((row_length, side), f32), jnp.ones((column_length, side), f32))
    return lax.fori_loop(0, SWEEPS + 1, sweep, start)


def on_device(tile_data, tile_rows, tile_cols, tile_counts):
    blocks = tile_data[0, 0]
    row_blocks = tile_rows[0, 0]
    column_blocks = tile_cols[0, 0]
    used_count = tile_counts[0, 0]
    n_row, n_col = lax.axis_size("row"), lax.axis_size("col")
    row_scale, column_scale, flag = sparse(blocks, row_blocks, column_blocks, used_count, n_row, n_col)
    row_scale, column_scale = lax.cond(
        flag[0, 0] > 0,
        lambda: dense(blocks, row_blocks, column_blocks, used_count),
        lambda: settle(row_scale, column_scale),
    )
    return (row_scale.reshape(-1), column_scale.reshape(-1))


def solution(mesh):
    placed = (
        P("row", "col", None, None, None),
        P("row", "col", None),
        P("row", "col", None),
        P("row", "col"),
    )
    return jax.shard_map(
        on_device, mesh=mesh, in_specs=placed, out_specs=(P("row"), P("col")), check_vma=False
    )
```

```python
import functools

import jax
import jax.numpy as jnp
from jax import lax
from jax.experimental import pallas as pl
from jax.experimental.pallas import tpu as pltpu
from jax.sharding import PartitionSpec as P

TILE = 128
DIAG = 128
SWEEPS = 4
epsilon = 1e-06

EXT = 256
ROW_CAP = 24
COL_CAP = 40
LEVELS = 8
GROUP = 8
PARTS = (2, 1, 1)
PIECE = 256
HOPS = (0, 1, 2, 1)
WIDTH = 4
TAIL = 32
QUARTERS = TILE // TAIL

f32 = jnp.float32
bf16 = jnp.bfloat16
MESH = pltpu.DeviceIdType.MESH if hasattr(pltpu, "DeviceIdType") else pl.DeviceIdType.MESH


def halves(x):
    hi = x.astype(bf16)
    lo = (x - hi.astype(f32)).astype(bf16)
    return jnp.concatenate([hi, lo], axis=1)


def select_rows(onehot, x):
    y = jnp.dot(onehot, halves(x), preferred_element_type=f32)
    return y[:, :TILE] + y[:, TILE:]


def iota(shape, dim):
    return lax.broadcasted_iota(jnp.int32, shape, dim).astype(f32)


def columns(row):
    parts = [
        jnp.broadcast_to(row[:, i : i + TILE], (TILE, TILE)).T for i in range(0, row.shape[1], TILE)
    ]
    return jnp.concatenate(parts, axis=0)


def earlier_equal(cols, rows):
    count = cols.shape[0] // TILE
    out = []
    before = iota((TILE, TILE), 0) < iota((TILE, TILE), 1)
    for b in range(count):
        total = jnp.zeros((1, TILE), f32)
        here = rows[b]
        for a in range(b + 1):
            same = cols[a * TILE : (a + 1) * TILE] == here
            if a == b:
                same = same & before
            total = total + jnp.sum(jnp.where(same, 1.0, 0.0), axis=0, keepdims=True)
        out.append(total)
    return out


def padded(entries):
    return -(-entries // TILE) * TILE


class Side:
    def __init__(self, axis, count, cap, key_row, refs):
        self.axis, self.count, self.cap, self.key_row = axis, count, cap, key_row
        self.entries = padded(count * cap)
        (
            self.own,
            self.own_turned,
            self.ext,
            self.tail,
            self.diag_term,
            self.ext_turned,
            self.tail_term,
            self.ext_term,
            self.pack,
            self.unpack,
            self.levels,
            self.expand,
            self.id_recv,
            self.p1_send,
            self.p1_recv,
            self.p2_send,
            self.p2_recv,
            self.fin,
            self.flags,
            self.send_sems,
            self.recv_sems,
        ) = refs
        self.me = lax.axis_index(axis)
        self.minor = minor = count // WIDTH
        steps = [(a, b) for a in range(WIDTH) for b in range(minor) if a or b]
        self.steps = sorted(steps, key=lambda s: -sum(HOPS[i] for i in s))
        self.major_me, self.minor_me = lax.div(self.me, minor), lax.rem(self.me, minor)

    def shifted(self, a, b):
        return lax.rem(self.major_me + a, WIDTH) * self.minor + lax.rem(self.minor_me + b, self.minor)

    def partner(self, d):
        a, b = self.steps[d - 1]
        return self.shifted(a, b)

    def copy(self, kind, src, dst, peer):
        kind, slot = kind
        return pltpu.make_async_remote_copy(
            src_ref=src,
            dst_ref=dst,
            send_sem=self.send_sems.at[kind],
            recv_sem=self.recv_sems.at[kind, slot],
            device_id={self.axis: peer},
            device_id_type=MESH,
        )

    def place(self, ref, peer):
        return ref.at[pl.ds(pl.multiple_of(peer * self.cap, 8), self.cap)]

    def send(self, kind, send, recv):
        for d in range(1, self.count):
            peer = self.partner(d)
            self.copy(kind, self.place(send, peer), self.place(recv, self.me), peer).start()
        self.place(recv, self.me)[...] = self.place(send, self.me)[...]

    def wait(self, sem, ref, size):
        whole = ref.at[pl.ds(0, size)]
        pltpu.make_async_copy(whole, whole, sem).wait()

    def wait_send(self, kind, send):
        self.wait(self.send_sems.at[kind[0]], send, (self.count - 1) * self.cap)

    def wait_recv(self, kind, recv):
        self.wait(self.recv_sems.at[kind[0], kind[1]], recv, (self.count - 1) * self.cap)

    def tell(self, flag_ref):
        for d in range(1, self.count):
            self.copy((4, 0), flag_ref, self.flags.at[self.me], self.partner(d)).start()
        self.flags[self.me] = flag_ref[...]

    def told(self):
        self.wait(self.recv_sems.at[4, 0], self.flags, self.count - 1)
        self.wait(self.send_sems.at[4], self.flags, self.count - 1)
        return jnp.max(self.flags[...], axis=0)


def ID():
    return (0, 0)


def FIRST(slot):
    return (1, slot)


def BACK(slot):
    return (2, slot)


def LAST():
    return (3, 0)


def prepare(side, blocks_ref, used_count, key_ref, flag_ref):
    cap, entries = side.cap, side.entries
    blocks = blocks_ref[...].astype(f32)
    key_ref[...] = jnp.full_like(key_ref, -1.0)
    key_ref[0:1, :TILE] = blocks[:, DIAG : DIAG + TILE]
    key_ref[0:1, TILE : TILE + TAIL] = blocks[:, DIAG + TILE :]
    slot = lax.broadcasted_iota(jnp.int32, (1, EXT), 1) + DIAG
    key = jnp.where(slot < used_count, key_ref[0:1, :], -1.0)
    owner = jnp.floor(key * (1.0 / DIAG))
    local = key - owner * DIAG
    used = key >= 0.0
    owner_cols = columns(owner)
    rank = earlier_equal(owner_cols, [owner[:, :TILE], owner[:, TILE:]])
    rank = jnp.concatenate(rank, axis=1)
    fits = used & (rank < float(cap))
    dest = jnp.where(fits, owner * cap + rank, -1.0)
    over = jnp.where(used & (rank >= float(cap)), 1.0, 0.0)
    flag_ref[...] = jnp.maximum(flag_ref[...], jnp.max(over, axis=1, keepdims=True))
    side.pack[...] = jnp.where(iota((entries, EXT), 0) == dest, 1.0, 0.0).astype(bf16)
    dest_cols = columns(dest)
    for i in range(0, entries, TILE):
        lanes = iota((EXT, TILE), 1) + float(i)
        side.unpack[:, i : i + TILE] = jnp.where(dest_cols == lanes, 1.0, 0.0).astype(bf16)
    side.ext_term[...] = jnp.where(columns(jnp.where(used, 1.0, 0.0)) > 0.0, columns(local) + 1.0, 0.0)


def fill(side):
    side.p1_send[...] = select_rows(side.pack[...], side.ext_term[...])


def learn(side, flag_ref):
    entries = side.entries
    ids = side.id_recv[...]
    lanes = iota((TILE, TILE), 1)
    rows = []
    for i in range(0, entries, TILE):
        block = ids[i : i + TILE]
        side.expand[i : i + TILE, :] = jnp.where(block == lanes + 1.0, 1.0, 0.0).astype(bf16)
        rows.append(block.T)
    level = earlier_equal(ids, rows)
    wanted = iota((TILE, TILE), 0) + 1.0
    over = jnp.zeros((1, TILE), f32)
    for b, i in enumerate(range(0, entries, TILE)):
        hit = rows[b] == wanted
        over = jnp.maximum(
            over, jnp.where((rows[b][0:1] > 0.0) & (level[b] >= float(LEVELS)), 1.0, 0.0)
        )
        for t in range(LEVELS):
            side.levels[t * TILE : (t + 1) * TILE, i : i + TILE] = jnp.where(
                hit & (level[b] == float(t)), 1.0, 0.0
            ).astype(bf16)
    flag_ref[...] = jnp.maximum(flag_ref[...], jnp.max(over, axis=1, keepdims=True))


def put(side, slot):
    side.send(FIRST(slot), side.p1_send, side.p1_recv.at[slot])


def put_done(side, slot):
    side.wait_send(FIRST(slot), side.p1_send)


def combine(side, slot, final):
    recv = side.p1_recv.at[slot]
    side.wait_recv(FIRST(slot), recv)
    terms = select_rows(side.levels[...], recv[...])
    terms = terms.reshape(LEVELS, TILE, TILE)
    if final:
        total = side.diag_term[...].T + jnp.sum(terms, axis=0)
    else:
        total = jnp.maximum(side.diag_term[...].T, jnp.max(terms, axis=0))
    own = side.own[...]
    own = own * lax.rsqrt((2.0 * total) * own + epsilon)
    side.own[...] = own
    side.own_turned[...] = own.T


def give_back(side, slot):
    side.p2_send[...] = select_rows(side.expand[...], side.own[...])
    side.send(BACK(slot), side.p2_send, side.p2_recv.at[slot])


def take_back(side, slot):
    recv = side.p2_recv.at[slot]
    side.wait_recv(BACK(slot), recv)
    scale = select_rows(side.unpack[...], recv[...])
    side.ext[...] = scale[:TILE].T
    tail = scale[TILE : TILE + TAIL]
    if side.axis == "col":
        tail = [tail] + [pltpu.roll(tail, TILE - q * TAIL, 1) for q in range(1, QUARTERS)]
        side.tail[...] = jnp.concatenate(tail, axis=0).T[:TAIL]
    else:
        side.tail[...] = jnp.concatenate([tail] * QUARTERS, axis=0).T
    side.wait_send(BACK(slot), side.p2_send)


def gather_terms(side, final):
    side.ext_term[:TILE, :] = side.ext_turned[...].T
    if side.axis == "col":
        empty = jnp.zeros((TILE - TAIL, TILE), f32)
        turned = jnp.concatenate([side.tail_term[...], empty], axis=0).T
        parts = [turned[:TAIL]]
        parts += [pltpu.roll(turned[q * TAIL : (q + 1) * TAIL], q * TAIL, 1) for q in range(1, QUARTERS)]
        side.ext_term[TILE : TILE + TAIL, :] = parts[0] + parts[1] + parts[2] + parts[3]
    else:
        parts = side.tail_term[...].T.reshape(QUARTERS, TAIL, TILE)
        side.ext_term[TILE : TILE + TAIL, :] = jnp.sum(parts, axis=0) if final else jnp.max(parts, axis=0)


def row_pass(tiles, scale, out, final):
    scale = scale[...]

    def step(g, carry):
        base = pl.multiple_of(g * GROUP, GROUP)
        results = []
        for j in range(GROUP):
            x = tiles[base + j] * scale
            reduce = jnp.sum if final else jnp.max
            results.append(reduce(x, axis=0, keepdims=True))
        out[pl.ds(base, GROUP), :] = jnp.concatenate(results, axis=0)
        return carry

    lax.fori_loop(0, tiles.shape[0] // GROUP, step, 0)


def col_pass(tiles, scale, out, final):
    def step(g, total):
        base = pl.multiple_of(g * GROUP, GROUP)
        for j in range(GROUP):
            x = tiles[base + j] * scale[pl.ds(base + j, 1), :]
            total = total + x if final else jnp.maximum(total, x)
        return total

    out[...] = lax.fori_loop(0, tiles.shape[0] // GROUP, step, jnp.zeros((TILE, TILE), f32))


def kernel(
    n_row,
    n_col,
    count_ref,
    rows_ref,
    cols_ref,
    data_ref,
    row_out,
    col_out,
    flag_out,
    diag_tiles,
    ext_tiles,
    tail_loaded,
    tail_tiles,
    key_ref,
    flag_ref,
    all_flags,
    load_sems,
    out_sems,
    near_sems,
    far_sems,
    *rest,
):
    rows = Side("col", n_col, ROW_CAP, 0, rest[: len(rest) // 2])
    cols = Side("row", n_row, COL_CAP, 1, rest[len(rest) // 2 :])
    sides = (cols, rows)

    barrier = pltpu.get_barrier_semaphore()
    for side in sides:
        for d in range(1, side.count):
            pl.semaphore_signal(barrier, inc=1, device_id={side.axis: side.partner(d)}, device_id_type=MESH)

    def load(group, part):
        tiles, first, count = ((ext_tiles, DIAG, TILE), (tail_loaded, DIAG + TILE, TAIL), (diag_tiles, 0, DIAG))[group]
        height = TILE // PARTS[group]
        at = part * height
        sem = load_sems.at[group, part]

        def step(s, carry):
            for j in range(GROUP):
                slot = s * GROUP + j
                pltpu.make_async_copy(
                    data_ref.at[first + slot, pl.ds(at, height)], tiles.at[pl.ds(at, height), slot], sem
                ).start()
            return carry

        lax.fori_loop(0, count // GROUP, step, 0)

    def loaded(group, part):
        tiles = (ext_tiles, tail_loaded, diag_tiles)[group]
        height = TILE // PARTS[group]
        whole = tiles.at[pl.ds(part * height, height)]
        pltpu.make_async_copy(whole, whole, load_sems.at[group, part]).wait()

    for group in range(2):
        for part in range(PARTS[group]):
            load(group, part)

    flag_ref[...] = jnp.zeros_like(flag_ref)
    count = count_ref[0, 0]
    for side, blocks_ref in ((cols, cols_ref), (rows, rows_ref)):
        prepare(side, blocks_ref, count, key_ref, flag_ref)
        for ref in (side.id_recv, side.p1_recv, side.p2_recv):
            empty = side.entries - side.count * side.cap
            if empty:
                ref[..., side.entries - empty :, :] = jnp.zeros((*ref.shape[:-2], empty, TILE), f32)
    for side in sides:
        fill(side)
    pl.semaphore_wait(barrier, n_row + n_col - 2)
    for side in sides:
        side.send(ID(), side.p1_send, side.id_recv)

    for part in range(PARTS[2]):
        load(2, part)

    lane = lax.broadcasted_iota(jnp.int32, (1, TILE), 1)
    ext_half = jnp.where(lane + DIAG < count, 0.5, 0.0)
    tail_half = jnp.where(lane % TAIL + (DIAG + TILE) < count, 0.5, 0.0)

    def first_pass(group, tiles, half, row_term, col_term):
        total = jnp.zeros((TILE, TILE), f32)
        steps = TILE // PARTS[group] // GROUP
        for part in range(PARTS[group]):
            loaded(group, part)

            def step(g, total):
                base = pl.multiple_of(g * GROUP, GROUP)
                results = []
                for j in range(GROUP):
                    x = jnp.abs(tiles[base + j]).T * half
                    tiles[base + j] = x
                    results.append(jnp.max(x, axis=0, keepdims=True))
                    total = jnp.maximum(total, x)
                row_term[pl.ds(base, GROUP), :] = jnp.concatenate(results, axis=0)
                return total

            total = lax.fori_loop(part * steps, (part + 1) * steps, step, total)
        col_term[...] = total

    def first_tail():
        loaded(1, 0)

        def step(g, total):
            base = pl.multiple_of(g * GROUP, GROUP)
            results = []
            for j in range(GROUP):
                x = jnp.concatenate([tail_loaded[q * TAIL + base + j] for q in range(QUARTERS)], axis=0)
                x = jnp.abs(x).T * tail_half
                tail_tiles[base + j] = x
                results.append(jnp.max(x, axis=0, keepdims=True))
                total = jnp.maximum(total, x)
            rows.tail_term[pl.ds(base, GROUP), :] = jnp.concatenate(results, axis=0)
            return total

        cols.tail_term[...] = lax.fori_loop(0, TAIL // GROUP, step, jnp.zeros((TILE, TILE), f32))

    for side in sides:
        side.ext_term[...] = jnp.zeros_like(side.ext_term)
        side.own[...] = jnp.ones_like(side.own)
    first_pass(0, ext_tiles, ext_half, rows.ext_turned, cols.ext_turned)
    first_tail()
    for side in (rows, cols):
        side.wait_send(ID(), side.p1_send)
        gather_terms(side, False)
        fill(side)
        put(side, 0)
    first_pass(2, diag_tiles, 0.5, rows.diag_term, cols.diag_term)
    for side in sides:
        side.wait_recv(ID(), side.id_recv)
        learn(side, flag_ref)
    rows.tell(flag_ref)
    for side in sides:
        combine(side, 0, False)
        give_back(side, 0)
        put_done(side, 0)

    def row_step(slot, before, final):
        take_back(cols, before)
        row_pass(ext_tiles, cols.ext, rows.ext_turned, final)
        row_pass(tail_tiles, cols.tail, rows.tail_term, final)
        gather_terms(rows, final)
        fill(rows)
        put(rows, slot)

    def col_step(slot, before, final):
        take_back(rows, before)
        col_pass(ext_tiles, rows.ext, cols.ext_turned, final)
        col_pass(tail_tiles, rows.tail, cols.tail_term, final)
        gather_terms(cols, final)
        fill(cols)
        put(cols, slot)

    def sweep(t, final):
        slot, before = t % 2, (t + 1) % 2
        first, second = (row_step, col_step) if t % 2 else (col_step, row_step)
        first(slot, before, final)
        second(slot, before, final)
        row_pass(diag_tiles, cols.own_turned, rows.diag_term, final)
        col_pass(diag_tiles, rows.own_turned, cols.diag_term, final)
        for side in (rows, cols) if t % 2 else (cols, rows):
            combine(side, slot, final)
            if not final:
                give_back(side, slot)
        for side in sides:
            put_done(side, slot)

    for t in range(1, SWEEPS):
        sweep(t, False)
    all_flags[...] = rows.told()
    cols.tell(all_flags)
    sweep(SWEEPS, True)

    height = DIAG // 2
    x, z = lax.div(rows.me, WIDTH), lax.rem(rows.me, WIDTH)

    def at(half, near, far):
        first, second = (z, x) if half == 0 else (x, z)
        first, second = lax.rem(first + near, WIDTH), lax.rem(second + far, WIDTH)
        return second * WIDTH + first if half == 0 else first * WIDTH + second

    def block(half, device):
        return row_out.at[pl.ds(pl.multiple_of(device * DIAG + half * height, 8), height)]

    def row_copy(half, source, sems, device):
        there = block(half, source[1])
        return pltpu.make_async_remote_copy(
            src_ref=source[0],
            dst_ref=there,
            send_sem=sems[0],
            recv_sem=sems[1],
            device_id={"col": device},
            device_id_type=MESH,
        )

    def near_copy(half, d, device, owner):
        sems = near_sems.at[0, half, d], near_sems.at[1, half, d]
        return row_copy(half, (rows.fin.at[pl.ds(half * height, height)], owner), sems, device)

    def far_copy(half, e, d, device, owner):
        sems = far_sems.at[0, half, e, d], far_sems.at[1, half, e, d]
        source = rows.fin.at[pl.ds(half * height, height)] if e == 0 else block(half, owner)
        return row_copy(half, (source, owner), sems, device)

    rows.fin[...] = rows.own[...]
    for d in range(1, WIDTH):
        for half in range(2):
            near_copy(half, d, at(half, d, 0), rows.me).start()
    cols.fin[...] = cols.own[...]
    col_place = col_out.at[pl.ds(pl.multiple_of(cols.me * DIAG, DIAG), DIAG)]
    for d in range(1, cols.count):
        cols.copy(LAST(), cols.fin, col_place, cols.partner(d)).start()
    for d in range(1, WIDTH):
        for half in range(2):
            far_copy(half, 0, d, at(half, 0, d), rows.me).start()
    row_place = row_out.at[pl.ds(pl.multiple_of(rows.me * DIAG, DIAG), DIAG)]
    kept = (
        pltpu.make_async_copy(rows.fin, row_place, out_sems.at[0]),
        pltpu.make_async_copy(cols.fin, col_place, out_sems.at[1]),
    )
    for copy in kept:
        copy.start()
    flag_out[0, 0] = jnp.max(cols.told()).astype(jnp.int32)
    for e in range(1, WIDTH):
        for half in range(2):
            owner = at(half, WIDTH - e, 0)
            near_copy(half, e, owner, owner).wait_recv()
            for d in range(1, WIDTH):
                far_copy(half, e, d, at(half, 0, d), owner).start()
    for d in range(1, WIDTH):
        for half in range(2):
            for e in range(WIDTH):
                sender = at(half, 0, WIDTH - d)
                far_copy(half, e, d, sender, at(half, WIDTH - e, WIDTH - d)).wait_recv()
    cols.wait(cols.recv_sems.at[3, 0], col_out, (cols.count - 1) * DIAG)
    cols.wait(cols.send_sems.at[3], col_out, (cols.count - 1) * DIAG)
    for d in range(1, WIDTH):
        for half in range(2):
            near_copy(half, d, at(half, d, 0), rows.me).wait_send()
            for e in range(WIDTH):
                owner = at(half, WIDTH - e, 0) if e else rows.me
                far_copy(half, e, d, at(half, 0, d), owner).wait_send()
    for copy in kept:
        copy.wait()


def side_scratch(count, cap, tail_scale, tail_term):
    entries = padded(count * cap)
    return [
        pltpu.VMEM((DIAG, TILE), f32),
        pltpu.VMEM((TILE, DIAG), f32),
        pltpu.VMEM((TILE, TILE), f32),
        pltpu.VMEM((tail_scale, TILE), f32),
        pltpu.VMEM((TILE, DIAG), f32),
        pltpu.VMEM((TILE, TILE), f32),
        pltpu.VMEM((tail_term, TILE), f32),
        pltpu.VMEM((EXT, TILE), f32),
        pltpu.VMEM((entries, EXT), bf16),
        pltpu.VMEM((EXT, entries), bf16),
        pltpu.VMEM((LEVELS * DIAG, entries), bf16),
        pltpu.VMEM((entries, DIAG), bf16),
        pltpu.VMEM((entries, TILE), f32),
        pltpu.VMEM((entries, TILE), f32),
        pltpu.VMEM((2, entries, TILE), f32),
        pltpu.VMEM((entries, TILE), f32),
        pltpu.VMEM((2, entries, TILE), f32),
        pltpu.VMEM((DIAG, TILE), f32),
        pltpu.VMEM((count, 8, TILE), f32),
        pltpu.SemaphoreType.DMA((5,)),
        pltpu.SemaphoreType.DMA((5, 2)),
    ]


def sparse(tiles, row_blocks, column_blocks, used_count, n_row, n_col):
    assert tiles.shape[0] == DIAG + TILE + TAIL and n_col == WIDTH * WIDTH
    return pl.pallas_call(
        functools.partial(kernel, n_row, n_col),
        out_shape=(
            jax.ShapeDtypeStruct((n_col * DIAG, TILE), f32),
            jax.ShapeDtypeStruct((n_row * DIAG, TILE), f32),
            jax.ShapeDtypeStruct((1, 1), jnp.int32),
        ),
        in_specs=[
            pl.BlockSpec(memory_space=pltpu.SMEM),
            pl.BlockSpec(memory_space=pltpu.VMEM),
            pl.BlockSpec(memory_space=pltpu.VMEM),
            pl.BlockSpec(memory_space=pltpu.HBM),
        ],
        out_specs=(
            pl.BlockSpec(memory_space=pl.ANY),
            pl.BlockSpec(memory_space=pl.ANY),
            pl.BlockSpec(memory_space=pltpu.SMEM),
        ),
        scratch_shapes=[
            pltpu.VMEM((TILE, TILE, DIAG), f32),
            pltpu.VMEM((TILE, TILE, TILE), f32),
            pltpu.VMEM((TILE, TAIL, TILE), f32),
            pltpu.VMEM((TAIL, TILE, TILE), f32),
            pltpu.VMEM((8, EXT), f32),
            pltpu.VMEM((8, TILE), f32),
            pltpu.VMEM((8, TILE), f32),
            pltpu.SemaphoreType.DMA((3, max(PARTS))),
            pltpu.SemaphoreType.DMA((2,)),
            pltpu.SemaphoreType.DMA((2, 2, WIDTH)),
            pltpu.SemaphoreType.DMA((2, 2, WIDTH, WIDTH)),
            *side_scratch(n_col, ROW_CAP, TAIL, TAIL),
            *side_scratch(n_row, COL_CAP, TILE, TILE),
        ],
        compiler_params=pltpu.CompilerParams(
            collective_id=0, has_side_effects=True, vmem_limit_bytes=52 << 20
        ),
    )(used_count.reshape(1, 1), row_blocks.reshape(1, -1), column_blocks.reshape(1, -1), tiles)


def settle_kernel(row_ref, col_ref, row_out, col_out, sems):
    copies = []
    for ref, out in ((row_ref, row_out), (col_ref, col_out)):
        for i in range(ref.shape[0] // PIECE):
            at = pl.ds(i * PIECE, PIECE)
            copies.append(pltpu.make_async_copy(ref.at[at], out.at[at], sems.at[len(copies)]))
    for copy in copies:
        copy.start()
    for copy in copies:
        copy.wait()


def settle(row_scale, column_scale):
    pieces = (row_scale.shape[0] + column_scale.shape[0]) // PIECE
    anywhere = pl.BlockSpec(memory_space=pl.ANY)
    return pl.pallas_call(
        settle_kernel,
        out_shape=tuple(jax.ShapeDtypeStruct(x.shape, x.dtype) for x in (row_scale, column_scale)),
        in_specs=[anywhere, anywhere],
        out_specs=(anywhere, anywhere),
        scratch_shapes=[pltpu.SemaphoreType.DMA((pieces,))],
    )(row_scale, column_scale)


def gathered(x, axis):
    n = lax.axis_size(axis)
    me = lax.axis_index(axis)
    ring = [(i, (i + 1) % n) for i in range(n)]
    out = jnp.zeros((n,) + x.shape, x.dtype).at[me].set(x)

    def step(i, carry):
        out, y = carry
        y = lax.ppermute(y, axis, ring)
        return out.at[lax.rem(me + n - i, n)].set(y), y

    return lax.fori_loop(1, n, step, (out, x))[0]


def dense(blocks, row_blocks, column_blocks, used_count):
    slots, side = blocks.shape[:2]
    row_length = DIAG * lax.axis_size("col")
    column_length = DIAG * lax.axis_size("row")
    in_use = jnp.arange(slots, dtype=jnp.int32) < used_count
    magnitude = jnp.where(in_use[:, None, None], jnp.abs(blocks), f32(0.0))

    def sweep(t, carry):
        row_scale, column_scale = carry
        scaled = magnitude * row_scale[row_blocks][:, :, None] * column_scale[column_blocks][:, None, :]
        no_rows = jnp.zeros((row_length, side), f32)
        no_columns = jnp.zeros((column_length, side), f32)
        peak = t < SWEEPS

        def peaks():
            rows = no_rows.at[row_blocks].max(scaled.max(axis=2))
            columns = no_columns.at[column_blocks].max(scaled.max(axis=1))
            return rows, columns

        def totals():
            rows = no_rows.at[row_blocks].add(scaled.sum(axis=2))
            columns = no_columns.at[column_blocks].add(scaled.sum(axis=1))
            return rows, columns

        rows, columns = lax.cond(peak, peaks, totals)
        rows, columns = gathered(rows, "col"), gathered(columns, "row")
        rows = jnp.where(peak, rows.max(axis=0), rows.sum(axis=0))
        columns = jnp.where(peak, columns.max(axis=0), columns.sum(axis=0))
        return row_scale * lax.rsqrt(rows + epsilon), column_scale * lax.rsqrt(columns + epsilon)

    start = (jnp.ones((row_length, side), f32), jnp.ones((column_length, side), f32))
    return lax.fori_loop(0, SWEEPS + 1, sweep, start)


def on_device(tile_data, tile_rows, tile_cols, tile_counts):
    blocks = tile_data[0, 0]
    row_blocks = tile_rows[0, 0]
    column_blocks = tile_cols[0, 0]
    used_count = tile_counts[0, 0]
    n_row, n_col = lax.axis_size("row"), lax.axis_size("col")
    row_scale, column_scale, flag = sparse(blocks, row_blocks, column_blocks, used_count, n_row, n_col)
    row_scale, column_scale = lax.cond(
        flag[0, 0] > 0,
        lambda: dense(blocks, row_blocks, column_blocks, used_count),
        lambda: settle(row_scale, column_scale),
    )
    return (row_scale.reshape(-1), column_scale.reshape(-1))


def solution(mesh):
    placed = (
        P("row", "col", None, None, None),
        P("row", "col", None),
        P("row", "col", None),
        P("row", "col"),
    )
    return jax.shard_map(
        on_device, mesh=mesh, in_specs=placed, out_specs=(P("row"), P("col")), check_vma=False
    )
```

```python
import functools

import jax
import jax.numpy as jnp
from jax import lax
from jax.experimental import pallas as pl
from jax.experimental.pallas import tpu as pltpu
from jax.sharding import PartitionSpec as P

TILE = 128
DIAG = 128
SWEEPS = 4
epsilon = 1e-06

EXT = 256
ROW_CAP = 24
COL_CAP = 40
LEVELS = 8
GROUP = 8
PARTS = (2, 1, 1)
PIECE = 256
HOPS = (0, 1, 2, 1)
WIDTH = 4
TAIL = 32
QUARTERS = TILE // TAIL

f32 = jnp.float32
bf16 = jnp.bfloat16
MESH = pltpu.DeviceIdType.MESH if hasattr(pltpu, "DeviceIdType") else pl.DeviceIdType.MESH


def halves(x):
    hi = x.astype(bf16)
    lo = (x - hi.astype(f32)).astype(bf16)
    return jnp.concatenate([hi, lo], axis=1)


def select_rows(onehot, x):
    y = jnp.dot(onehot, halves(x), preferred_element_type=f32)
    return y[:, :TILE] + y[:, TILE:]


def iota(shape, dim):
    return lax.broadcasted_iota(jnp.int32, shape, dim).astype(f32)


def columns(row):
    parts = [
        jnp.broadcast_to(row[:, i : i + TILE], (TILE, TILE)).T for i in range(0, row.shape[1], TILE)
    ]
    return jnp.concatenate(parts, axis=0)


def earlier_equal(cols, rows):
    count = cols.shape[0] // TILE
    out = []
    before = iota((TILE, TILE), 0) < iota((TILE, TILE), 1)
    for b in range(count):
        total = jnp.zeros((1, TILE), f32)
        here = rows[b]
        for a in range(b + 1):
            same = cols[a * TILE : (a + 1) * TILE] == here
            if a == b:
                same = same & before
            total = total + jnp.sum(jnp.where(same, 1.0, 0.0), axis=0, keepdims=True)
        out.append(total)
    return out


def padded(entries):
    return -(-entries // TILE) * TILE


class Side:
    def __init__(self, axis, count, cap, key_row, refs):
        self.axis, self.count, self.cap, self.key_row = axis, count, cap, key_row
        self.entries = padded(count * cap)
        (
            self.own,
            self.own_turned,
            self.ext,
            self.tail,
            self.diag_term,
            self.ext_turned,
            self.tail_term,
            self.ext_term,
            self.pack,
            self.unpack,
            self.levels,
            self.expand,
            self.id_recv,
            self.p1_send,
            self.p1_recv,
            self.p2_send,
            self.p2_recv,
            self.fin,
            self.flags,
            self.send_sems,
            self.recv_sems,
        ) = refs
        self.me = lax.axis_index(axis)
        self.minor = minor = count // WIDTH
        steps = [(a, b) for a in range(WIDTH) for b in range(minor) if a or b]
        self.steps = sorted(steps, key=lambda s: -sum(HOPS[i] for i in s))
        self.major_me, self.minor_me = lax.div(self.me, minor), lax.rem(self.me, minor)

    def shifted(self, a, b):
        return lax.rem(self.major_me + a, WIDTH) * self.minor + lax.rem(self.minor_me + b, self.minor)

    def partner(self, d):
        a, b = self.steps[d - 1]
        return self.shifted(a, b)

    def copy(self, kind, src, dst, peer):
        kind, slot = kind
        return pltpu.make_async_remote_copy(
            src_ref=src,
            dst_ref=dst,
            send_sem=self.send_sems.at[kind],
            recv_sem=self.recv_sems.at[kind, slot],
            device_id={self.axis: peer},
            device_id_type=MESH,
        )

    def place(self, ref, peer):
        return ref.at[pl.ds(pl.multiple_of(peer * self.cap, 8), self.cap)]

    def send(self, kind, send, recv):
        for d in range(1, self.count):
            peer = self.partner(d)
            self.copy(kind, self.place(send, peer), self.place(recv, self.me), peer).start()
        self.place(recv, self.me)[...] = self.place(send, self.me)[...]

    def wait(self, sem, ref, size):
        whole = ref.at[pl.ds(0, size)]
        pltpu.make_async_copy(whole, whole, sem).wait()

    def wait_send(self, kind, send):
        self.wait(self.send_sems.at[kind[0]], send, (self.count - 1) * self.cap)

    def wait_recv(self, kind, recv):
        self.wait(self.recv_sems.at[kind[0], kind[1]], recv, (self.count - 1) * self.cap)

    def tell(self, flag_ref):
        for d in range(1, self.count):
            self.copy((4, 0), flag_ref, self.flags.at[self.me], self.partner(d)).start()
        self.flags[self.me] = flag_ref[...]

    def told(self):
        self.wait(self.recv_sems.at[4, 0], self.flags, self.count - 1)
        self.wait(self.send_sems.at[4], self.flags, self.count - 1)
        return jnp.max(self.flags[...], axis=0)


def ID():
    return (0, 0)


def FIRST(slot):
    return (1, slot)


def BACK(slot):
    return (2, slot)


def LAST():
    return (3, 0)


def prepare(side, blocks_ref, used_count, key_ref, flag_ref):
    cap, entries = side.cap, side.entries
    blocks = blocks_ref[...].astype(f32)
    key_ref[...] = jnp.full_like(key_ref, -1.0)
    key_ref[0:1, :TILE] = blocks[:, DIAG : DIAG + TILE]
    key_ref[0:1, TILE : TILE + TAIL] = blocks[:, DIAG + TILE :]
    slot = lax.broadcasted_iota(jnp.int32, (1, EXT), 1) + DIAG
    key = jnp.where(slot < used_count, key_ref[0:1, :], -1.0)
    owner = jnp.floor(key * (1.0 / DIAG))
    local = key - owner * DIAG
    used = key >= 0.0
    owner_cols = columns(owner)
    rank = earlier_equal(owner_cols, [owner[:, :TILE], owner[:, TILE:]])
    rank = jnp.concatenate(rank, axis=1)
    fits = used & (rank < float(cap))
    dest = jnp.where(fits, owner * cap + rank, -1.0)
    over = jnp.where(used & (rank >= float(cap)), 1.0, 0.0)
    flag_ref[...] = jnp.maximum(flag_ref[...], jnp.max(over, axis=1, keepdims=True))
    side.pack[...] = jnp.where(iota((entries, EXT), 0) == dest, 1.0, 0.0).astype(bf16)
    dest_cols = columns(dest)
    for i in range(0, entries, TILE):
        lanes = iota((EXT, TILE), 1) + float(i)
        side.unpack[:, i : i + TILE] = jnp.where(dest_cols == lanes, 1.0, 0.0).astype(bf16)
    side.ext_term[...] = jnp.where(columns(jnp.where(used, 1.0, 0.0)) > 0.0, columns(local) + 1.0, 0.0)


def fill(side):
    side.p1_send[...] = select_rows(side.pack[...], side.ext_term[...])


def learn(side, flag_ref):
    entries = side.entries
    ids = side.id_recv[...]
    lanes = iota((TILE, TILE), 1)
    rows = []
    for i in range(0, entries, TILE):
        block = ids[i : i + TILE]
        side.expand[i : i + TILE, :] = jnp.where(block == lanes + 1.0, 1.0, 0.0).astype(bf16)
        rows.append(block.T)
    level = earlier_equal(ids, rows)
    wanted = iota((TILE, TILE), 0) + 1.0
    over = jnp.zeros((1, TILE), f32)
    for b, i in enumerate(range(0, entries, TILE)):
        hit = rows[b] == wanted
        over = jnp.maximum(
            over, jnp.where((rows[b][0:1] > 0.0) & (level[b] >= float(LEVELS)), 1.0, 0.0)
        )
        for t in range(LEVELS):
            side.levels[t * TILE : (t + 1) * TILE, i : i + TILE] = jnp.where(
                hit & (level[b] == float(t)), 1.0, 0.0
            ).astype(bf16)
    flag_ref[...] = jnp.maximum(flag_ref[...], jnp.max(over, axis=1, keepdims=True))


def put(side, slot):
    side.send(FIRST(slot), side.p1_send, side.p1_recv.at[slot])


def put_done(side, slot):
    side.wait_send(FIRST(slot), side.p1_send)


def combine(side, slot, final):
    recv = side.p1_recv.at[slot]
    side.wait_recv(FIRST(slot), recv)
    terms = select_rows(side.levels[...], recv[...])
    terms = terms.reshape(LEVELS, TILE, TILE)
    if final:
        total = side.diag_term[...].T + jnp.sum(terms, axis=0)
    else:
        total = jnp.maximum(side.diag_term[...].T, jnp.max(terms, axis=0))
    own = side.own[...]
    own = own * lax.rsqrt((2.0 * total) * own + epsilon)
    side.own[...] = own
    side.own_turned[...] = own.T


def give_back(side, slot):
    side.p2_send[...] = select_rows(side.expand[...], side.own[...])
    side.send(BACK(slot), side.p2_send, side.p2_recv.at[slot])


def take_back(side, slot):
    recv = side.p2_recv.at[slot]
    side.wait_recv(BACK(slot), recv)
    scale = select_rows(side.unpack[...], recv[...])
    side.ext[...] = scale[:TILE].T
    tail = scale[TILE : TILE + TAIL]
    if side.axis == "col":
        tail = [tail] + [pltpu.roll(tail, TILE - q * TAIL, 1) for q in range(1, QUARTERS)]
        side.tail[...] = jnp.concatenate(tail, axis=0).T[:TAIL]
    else:
        side.tail[...] = jnp.concatenate([tail] * QUARTERS, axis=0).T
    side.wait_send(BACK(slot), side.p2_send)


def gather_terms(side, final):
    side.ext_term[:TILE, :] = side.ext_turned[...].T
    if side.axis == "col":
        empty = jnp.zeros((TILE - TAIL, TILE), f32)
        turned = jnp.concatenate([side.tail_term[...], empty], axis=0).T
        parts = [turned[:TAIL]]
        parts += [pltpu.roll(turned[q * TAIL : (q + 1) * TAIL], q * TAIL, 1) for q in range(1, QUARTERS)]
        side.ext_term[TILE : TILE + TAIL, :] = parts[0] + parts[1] + parts[2] + parts[3]
    else:
        parts = side.tail_term[...].T.reshape(QUARTERS, TAIL, TILE)
        side.ext_term[TILE : TILE + TAIL, :] = jnp.sum(parts, axis=0) if final else jnp.max(parts, axis=0)


def row_pass(tiles, scale, out, final):
    scale = scale[...]

    def step(g, carry):
        base = pl.multiple_of(g * GROUP, GROUP)
        results = []
        for j in range(GROUP):
            x = tiles[base + j] * scale
            reduce = jnp.sum if final else jnp.max
            results.append(reduce(x, axis=0, keepdims=True))
        out[pl.ds(base, GROUP), :] = jnp.concatenate(results, axis=0)
        return carry

    lax.fori_loop(0, tiles.shape[0] // GROUP, step, 0)


def col_pass(tiles, scale, out, final):
    def step(g, total):
        base = pl.multiple_of(g * GROUP, GROUP)
        for j in range(GROUP):
            x = tiles[base + j] * scale[pl.ds(base + j, 1), :]
            total = total + x if final else jnp.maximum(total, x)
        return total

    out[...] = lax.fori_loop(0, tiles.shape[0] // GROUP, step, jnp.zeros((TILE, TILE), f32))


def kernel(
    n_row,
    n_col,
    count_ref,
    rows_ref,
    cols_ref,
    data_ref,
    row_out,
    col_out,
    flag_out,
    diag_tiles,
    ext_tiles,
    tail_loaded,
    tail_tiles,
    key_ref,
    flag_ref,
    all_flags,
    load_sems,
    out_sems,
    near_sems,
    far_sem,
    *rest,
):
    rows = Side("col", n_col, ROW_CAP, 0, rest[: len(rest) // 2])
    cols = Side("row", n_row, COL_CAP, 1, rest[len(rest) // 2 :])
    sides = (cols, rows)

    barrier = pltpu.get_barrier_semaphore()
    for side in sides:
        for d in range(1, side.count):
            pl.semaphore_signal(barrier, inc=1, device_id={side.axis: side.partner(d)}, device_id_type=MESH)

    def load(group, part):
        tiles, first, count = ((ext_tiles, DIAG, TILE), (tail_loaded, DIAG + TILE, TAIL), (diag_tiles, 0, DIAG))[group]
        height = TILE // PARTS[group]
        at = part * height
        sem = load_sems.at[group, part]

        def step(s, carry):
            for j in range(GROUP):
                slot = s * GROUP + j
                pltpu.make_async_copy(
                    data_ref.at[first + slot, pl.ds(at, height)], tiles.at[pl.ds(at, height), slot], sem
                ).start()
            return carry

        lax.fori_loop(0, count // GROUP, step, 0)

    def loaded(group, part):
        tiles = (ext_tiles, tail_loaded, diag_tiles)[group]
        height = TILE // PARTS[group]
        whole = tiles.at[pl.ds(part * height, height)]
        pltpu.make_async_copy(whole, whole, load_sems.at[group, part]).wait()

    for group in range(2):
        for part in range(PARTS[group]):
            load(group, part)

    flag_ref[...] = jnp.zeros_like(flag_ref)
    count = count_ref[0, 0]
    for side, blocks_ref in ((cols, cols_ref), (rows, rows_ref)):
        prepare(side, blocks_ref, count, key_ref, flag_ref)
        for ref in (side.id_recv, side.p1_recv, side.p2_recv):
            empty = side.entries - side.count * side.cap
            if empty:
                ref[..., side.entries - empty :, :] = jnp.zeros((*ref.shape[:-2], empty, TILE), f32)
    for side in sides:
        fill(side)
    pl.semaphore_wait(barrier, n_row + n_col - 2)
    for side in sides:
        side.send(ID(), side.p1_send, side.id_recv)

    for part in range(PARTS[2]):
        load(2, part)

    lane = lax.broadcasted_iota(jnp.int32, (1, TILE), 1)
    ext_half = jnp.where(lane + DIAG < count, 0.5, 0.0)
    tail_half = jnp.where(lane % TAIL + (DIAG + TILE) < count, 0.5, 0.0)

    def first_pass(group, tiles, half, row_term, col_term):
        total = jnp.zeros((TILE, TILE), f32)
        steps = TILE // PARTS[group] // GROUP
        for part in range(PARTS[group]):
            loaded(group, part)

            def step(g, total):
                base = pl.multiple_of(g * GROUP, GROUP)
                results = []
                for j in range(GROUP):
                    x = jnp.abs(tiles[base + j]).T * half
                    tiles[base + j] = x
                    results.append(jnp.max(x, axis=0, keepdims=True))
                    total = jnp.maximum(total, x)
                row_term[pl.ds(base, GROUP), :] = jnp.concatenate(results, axis=0)
                return total

            total = lax.fori_loop(part * steps, (part + 1) * steps, step, total)
        col_term[...] = total

    def first_tail():
        loaded(1, 0)

        def step(g, total):
            base = pl.multiple_of(g * GROUP, GROUP)
            results = []
            for j in range(GROUP):
                x = jnp.concatenate([tail_loaded[q * TAIL + base + j] for q in range(QUARTERS)], axis=0)
                x = jnp.abs(x).T * tail_half
                tail_tiles[base + j] = x
                results.append(jnp.max(x, axis=0, keepdims=True))
                total = jnp.maximum(total, x)
            rows.tail_term[pl.ds(base, GROUP), :] = jnp.concatenate(results, axis=0)
            return total

        cols.tail_term[...] = lax.fori_loop(0, TAIL // GROUP, step, jnp.zeros((TILE, TILE), f32))

    for side in sides:
        side.ext_term[...] = jnp.zeros_like(side.ext_term)
        side.own[...] = jnp.ones_like(side.own)
    first_pass(0, ext_tiles, ext_half, rows.ext_turned, cols.ext_turned)
    first_tail()
    for side in (rows, cols):
        side.wait_send(ID(), side.p1_send)
        gather_terms(side, False)
        fill(side)
        put(side, 0)
    first_pass(2, diag_tiles, 0.5, rows.diag_term, cols.diag_term)
    for side in sides:
        side.wait_recv(ID(), side.id_recv)
        learn(side, flag_ref)
    rows.tell(flag_ref)
    for side in sides:
        combine(side, 0, False)
        give_back(side, 0)
        put_done(side, 0)

    def row_step(slot, before, final):
        take_back(cols, before)
        row_pass(ext_tiles, cols.ext, rows.ext_turned, final)
        row_pass(tail_tiles, cols.tail, rows.tail_term, final)
        gather_terms(rows, final)
        fill(rows)
        put(rows, slot)

    def col_step(slot, before, final):
        take_back(rows, before)
        col_pass(ext_tiles, rows.ext, cols.ext_turned, final)
        col_pass(tail_tiles, rows.tail, cols.tail_term, final)
        gather_terms(cols, final)
        fill(cols)
        put(cols, slot)

    col_place = col_out.at[pl.ds(pl.multiple_of(cols.me * DIAG, DIAG), DIAG)]
    kept_columns = pltpu.make_async_copy(cols.fin, col_place, out_sems.at[1])

    def spread_columns():
        cols.fin[...] = cols.own[...]
        for d in range(1, cols.count):
            cols.copy(LAST(), cols.fin, col_place, cols.partner(d)).start()
        kept_columns.start()

    def sweep(t, final):
        slot, before = t % 2, (t + 1) % 2
        first, second = (row_step, col_step) if t % 2 else (col_step, row_step)
        first(slot, before, final)
        second(slot, before, final)
        row_pass(diag_tiles, cols.own_turned, rows.diag_term, final)
        col_pass(diag_tiles, rows.own_turned, cols.diag_term, final)
        for side in (rows, cols) if t % 2 else (cols, rows):
            combine(side, slot, final)
            if not final:
                give_back(side, slot)
            elif side is cols:
                spread_columns()
        for side in sides:
            put_done(side, slot)

    for t in range(1, SWEEPS):
        sweep(t, False)
    all_flags[...] = rows.told()
    cols.tell(all_flags)
    sweep(SWEEPS, True)

    height = DIAG // 2
    x, z = lax.div(rows.me, WIDTH), lax.rem(rows.me, WIDTH)

    def at(half, near, far):
        first, second = (z, x) if half == 0 else (x, z)
        first, second = lax.rem(first + near, WIDTH), lax.rem(second + far, WIDTH)
        return second * WIDTH + first if half == 0 else first * WIDTH + second

    def block(half, device):
        return row_out.at[pl.ds(pl.multiple_of(device * DIAG + half * height, 8), height)]

    def row_copy(half, source, sems, device):
        there = block(half, source[1])
        return pltpu.make_async_remote_copy(
            src_ref=source[0],
            dst_ref=there,
            send_sem=sems[0],
            recv_sem=sems[1],
            device_id={"col": device},
            device_id_type=MESH,
        )

    def near_copy(half, d, device, owner):
        sems = rows.send_sems.at[3], near_sems.at[half, d]
        return row_copy(half, (rows.fin.at[pl.ds(half * height, height)], owner), sems, device)

    def far_copy(half, e, d, device, owner):
        sems = rows.send_sems.at[3], far_sem.at[0]
        source = rows.fin.at[pl.ds(half * height, height)] if e == 0 else block(half, owner)
        return row_copy(half, (source, owner), sems, device)

    rows.fin[...] = rows.own[...]
    for d in range(1, WIDTH):
        for half in range(2):
            near_copy(half, d, at(half, d, 0), rows.me).start()
    for d in range(1, WIDTH):
        for half in range(2):
            far_copy(half, 0, d, at(half, 0, d), rows.me).start()
    row_place = row_out.at[pl.ds(pl.multiple_of(rows.me * DIAG, DIAG), DIAG)]
    kept_rows = pltpu.make_async_copy(rows.fin, row_place, out_sems.at[0])
    kept_rows.start()
    flag_out[0, 0] = jnp.max(cols.told()).astype(jnp.int32)
    for e in range(1, WIDTH):
        for half in range(2):
            owner = at(half, WIDTH - e, 0)
            near_copy(half, e, owner, owner).wait_recv()
            for d in range(1, WIDTH):
                far_copy(half, e, d, at(half, 0, d), owner).start()
    far_count, near_count = 2 * WIDTH * (WIDTH - 1), 2 * (WIDTH - 1)
    rows.wait(far_sem.at[0], row_out, far_count * height)
    cols.wait(cols.recv_sems.at[3, 0], col_out, (cols.count - 1) * DIAG)
    cols.wait(cols.send_sems.at[3], col_out, (cols.count - 1) * DIAG)
    rows.wait(rows.send_sems.at[3], row_out, (far_count + near_count) * height)
    kept_rows.wait()
    kept_columns.wait()


def side_scratch(count, cap, tail_scale, tail_term):
    entries = padded(count * cap)
    return [
        pltpu.VMEM((DIAG, TILE), f32),
        pltpu.VMEM((TILE, DIAG), f32),
        pltpu.VMEM((TILE, TILE), f32),
        pltpu.VMEM((tail_scale, TILE), f32),
        pltpu.VMEM((TILE, DIAG), f32),
        pltpu.VMEM((TILE, TILE), f32),
        pltpu.VMEM((tail_term, TILE), f32),
        pltpu.VMEM((EXT, TILE), f32),
        pltpu.VMEM((entries, EXT), bf16),
        pltpu.VMEM((EXT, entries), bf16),
        pltpu.VMEM((LEVELS * DIAG, entries), bf16),
        pltpu.VMEM((entries, DIAG), bf16),
        pltpu.VMEM((entries, TILE), f32),
        pltpu.VMEM((entries, TILE), f32),
        pltpu.VMEM((2, entries, TILE), f32),
        pltpu.VMEM((entries, TILE), f32),
        pltpu.VMEM((2, entries, TILE), f32),
        pltpu.VMEM((DIAG, TILE), f32),
        pltpu.VMEM((count, 8, TILE), f32),
        pltpu.SemaphoreType.DMA((5,)),
        pltpu.SemaphoreType.DMA((5, 2)),
    ]


def sparse(tiles, row_blocks, column_blocks, used_count, n_row, n_col):
    assert tiles.shape[0] == DIAG + TILE + TAIL and n_col == WIDTH * WIDTH
    return pl.pallas_call(
        functools.partial(kernel, n_row, n_col),
        out_shape=(
            jax.ShapeDtypeStruct((n_col * DIAG, TILE), f32),
            jax.ShapeDtypeStruct((n_row * DIAG, TILE), f32),
            jax.ShapeDtypeStruct((1, 1), jnp.int32),
        ),
        in_specs=[
            pl.BlockSpec(memory_space=pltpu.SMEM),
            pl.BlockSpec(memory_space=pltpu.VMEM),
            pl.BlockSpec(memory_space=pltpu.VMEM),
            pl.BlockSpec(memory_space=pltpu.HBM),
        ],
        out_specs=(
            pl.BlockSpec(memory_space=pl.ANY),
            pl.BlockSpec(memory_space=pl.ANY),
            pl.BlockSpec(memory_space=pltpu.SMEM),
        ),
        scratch_shapes=[
            pltpu.VMEM((TILE, TILE, DIAG), f32),
            pltpu.VMEM((TILE, TILE, TILE), f32),
            pltpu.VMEM((TILE, TAIL, TILE), f32),
            pltpu.VMEM((TAIL, TILE, TILE), f32),
            pltpu.VMEM((8, EXT), f32),
            pltpu.VMEM((8, TILE), f32),
            pltpu.VMEM((8, TILE), f32),
            pltpu.SemaphoreType.DMA((3, max(PARTS))),
            pltpu.SemaphoreType.DMA((2,)),
            pltpu.SemaphoreType.DMA((2, WIDTH)),
            pltpu.SemaphoreType.DMA((1,)),
            *side_scratch(n_col, ROW_CAP, TAIL, TAIL),
            *side_scratch(n_row, COL_CAP, TILE, TILE),
        ],
        compiler_params=pltpu.CompilerParams(
            collective_id=0, has_side_effects=True, vmem_limit_bytes=52 << 20
        ),
    )(used_count.reshape(1, 1), row_blocks.reshape(1, -1), column_blocks.reshape(1, -1), tiles)


def settle_kernel(row_ref, col_ref, row_out, col_out, sems):
    copies = []
    for ref, out in ((row_ref, row_out), (col_ref, col_out)):
        for i in range(ref.shape[0] // PIECE):
            at = pl.ds(i * PIECE, PIECE)
            copies.append(pltpu.make_async_copy(ref.at[at], out.at[at], sems.at[len(copies)]))
    for copy in copies:
        copy.start()
    for copy in copies:
        copy.wait()


def settle(row_scale, column_scale):
    pieces = (row_scale.shape[0] + column_scale.shape[0]) // PIECE
    anywhere = pl.BlockSpec(memory_space=pl.ANY)
    return pl.pallas_call(
        settle_kernel,
        out_shape=tuple(jax.ShapeDtypeStruct(x.shape, x.dtype) for x in (row_scale, column_scale)),
        in_specs=[anywhere, anywhere],
        out_specs=(anywhere, anywhere),
        scratch_shapes=[pltpu.SemaphoreType.DMA((pieces,))],
    )(row_scale, column_scale)


def gathered(x, axis):
    n = lax.axis_size(axis)
    me = lax.axis_index(axis)
    ring = [(i, (i + 1) % n) for i in range(n)]
    out = jnp.zeros((n,) + x.shape, x.dtype).at[me].set(x)

    def step(i, carry):
        out, y = carry
        y = lax.ppermute(y, axis, ring)
        return out.at[lax.rem(me + n - i, n)].set(y), y

    return lax.fori_loop(1, n, step, (out, x))[0]


def dense(blocks, row_blocks, column_blocks, used_count):
    slots, side = blocks.shape[:2]
    row_length = DIAG * lax.axis_size("col")
    column_length = DIAG * lax.axis_size("row")
    in_use = jnp.arange(slots, dtype=jnp.int32) < used_count
    magnitude = jnp.where(in_use[:, None, None], jnp.abs(blocks), f32(0.0))

    def sweep(t, carry):
        row_scale, column_scale = carry
        scaled = magnitude * row_scale[row_blocks][:, :, None] * column_scale[column_blocks][:, None, :]
        no_rows = jnp.zeros((row_length, side), f32)
        no_columns = jnp.zeros((column_length, side), f32)
        peak = t < SWEEPS

        def peaks():
            rows = no_rows.at[row_blocks].max(scaled.max(axis=2))
            columns = no_columns.at[column_blocks].max(scaled.max(axis=1))
            return rows, columns

        def totals():
            rows = no_rows.at[row_blocks].add(scaled.sum(axis=2))
            columns = no_columns.at[column_blocks].add(scaled.sum(axis=1))
            return rows, columns

        rows, columns = lax.cond(peak, peaks, totals)
        rows, columns = gathered(rows, "col"), gathered(columns, "row")
        rows = jnp.where(peak, rows.max(axis=0), rows.sum(axis=0))
        columns = jnp.where(peak, columns.max(axis=0), columns.sum(axis=0))
        return row_scale * lax.rsqrt(rows + epsilon), column_scale * lax.rsqrt(columns + epsilon)

    start = (jnp.ones((row_length, side), f32), jnp.ones((column_length, side), f32))
    return lax.fori_loop(0, SWEEPS + 1, sweep, start)


def on_device(tile_data, tile_rows, tile_cols, tile_counts):
    blocks = tile_data[0, 0]
    row_blocks = tile_rows[0, 0]
    column_blocks = tile_cols[0, 0]
    used_count = tile_counts[0, 0]
    n_row, n_col = lax.axis_size("row"), lax.axis_size("col")
    row_scale, column_scale, flag = sparse(blocks, row_blocks, column_blocks, used_count, n_row, n_col)
    row_scale, column_scale = lax.cond(
        flag[0, 0] > 0,
        lambda: dense(blocks, row_blocks, column_blocks, used_count),
        lambda: settle(row_scale, column_scale),
    )
    return (row_scale.reshape(-1), column_scale.reshape(-1))


def solution(mesh):
    placed = (
        P("row", "col", None, None, None),
        P("row", "col", None),
        P("row", "col", None),
        P("row", "col"),
    )
    return jax.shard_map(
        on_device, mesh=mesh, in_specs=placed, out_specs=(P("row"), P("col")), check_vma=False
    )
```

```python
import functools

import jax
import jax.numpy as jnp
from jax import lax
from jax.experimental import pallas as pl
from jax.experimental.pallas import tpu as pltpu
from jax.sharding import PartitionSpec as P

TILE = 128
DIAG = 128
SWEEPS = 4
epsilon = 1e-06

EXT = 256
ROW_CAP = 24
COL_CAP = 40
LEVELS = 8
GROUP = 8
PARTS = (2, 1, 1)
PIECE = 256
HOPS = (0, 1, 2, 1)
WIDTH = 4
TAIL = 32
QUARTERS = TILE // TAIL

f32 = jnp.float32
bf16 = jnp.bfloat16
MESH = pltpu.DeviceIdType.MESH if hasattr(pltpu, "DeviceIdType") else pl.DeviceIdType.MESH


def halves(x):
    hi = x.astype(bf16)
    lo = (x - hi.astype(f32)).astype(bf16)
    return jnp.concatenate([hi, lo], axis=1)


def select_rows(onehot, x):
    y = jnp.dot(onehot, halves(x), preferred_element_type=f32)
    return y[:, :TILE] + y[:, TILE:]


def iota(shape, dim):
    return lax.broadcasted_iota(jnp.int32, shape, dim).astype(f32)


def columns(row):
    parts = [
        jnp.broadcast_to(row[:, i : i + TILE], (TILE, TILE)).T for i in range(0, row.shape[1], TILE)
    ]
    return jnp.concatenate(parts, axis=0)


def earlier_equal(cols, rows):
    count = cols.shape[0] // TILE
    out = []
    before = iota((TILE, TILE), 0) < iota((TILE, TILE), 1)
    for b in range(count):
        total = jnp.zeros((1, TILE), f32)
        here = rows[b]
        for a in range(b + 1):
            same = cols[a * TILE : (a + 1) * TILE] == here
            if a == b:
                same = same & before
            total = total + jnp.sum(jnp.where(same, 1.0, 0.0), axis=0, keepdims=True)
        out.append(total)
    return out


def padded(entries):
    return -(-entries // TILE) * TILE


class Side:
    def __init__(self, axis, count, cap, key_row, refs):
        self.axis, self.count, self.cap, self.key_row = axis, count, cap, key_row
        self.entries = padded(count * cap)
        (
            self.own,
            self.own_turned,
            self.ext,
            self.tail,
            self.diag_term,
            self.ext_turned,
            self.tail_term,
            self.ext_term,
            self.pack,
            self.unpack,
            self.levels,
            self.expand,
            self.id_recv,
            self.p1_send,
            self.p1_recv,
            self.p2_send,
            self.p2_recv,
            self.fin,
            self.flags,
            self.send_sems,
            self.recv_sems,
        ) = refs
        self.me = lax.axis_index(axis)
        self.minor = minor = count // WIDTH
        steps = [(a, b) for a in range(WIDTH) for b in range(minor) if a or b]
        self.steps = sorted(steps, key=lambda s: -sum(HOPS[i] for i in s))
        self.major_me, self.minor_me = lax.div(self.me, minor), lax.rem(self.me, minor)

    def shifted(self, a, b):
        return lax.rem(self.major_me + a, WIDTH) * self.minor + lax.rem(self.minor_me + b, self.minor)

    def partner(self, d):
        a, b = self.steps[d - 1]
        return self.shifted(a, b)

    def copy(self, kind, src, dst, peer):
        kind, slot = kind
        return pltpu.make_async_remote_copy(
            src_ref=src,
            dst_ref=dst,
            send_sem=self.send_sems.at[kind],
            recv_sem=self.recv_sems.at[kind, slot],
            device_id={self.axis: peer},
            device_id_type=MESH,
        )

    def place(self, ref, peer):
        return ref.at[pl.ds(pl.multiple_of(peer * self.cap, 8), self.cap)]

    def send(self, kind, send, recv):
        for d in range(1, self.count):
            peer = self.partner(d)
            self.copy(kind, self.place(send, peer), self.place(recv, self.me), peer).start()
        self.place(recv, self.me)[...] = self.place(send, self.me)[...]

    def wait(self, sem, ref, size):
        whole = ref.at[pl.ds(0, size)]
        pltpu.make_async_copy(whole, whole, sem).wait()

    def wait_send(self, kind, send):
        self.wait(self.send_sems.at[kind[0]], send, (self.count - 1) * self.cap)

    def wait_recv(self, kind, recv):
        self.wait(self.recv_sems.at[kind[0], kind[1]], recv, (self.count - 1) * self.cap)

    def tell(self, flag_ref):
        for d in range(1, self.count):
            self.copy((4, 0), flag_ref, self.flags.at[self.me], self.partner(d)).start()
        self.flags[self.me] = flag_ref[...]

    def told(self):
        self.wait(self.recv_sems.at[4, 0], self.flags, self.count - 1)
        self.wait(self.send_sems.at[4], self.flags, self.count - 1)
        return jnp.max(self.flags[...], axis=0)


def ID():
    return (0, 0)


def FIRST(slot):
    return (1, slot)


def BACK(slot):
    return (2, slot)


def LAST():
    return (3, 0)


def prepare(side, blocks_ref, used_count, key_ref, flag_ref):
    cap, entries = side.cap, side.entries
    blocks = blocks_ref[...].astype(f32)
    key_ref[...] = jnp.full_like(key_ref, -1.0)
    key_ref[0:1, :TILE] = blocks[:, DIAG : DIAG + TILE]
    key_ref[0:1, TILE : TILE + TAIL] = blocks[:, DIAG + TILE :]
    slot = lax.broadcasted_iota(jnp.int32, (1, EXT), 1) + DIAG
    key = jnp.where(slot < used_count, key_ref[0:1, :], -1.0)
    owner = jnp.floor(key * (1.0 / DIAG))
    local = key - owner * DIAG
    used = key >= 0.0
    owner_cols = columns(owner)
    rank = earlier_equal(owner_cols, [owner[:, :TILE], owner[:, TILE:]])
    rank = jnp.concatenate(rank, axis=1)
    fits = used & (rank < float(cap))
    dest = jnp.where(fits, owner * cap + rank, -1.0)
    over = jnp.where(used & (rank >= float(cap)), 1.0, 0.0)
    flag_ref[...] = jnp.maximum(flag_ref[...], jnp.max(over, axis=1, keepdims=True))
    side.pack[...] = jnp.where(iota((entries, EXT), 0) == dest, 1.0, 0.0).astype(bf16)
    dest_cols = columns(dest)
    for i in range(0, entries, TILE):
        lanes = iota((EXT, TILE), 1) + float(i)
        side.unpack[:, i : i + TILE] = jnp.where(dest_cols == lanes, 1.0, 0.0).astype(bf16)
    side.ext_term[...] = jnp.where(columns(jnp.where(used, 1.0, 0.0)) > 0.0, columns(local) + 1.0, 0.0)


def fill(side):
    side.p1_send[...] = select_rows(side.pack[...], side.ext_term[...])


def learn(side, flag_ref):
    entries = side.entries
    ids = side.id_recv[...]
    lanes = iota((TILE, TILE), 1)
    rows = []
    for i in range(0, entries, TILE):
        block = ids[i : i + TILE]
        side.expand[i : i + TILE, :] = jnp.where(block == lanes + 1.0, 1.0, 0.0).astype(bf16)
        rows.append(block.T)
    level = earlier_equal(ids, rows)
    wanted = iota((TILE, TILE), 0) + 1.0
    over = jnp.zeros((1, TILE), f32)
    for b, i in enumerate(range(0, entries, TILE)):
        hit = rows[b] == wanted
        over = jnp.maximum(
            over, jnp.where((rows[b][0:1] > 0.0) & (level[b] >= float(LEVELS)), 1.0, 0.0)
        )
        for t in range(LEVELS):
            side.levels[t * TILE : (t + 1) * TILE, i : i + TILE] = jnp.where(
                hit & (level[b] == float(t)), 1.0, 0.0
            ).astype(bf16)
    flag_ref[...] = jnp.maximum(flag_ref[...], jnp.max(over, axis=1, keepdims=True))


def put(side, slot):
    side.send(FIRST(slot), side.p1_send, side.p1_recv.at[slot])


def put_done(side, slot):
    side.wait_send(FIRST(slot), side.p1_send)


def combine(side, slot, final):
    recv = side.p1_recv.at[slot]
    side.wait_recv(FIRST(slot), recv)
    terms = select_rows(side.levels[...], recv[...])
    terms = terms.reshape(LEVELS, TILE, TILE)
    if final:
        total = side.diag_term[...].T + jnp.sum(terms, axis=0)
    else:
        total = jnp.maximum(side.diag_term[...].T, jnp.max(terms, axis=0))
    own = side.own[...]
    own = own * lax.rsqrt((2.0 * total) * own + epsilon)
    side.own[...] = own
    side.own_turned[...] = own.T


def give_back(side, slot):
    side.p2_send[...] = select_rows(side.expand[...], side.own[...])
    side.send(BACK(slot), side.p2_send, side.p2_recv.at[slot])


def take_back(side, slot):
    recv = side.p2_recv.at[slot]
    side.wait_recv(BACK(slot), recv)
    scale = select_rows(side.unpack[...], recv[...])
    side.ext[...] = scale[:TILE].T
    tail = scale[TILE : TILE + TAIL]
    if side.axis == "col":
        tail = [tail] + [pltpu.roll(tail, TILE - q * TAIL, 1) for q in range(1, QUARTERS)]
        side.tail[...] = jnp.concatenate(tail, axis=0).T[:TAIL]
    else:
        side.tail[...] = jnp.concatenate([tail] * QUARTERS, axis=0).T
    side.wait_send(BACK(slot), side.p2_send)


def gather_terms(side, final):
    side.ext_term[:TILE, :] = side.ext_turned[...].T
    if side.axis == "col":
        empty = jnp.zeros((TILE - TAIL, TILE), f32)
        turned = jnp.concatenate([side.tail_term[...], empty], axis=0).T
        parts = [turned[:TAIL]]
        parts += [pltpu.roll(turned[q * TAIL : (q + 1) * TAIL], q * TAIL, 1) for q in range(1, QUARTERS)]
        side.ext_term[TILE : TILE + TAIL, :] = parts[0] + parts[1] + parts[2] + parts[3]
    else:
        parts = side.tail_term[...].T.reshape(QUARTERS, TAIL, TILE)
        side.ext_term[TILE : TILE + TAIL, :] = jnp.sum(parts, axis=0) if final else jnp.max(parts, axis=0)


def row_pass(tiles, scale, out, final):
    scale = scale[...]

    def step(g, carry):
        base = pl.multiple_of(g * GROUP, GROUP)
        results = []
        for j in range(GROUP):
            x = tiles[base + j] * scale
            reduce = jnp.sum if final else jnp.max
            results.append(reduce(x, axis=0, keepdims=True))
        out[pl.ds(base, GROUP), :] = jnp.concatenate(results, axis=0)
        return carry

    lax.fori_loop(0, tiles.shape[0] // GROUP, step, 0)


def col_pass(tiles, scale, out, final):
    def step(g, total):
        base = pl.multiple_of(g * GROUP, GROUP)
        for j in range(GROUP):
            x = tiles[base + j] * scale[pl.ds(base + j, 1), :]
            total = total + x if final else jnp.maximum(total, x)
        return total

    out[...] = lax.fori_loop(0, tiles.shape[0] // GROUP, step, jnp.zeros((TILE, TILE), f32))


def kernel(
    n_row,
    n_col,
    count_ref,
    rows_ref,
    cols_ref,
    data_ref,
    row_out,
    col_out,
    flag_out,
    diag_tiles,
    ext_tiles,
    tail_loaded,
    tail_tiles,
    key_ref,
    flag_ref,
    all_flags,
    load_sems,
    out_sems,
    near_sems,
    far_sem,
    *rest,
):
    rows = Side("col", n_col, ROW_CAP, 0, rest[: len(rest) // 2])
    cols = Side("row", n_row, COL_CAP, 1, rest[len(rest) // 2 :])
    sides = (cols, rows)

    barrier = pltpu.get_barrier_semaphore()
    for side in sides:
        for d in range(1, side.count):
            pl.semaphore_signal(barrier, inc=1, device_id={side.axis: side.partner(d)}, device_id_type=MESH)

    def load(group, part):
        tiles, first, count = ((ext_tiles, DIAG, TILE), (tail_loaded, DIAG + TILE, TAIL), (diag_tiles, 0, DIAG))[group]
        height = TILE // PARTS[group]
        at = part * height
        sem = load_sems.at[group, part]

        def step(s, carry):
            for j in range(GROUP):
                slot = s * GROUP + j
                pltpu.make_async_copy(
                    data_ref.at[first + slot, pl.ds(at, height)], tiles.at[pl.ds(at, height), slot], sem
                ).start()
            return carry

        lax.fori_loop(0, count // GROUP, step, 0)

    def loaded(group, part):
        tiles = (ext_tiles, tail_loaded, diag_tiles)[group]
        height = TILE // PARTS[group]
        whole = tiles.at[pl.ds(part * height, height)]
        pltpu.make_async_copy(whole, whole, load_sems.at[group, part]).wait()

    for group in range(2):
        for part in range(PARTS[group]):
            load(group, part)

    flag_ref[...] = jnp.zeros_like(flag_ref)
    count = count_ref[0, 0]
    for side, blocks_ref in ((cols, cols_ref), (rows, rows_ref)):
        prepare(side, blocks_ref, count, key_ref, flag_ref)
        for ref in (side.id_recv, side.p1_recv, side.p2_recv):
            empty = side.entries - side.count * side.cap
            if empty:
                ref[..., side.entries - empty :, :] = jnp.zeros((*ref.shape[:-2], empty, TILE), f32)
    for side in sides:
        fill(side)
    pl.semaphore_wait(barrier, n_row + n_col - 2)
    for side in sides:
        side.send(ID(), side.p1_send, side.id_recv)

    for part in range(PARTS[2]):
        load(2, part)

    lane = lax.broadcasted_iota(jnp.int32, (1, TILE), 1)
    ext_half = jnp.where(lane + DIAG < count, 0.5, 0.0)
    tail_half = jnp.where(lane % TAIL + (DIAG + TILE) < count, 0.5, 0.0)

    def first_pass(group, tiles, half, row_term, col_term):
        total = jnp.zeros((TILE, TILE), f32)
        steps = TILE // PARTS[group] // GROUP
        for part in range(PARTS[group]):
            loaded(group, part)

            def step(g, total):
                base = pl.multiple_of(g * GROUP, GROUP)
                results = []
                for j in range(GROUP):
                    x = jnp.abs(tiles[base + j]).T * half
                    tiles[base + j] = x
                    results.append(jnp.max(x, axis=0, keepdims=True))
                    total = jnp.maximum(total, x)
                row_term[pl.ds(base, GROUP), :] = jnp.concatenate(results, axis=0)
                return total

            total = lax.fori_loop(part * steps, (part + 1) * steps, step, total)
        col_term[...] = total

    def first_tail():
        loaded(1, 0)

        def step(g, total):
            base = pl.multiple_of(g * GROUP, GROUP)
            results = []
            for j in range(GROUP):
                x = jnp.concatenate([tail_loaded[q * TAIL + base + j] for q in range(QUARTERS)], axis=0)
                x = jnp.abs(x).T * tail_half
                tail_tiles[base + j] = x
                results.append(jnp.max(x, axis=0, keepdims=True))
                total = jnp.maximum(total, x)
            rows.tail_term[pl.ds(base, GROUP), :] = jnp.concatenate(results, axis=0)
            return total

        cols.tail_term[...] = lax.fori_loop(0, TAIL // GROUP, step, jnp.zeros((TILE, TILE), f32))

    for side in sides:
        side.ext_term[...] = jnp.zeros_like(side.ext_term)
        side.own[...] = jnp.ones_like(side.own)
    first_pass(0, ext_tiles, ext_half, rows.ext_turned, cols.ext_turned)
    first_tail()
    for side in (rows, cols):
        side.wait_send(ID(), side.p1_send)
        gather_terms(side, False)
        fill(side)
        put(side, 0)
    first_pass(2, diag_tiles, 0.5, rows.diag_term, cols.diag_term)
    for side in sides:
        side.wait_recv(ID(), side.id_recv)
        learn(side, flag_ref)
    rows.tell(flag_ref)
    for side in sides:
        combine(side, 0, False)
        give_back(side, 0)
        put_done(side, 0)

    def row_step(slot, before, final):
        take_back(cols, before)
        row_pass(ext_tiles, cols.ext, rows.ext_turned, final)
        row_pass(tail_tiles, cols.tail, rows.tail_term, final)
        gather_terms(rows, final)
        fill(rows)
        put(rows, slot)

    def col_step(slot, before, final):
        take_back(rows, before)
        col_pass(ext_tiles, rows.ext, cols.ext_turned, final)
        col_pass(tail_tiles, rows.tail, cols.tail_term, final)
        gather_terms(cols, final)
        fill(cols)
        put(cols, slot)

    col_place = col_out.at[pl.ds(pl.multiple_of(cols.me * DIAG, DIAG), DIAG)]
    kept_columns = pltpu.make_async_copy(cols.fin, col_place, out_sems.at[1])

    def spread_columns():
        cols.fin[...] = cols.own[...]
        for d in range(1, cols.count):
            cols.copy(LAST(), cols.fin, col_place, cols.partner(d)).start()
        kept_columns.start()

    def sweep(t, final):
        slot, before = t % 2, (t + 1) % 2
        first, second = (row_step, col_step) if t % 2 else (col_step, row_step)
        first(slot, before, final)
        if t % 2:
            row_pass(diag_tiles, cols.own_turned, rows.diag_term, final)
        second(slot, before, final)
        if t % 2 == 0:
            row_pass(diag_tiles, cols.own_turned, rows.diag_term, final)
        col_pass(diag_tiles, rows.own_turned, cols.diag_term, final)
        for side in (rows, cols) if t % 2 else (cols, rows):
            combine(side, slot, final)
            if not final:
                give_back(side, slot)
            elif side is cols:
                spread_columns()
        for side in sides:
            put_done(side, slot)

    for t in range(1, SWEEPS):
        sweep(t, False)
    all_flags[...] = rows.told()
    cols.tell(all_flags)
    sweep(SWEEPS, True)

    height = DIAG // 2
    x, z = lax.div(rows.me, WIDTH), lax.rem(rows.me, WIDTH)

    def at(half, near, far):
        first, second = (z, x) if half == 0 else (x, z)
        first, second = lax.rem(first + near, WIDTH), lax.rem(second + far, WIDTH)
        return second * WIDTH + first if half == 0 else first * WIDTH + second

    def block(half, device):
        return row_out.at[pl.ds(pl.multiple_of(device * DIAG + half * height, 8), height)]

    def row_copy(half, source, sems, device):
        there = block(half, source[1])
        return pltpu.make_async_remote_copy(
            src_ref=source[0],
            dst_ref=there,
            send_sem=sems[0],
            recv_sem=sems[1],
            device_id={"col": device},
            device_id_type=MESH,
        )

    def near_copy(half, d, device, owner):
        sems = rows.send_sems.at[3], near_sems.at[half, d]
        return row_copy(half, (rows.fin.at[pl.ds(half * height, height)], owner), sems, device)

    def far_copy(half, e, d, device, owner):
        sems = rows.send_sems.at[3], far_sem.at[0]
        source = rows.fin.at[pl.ds(half * height, height)] if e == 0 else block(half, owner)
        return row_copy(half, (source, owner), sems, device)

    rows.fin[...] = rows.own[...]
    for d in range(1, WIDTH):
        for half in range(2):
            near_copy(half, d, at(half, d, 0), rows.me).start()
    for d in range(1, WIDTH):
        for half in range(2):
            far_copy(half, 0, d, at(half, 0, d), rows.me).start()
    row_place = row_out.at[pl.ds(pl.multiple_of(rows.me * DIAG, DIAG), DIAG)]
    kept_rows = pltpu.make_async_copy(rows.fin, row_place, out_sems.at[0])
    kept_rows.start()
    flag_out[0, 0] = jnp.max(cols.told()).astype(jnp.int32)
    for e in range(1, WIDTH):
        for half in range(2):
            owner = at(half, WIDTH - e, 0)
            near_copy(half, e, owner, owner).wait_recv()
            for d in range(1, WIDTH):
                far_copy(half, e, d, at(half, 0, d), owner).start()
    far_count, near_count = 2 * WIDTH * (WIDTH - 1), 2 * (WIDTH - 1)
    rows.wait(far_sem.at[0], row_out, far_count * height)
    cols.wait(cols.recv_sems.at[3, 0], col_out, (cols.count - 1) * DIAG)
    cols.wait(cols.send_sems.at[3], col_out, (cols.count - 1) * DIAG)
    rows.wait(rows.send_sems.at[3], row_out, (far_count + near_count) * height)
    kept_rows.wait()
    kept_columns.wait()


def side_scratch(count, cap, tail_scale, tail_term):
    entries = padded(count * cap)
    return [
        pltpu.VMEM((DIAG, TILE), f32),
        pltpu.VMEM((TILE, DIAG), f32),
        pltpu.VMEM((TILE, TILE), f32),
        pltpu.VMEM((tail_scale, TILE), f32),
        pltpu.VMEM((TILE, DIAG), f32),
        pltpu.VMEM((TILE, TILE), f32),
        pltpu.VMEM((tail_term, TILE), f32),
        pltpu.VMEM((EXT, TILE), f32),
        pltpu.VMEM((entries, EXT), bf16),
        pltpu.VMEM((EXT, entries), bf16),
        pltpu.VMEM((LEVELS * DIAG, entries), bf16),
        pltpu.VMEM((entries, DIAG), bf16),
        pltpu.VMEM((entries, TILE), f32),
        pltpu.VMEM((entries, TILE), f32),
        pltpu.VMEM((2, entries, TILE), f32),
        pltpu.VMEM((entries, TILE), f32),
        pltpu.VMEM((2, entries, TILE), f32),
        pltpu.VMEM((DIAG, TILE), f32),
        pltpu.VMEM((count, 8, TILE), f32),
        pltpu.SemaphoreType.DMA((5,)),
        pltpu.SemaphoreType.DMA((5, 2)),
    ]


def sparse(tiles, row_blocks, column_blocks, used_count, n_row, n_col):
    assert tiles.shape[0] == DIAG + TILE + TAIL and n_col == WIDTH * WIDTH
    return pl.pallas_call(
        functools.partial(kernel, n_row, n_col),
        out_shape=(
            jax.ShapeDtypeStruct((n_col * DIAG, TILE), f32),
            jax.ShapeDtypeStruct((n_row * DIAG, TILE), f32),
            jax.ShapeDtypeStruct((1, 1), jnp.int32),
        ),
        in_specs=[
            pl.BlockSpec(memory_space=pltpu.SMEM),
            pl.BlockSpec(memory_space=pltpu.VMEM),
            pl.BlockSpec(memory_space=pltpu.VMEM),
            pl.BlockSpec(memory_space=pltpu.HBM),
        ],
        out_specs=(
            pl.BlockSpec(memory_space=pl.ANY),
            pl.BlockSpec(memory_space=pl.ANY),
            pl.BlockSpec(memory_space=pltpu.SMEM),
        ),
        scratch_shapes=[
            pltpu.VMEM((TILE, TILE, DIAG), f32),
            pltpu.VMEM((TILE, TILE, TILE), f32),
            pltpu.VMEM((TILE, TAIL, TILE), f32),
            pltpu.VMEM((TAIL, TILE, TILE), f32),
            pltpu.VMEM((8, EXT), f32),
            pltpu.VMEM((8, TILE), f32),
            pltpu.VMEM((8, TILE), f32),
            pltpu.SemaphoreType.DMA((3, max(PARTS))),
            pltpu.SemaphoreType.DMA((2,)),
            pltpu.SemaphoreType.DMA((2, WIDTH)),
            pltpu.SemaphoreType.DMA((1,)),
            *side_scratch(n_col, ROW_CAP, TAIL, TAIL),
            *side_scratch(n_row, COL_CAP, TILE, TILE),
        ],
        compiler_params=pltpu.CompilerParams(
            collective_id=0, has_side_effects=True, vmem_limit_bytes=52 << 20
        ),
    )(used_count.reshape(1, 1), row_blocks.reshape(1, -1), column_blocks.reshape(1, -1), tiles)


def settle_kernel(row_ref, col_ref, row_out, col_out, sems):
    copies = []
    for ref, out in ((row_ref, row_out), (col_ref, col_out)):
        for i in range(ref.shape[0] // PIECE):
            at = pl.ds(i * PIECE, PIECE)
            copies.append(pltpu.make_async_copy(ref.at[at], out.at[at], sems.at[len(copies)]))
    for copy in copies:
        copy.start()
    for copy in copies:
        copy.wait()


def settle(row_scale, column_scale):
    pieces = (row_scale.shape[0] + column_scale.shape[0]) // PIECE
    anywhere = pl.BlockSpec(memory_space=pl.ANY)
    return pl.pallas_call(
        settle_kernel,
        out_shape=tuple(jax.ShapeDtypeStruct(x.shape, x.dtype) for x in (row_scale, column_scale)),
        in_specs=[anywhere, anywhere],
        out_specs=(anywhere, anywhere),
        scratch_shapes=[pltpu.SemaphoreType.DMA((pieces,))],
    )(row_scale, column_scale)


def gathered(x, axis):
    n = lax.axis_size(axis)
    me = lax.axis_index(axis)
    ring = [(i, (i + 1) % n) for i in range(n)]
    out = jnp.zeros((n,) + x.shape, x.dtype).at[me].set(x)

    def step(i, carry):
        out, y = carry
        y = lax.ppermute(y, axis, ring)
        return out.at[lax.rem(me + n - i, n)].set(y), y

    return lax.fori_loop(1, n, step, (out, x))[0]


def dense(blocks, row_blocks, column_blocks, used_count):
    slots, side = blocks.shape[:2]
    row_length = DIAG * lax.axis_size("col")
    column_length = DIAG * lax.axis_size("row")
    in_use = jnp.arange(slots, dtype=jnp.int32) < used_count
    magnitude = jnp.where(in_use[:, None, None], jnp.abs(blocks), f32(0.0))

    def sweep(t, carry):
        row_scale, column_scale = carry
        scaled = magnitude * row_scale[row_blocks][:, :, None] * column_scale[column_blocks][:, None, :]
        no_rows = jnp.zeros((row_length, side), f32)
        no_columns = jnp.zeros((column_length, side), f32)
        peak = t < SWEEPS

        def peaks():
            rows = no_rows.at[row_blocks].max(scaled.max(axis=2))
            columns = no_columns.at[column_blocks].max(scaled.max(axis=1))
            return rows, columns

        def totals():
            rows = no_rows.at[row_blocks].add(scaled.sum(axis=2))
            columns = no_columns.at[column_blocks].add(scaled.sum(axis=1))
            return rows, columns

        rows, columns = lax.cond(peak, peaks, totals)
        rows, columns = gathered(rows, "col"), gathered(columns, "row")
        rows = jnp.where(peak, rows.max(axis=0), rows.sum(axis=0))
        columns = jnp.where(peak, columns.max(axis=0), columns.sum(axis=0))
        return row_scale * lax.rsqrt(rows + epsilon), column_scale * lax.rsqrt(columns + epsilon)

    start = (jnp.ones((row_length, side), f32), jnp.ones((column_length, side), f32))
    return lax.fori_loop(0, SWEEPS + 1, sweep, start)


def on_device(tile_data, tile_rows, tile_cols, tile_counts):
    blocks = tile_data[0, 0]
    row_blocks = tile_rows[0, 0]
    column_blocks = tile_cols[0, 0]
    used_count = tile_counts[0, 0]
    n_row, n_col = lax.axis_size("row"), lax.axis_size("col")
    row_scale, column_scale, flag = sparse(blocks, row_blocks, column_blocks, used_count, n_row, n_col)
    row_scale, column_scale = lax.cond(
        flag[0, 0] > 0,
        lambda: dense(blocks, row_blocks, column_blocks, used_count),
        lambda: settle(row_scale, column_scale),
    )
    return (row_scale.reshape(-1), column_scale.reshape(-1))


def solution(mesh):
    placed = (
        P("row", "col", None, None, None),
        P("row", "col", None),
        P("row", "col", None),
        P("row", "col"),
    )
    return jax.shard_map(
        on_device, mesh=mesh, in_specs=placed, out_specs=(P("row"), P("col")), check_vma=False
    )
```
